32 devices in a mesh: groups: 2 (over y), samples: 4 (over z), blocks: 2 (over x), folds: 2 (over core).
Axes of the slice: x: 2, y: 2, z: 4, core: 2. Of those that a mesh axis runs over, the one named last changes fastest.
Arguments:
- allele_dosage_table: bfloat16 [1000, 4096], P('blocks', ('groups', 'samples')), parts along dimension 1, may hold values from -6 to 6
- phenotype_values: bfloat16 [20, 4096], P(None, ('groups', 'samples')), parts along dimension 1, may hold values from -8 to 8
- individual_partition_label: int32 [4096], P(('groups', 'samples')), parts along dimension 0, may hold values from 0 to 3, as said below
- shrink_strengths: float32 [2], replicated, may hold values from 0.005 to 2, as said below
Outputs:
- predictions: bfloat16 [4, 2, 2, 20, 1024], P('folds', 'blocks', None, None, ('groups', 'samples')), parts along dimension 4
- level_gram: float32 [8, 2, 2, 20, 2, 2], P(('groups', 'folds'), 'blocks'), parts along dimension 0
- level_cross: float32 [8, 2, 2, 20], P(('groups', 'folds'), 'blocks'), parts along dimension 0
The draws below stay inside these ranges and needn't reach their ends.
There are 2 independent parts, one for each index of `groups`. The reference program is written for one: setup_inputs(seed, part) draws one part's arguments, and reference() takes and returns one part's arrays. A program takes and returns all parts, laid end to end along the dimension named above; an argument that names none is the same for every part. Nothing has to cross between parts.
Inputs may be any that keep to these rules, and one draw needn't show every extreme that they name: `individual_partition_label`: among the 512 samples of each device (aligned runs of 512 indices) every fold number appears equally often, 512 / 4 times. `shrink_strengths`: the first penalty lies between 0.005 and 0.02, every other one between 0.1 and 2.
All inputs are finite; a program needn't handle non-finite values.
Results may differ from the reference program's by a relative error of at most 0.0055.
Values may be sent and summed in bfloat16 or wider, within the bound.
No kernel may reach another device: no remote copies, remote signals or barrier semaphores. Data moves between devices by JAX's collectives and lax.ppermute only.
A program may use at most 64 MiB of HBM per device.

```python
import math
import jax
import jax.numpy as jnp
from jax import lax

BSIZE = 500
TRAITS = 20
SHRINK_LEVELS = 2
FOLDS = 4
SAMP_DEV = 512
SAMPLES = 2048
VARIANTS = 1000
N_BLOCKS = 2


def linked_chains(key):
    gap_key, second_gap_key, noise_key = jax.random.split(key, 3)
    first_low, first_high = (0.002, 0.2)
    second_low, second_high = (0.01, 0.5)
    first_weight = 0.8
    innovation = jax.random.normal(noise_key, (VARIANTS, 2, SAMPLES), jnp.float32)
    first_unit = jax.random.uniform(gap_key, (VARIANTS,), jnp.float32)
    second_unit = jax.random.uniform(second_gap_key, (VARIANTS,), jnp.float32)
    first_gap = jnp.exp(math.log(first_low) + first_unit * (math.log(first_high) - math.log(first_low)))
    second_gap = jnp.exp(math.log(second_low) + second_unit * (math.log(second_high) - math.log(second_low)))
    carry_rate = 1.0 - jnp.stack([first_gap, second_gap], axis=1)
    position = jnp.arange(VARIANTS, dtype=jnp.int32)[:, None]
    carry_rate = jnp.where(position == 0, 0.0, carry_rate).astype(jnp.float32)
    fresh_rate = jnp.sqrt(1.0 - carry_rate * carry_rate).astype(jnp.float32)

    def advance(state, inputs):
        rate, fresh, noise = inputs
        updated = rate[:, None] * state + fresh[:, None] * noise
        return (updated, updated)
    start = jnp.zeros((2, SAMPLES), jnp.float32)
    final_state, chains = lax.scan(advance, start, (carry_rate, fresh_rate, innovation))
    mixed = math.sqrt(first_weight) * chains[:, 0] + math.sqrt(1.0 - first_weight) * chains[:, 1]
    return jnp.clip(mixed, -6.0, 6.0)


def joint_draw(key):
    base = jax.random.fold_in(key, 17)
    chain_key, effect_key, trait_key = jax.random.split(base, 3)
    dosages = linked_chains(chain_key)
    effects = jax.random.normal(effect_key, (TRAITS, VARIANTS), jnp.float32) * math.sqrt(0.8 / VARIANTS)
    residual = math.sqrt(0.2) * jax.random.normal(trait_key, (TRAITS, SAMPLES), jnp.float32)
    values = jnp.dot(effects, dosages, precision=lax.Precision.HIGHEST) + residual
    return (dosages, jnp.clip(values, -8.0, 8.0))


def draw_allele_dosage_table(key, part):
    dosages, values = joint_draw(key)
    return dosages.astype(jnp.bfloat16)


def draw_phenotype_values(key, part):
    dosages, values = joint_draw(key)
    return values.astype(jnp.bfloat16)


def draw_individual_partition_label(key, part):
    shard_keys = jax.random.split(jax.random.fold_in(key, 29), SAMPLES // SAMP_DEV)
    pattern = jnp.arange(SAMP_DEV, dtype=jnp.int32) % FOLDS

    def shuffle(shard_key):
        return jax.random.permutation(shard_key, pattern)
    return jax.vmap(shuffle)(shard_keys).reshape(SAMPLES).astype(jnp.int32)


def draw_shrink_strengths(key, part):
    position = jnp.arange(SHRINK_LEVELS, dtype=jnp.int32)
    lower = jnp.where(position == 0, math.log(0.005), math.log(0.1)).astype(jnp.float32)
    upper = jnp.where(position == 0, math.log(0.02), math.log(2.0)).astype(jnp.float32)
    unit = jax.random.uniform(jax.random.fold_in(key, 41), (SHRINK_LEVELS,), jnp.float32)
    return jnp.exp(lower + unit * (upper - lower)).astype(jnp.float32)


def setup_inputs(seed: int = 0, part: int = 0) -> dict:
    arg_keys = jax.random.split(jax.random.key(seed), 5)
    part_splits = jax.random.split(jax.random.fold_in(arg_keys[4], part), 5)
    return {
        "allele_dosage_table": draw_allele_dosage_table(jax.random.fold_in(jax.random.fold_in(arg_keys[4], part), 71), part),
        "phenotype_values": draw_phenotype_values(jax.random.fold_in(jax.random.fold_in(arg_keys[4], part), 71), part),
        "individual_partition_label": draw_individual_partition_label(jax.random.fold_in(jax.random.fold_in(arg_keys[4], part), 71), part),
        "shrink_strengths": draw_shrink_strengths(jax.random.fold_in(arg_keys[4], 71), part),
    }


def segment_shrinkage_estimate(learning_design_inner, learning_design_response, shrink_strengths, individual_total):
    matrix_a = learning_design_inner / individual_total
    right_side = learning_design_response / individual_total
    identity = jnp.eye(learning_design_inner.shape[-1], dtype=jnp.float32)

    def lone_shrink_strength(value):
        factor = jnp.linalg.cholesky(matrix_a + value * identity)
        inner = lax.linalg.triangular_solve(factor, right_side, left_side=True, lower=True)
        return lax.linalg.triangular_solve(factor, inner, left_side=True, lower=True, transpose_a=True)
    return lax.map(lone_shrink_strength, shrink_strengths)

def reference(allele_dosage_table, phenotype_values, individual_partition_label, shrink_strengths):
    rows = SAMPLES // FOLDS
    learning_individual_tally = SAMPLES - rows
    sample_order = jnp.argsort(individual_partition_label, stable=True).astype(jnp.int32).reshape(FOLDS, rows)
    trait_sorted = jnp.take(phenotype_values, sample_order, axis=1).astype(jnp.float32)
    blocks_view = allele_dosage_table.reshape(N_BLOCKS, BSIZE, SAMPLES)

    def one_block(block):
        geno_sorted = jnp.take(block, sample_order, axis=1).astype(jnp.float32)
        held_gram = jnp.einsum('bki,cki->kbc', geno_sorted, geno_sorted, precision=lax.Precision.HIGHEST)
        held_cross = jnp.einsum('bki,pki->kbp', geno_sorted, trait_sorted, precision=lax.Precision.HIGHEST)
        learning_design_inner = jnp.sum(held_gram, 0)[None] - held_gram
        learning_design_response = jnp.sum(held_cross, 0)[None] - held_cross
        estimated_weights = segment_shrinkage_estimate(learning_design_inner, learning_design_response, shrink_strengths, learning_individual_tally)
        coefficient_half = lax.optimization_barrier(estimated_weights.astype(jnp.bfloat16)).astype(jnp.float32)
        preds = jnp.einsum('rkbp,bki->krpi', coefficient_half, geno_sorted, precision=lax.Precision.HIGHEST)
        return preds.astype(jnp.bfloat16)
    preds = lax.map(one_block, blocks_view)
    predictions = jnp.transpose(preds, (1, 0, 2, 3, 4))
    wide = lax.optimization_barrier(predictions).astype(jnp.float32)
    level_gram = jnp.einsum('kbrpi,kcspi->kbrpcs', wide, wide, precision=lax.Precision.HIGHEST) / rows
    level_cross = jnp.einsum('kbrpi,pki->kbrp', wide, trait_sorted, precision=lax.Precision.HIGHEST) / rows
    return (predictions, level_gram, level_cross)
```

```python
import functools

import jax
import jax.numpy as jnp
from jax import lax
from jax.experimental import pallas as pl
from jax.experimental.pallas import tpu as pltpu
from jax.sharding import PartitionSpec as P

SHRINK_LEVELS = 2
FOLDS = 4
LANES = 128
PANEL = 32
PIVOTS = 8
HIGHEST = lax.Precision.HIGHEST
F32 = jnp.float32
BF16 = jnp.bfloat16


def round_up(value, step):
    return (value + step - 1) // step * step


def dot_nt(left, right):
    return lax.dot_general(left, right, (((1,), (1,)), ((), ())), preferred_element_type=F32)


def spread(value):
    return jnp.broadcast_to(value, (8, LANES))


def sort_kernel(own_count, variants, traits, pad_rows, geno_ref, trait_ref, label_ref, other_ref, own_ref):
    rows = label_ref.shape[1]
    core = lax.axis_index("folds")
    cores = lax.axis_size("folds")
    slot = lax.rem(label_ref[...] + own_count * (cores - 1 - core), FOLDS)
    width = rows // FOLDS
    before = lax.broadcasted_iota(jnp.int32, (rows, rows), 0) < lax.broadcasted_iota(jnp.int32, (rows, rows), 1)
    fold_row = lax.broadcasted_iota(jnp.int32, (16, rows), 0)
    hit = jnp.broadcast_to(slot, (16, rows)) == fold_row
    rank = jnp.dot(
        jnp.where(hit, 1.0, 0.0).astype(BF16),
        jnp.where(before, 1.0, 0.0).astype(BF16),
        preferred_element_type=F32,
    )
    place = jnp.sum(jnp.where(hit, rank + (fold_row * width).astype(F32), 0.0), axis=0, keepdims=True)
    place = place.astype(jnp.int32)
    target = lax.broadcasted_iota(jnp.int32, (rows, rows), 0)
    move = jnp.where(target == jnp.broadcast_to(place, (rows, rows)), 1.0, 0.0).astype(BF16)
    sorted_geno = dot_nt(geno_ref[...], move).astype(BF16)
    sorted_trait = dot_nt(trait_ref[...], move).astype(BF16)
    half = other_ref.shape[1]
    height = other_ref.shape[0]
    low = variants // 16 * 16
    for part, ref in enumerate((other_ref, own_ref)):
        ref[low:height, :] = jnp.zeros((height - low, half), BF16)
        ref[0:variants, :] = sorted_geno[:, part * half : (part + 1) * half]
        ref[pad_rows : pad_rows + traits, :] = sorted_trait[:, part * half : (part + 1) * half]


def eliminate_panel(panels, first, ones):
    lane = lax.broadcasted_iota(jnp.int32, (8, LANES), 1)
    sub = lax.broadcasted_iota(jnp.int32, (8, LANES), 0)
    systems = range(len(panels))
    count = len(panels[0])
    panels = [list(panel) for panel in panels]
    for b in range(count):
        base_col = first + 8 * b
        in_pivot = (lane >= base_col) & (lane < base_col + 8)
        rest = [(b + 1 + i) % count for i in range(count - 1)]
        cols = [[None] * 8 for _ in systems]
        factors = [{i: [None] * 8 for i in rest} for _ in systems]
        for u in range(8):
            for q in systems:
                cols[q][u] = spread(panels[q][b][:, base_col + u : base_col + u + 1]) * ones
        for u in range(8):
            for q in systems:
                for i in rest:
                    factors[q][i][u] = spread(panels[q][i][:, base_col + u : base_col + u + 1])
        for t in range(8):
            for q in systems:
                inverse = 1.0 / spread(cols[q][t][t : t + 1, :])
                factor = jnp.where(sub == t, -1.0, cols[q][t])
                for u in range(t + 1, 8):
                    row = spread(cols[q][u][t : t + 1, :])
                    cols[q][u] = jnp.where(sub == t, 0.0, cols[q][u]) - (factor * row) * inverse
                row = jnp.where(lane == base_col + t, 1.0, spread(panels[q][b][t : t + 1, :]))
                keep = jnp.where((lane == base_col + t) | (sub == t), 0.0, panels[q][b])
                panels[q][b] = keep - (factor * row) * inverse
        for q in systems:
            rows = [spread(panels[q][b][t : t + 1, :]) for t in range(8)]
            for i in rest:
                parts = [factors[q][i][t] * rows[t] for t in range(8)]
                while len(parts) > 1:
                    parts = [parts[k] + parts[k + 1] for k in range(0, len(parts), 2)]
                panels[q][i] = jnp.where(in_pivot, 0.0, panels[q][i]) - parts[0]
    return panels


def invert_blocks(blocks, ones):
    lane = lax.broadcasted_iota(jnp.int32, (LANES, LANES), 1)
    row = lax.broadcasted_iota(jnp.int32, (LANES, LANES), 0)
    blocks = list(blocks)
    for b in range(LANES // PANEL):
        r0 = PANEL * b
        panels = eliminate_panel(
            [[block[r0 + 8 * i : r0 + 8 * i + 8, :] for i in range(PANEL // 8)] for block in blocks], r0, ones
        )
        for q, block in enumerate(blocks):
            pieces = list(panels[q])
            if r0:
                pieces.insert(0, jnp.zeros((r0, LANES), F32))
            if LANES - PANEL - r0:
                pieces.append(jnp.zeros((LANES - PANEL - r0, LANES), F32))
            wide = jnp.concatenate(pieces, axis=0)
            keep = jnp.where((lane >= r0) & (lane < r0 + PANEL), 0.0, block)
            update = keep - jnp.dot(block, wide, precision=HIGHEST, preferred_element_type=F32)
            blocks[q] = jnp.where((row >= r0) & (row < r0 + PANEL), wide, update)
    return blocks


def solve_kernel(sources, own_count, learning_tally, pad_rows, trait_rows, *refs):
    shrink_ref = refs[0]
    others, owns = refs[1 : 1 + sources], refs[1 + sources : 1 + 2 * sources]
    message_ref, mat_ref, inv_ref, ones_ref = refs[1 + 2 * sources :]
    levels = shrink_ref.shape[0]
    half = others[0].shape[1]
    width = half // own_count
    pick = lax.rem(lax.axis_index("samples"), own_count)
    held = pl.multiple_of(pick * width, width)
    train = [
        pl.multiple_of(lax.rem(pick + 1 + i, own_count) * width, width) for i in range(own_count - 1)
    ]
    ones_ref[...] = jnp.ones((8, LANES), F32)
    blocks = pad_rows // LANES
    height = others[0].shape[0]
    total = mat_ref.shape[2]
    lane = lax.broadcasted_iota(jnp.int32, (LANES, LANES), 1)
    diagonal = lane == lax.broadcasted_iota(jnp.int32, (LANES, LANES), 0)
    for j in range(blocks):
        r0 = j * LANES
        acc = None
        for s in range(sources):
            pieces = [(others[s][r0 : r0 + LANES, :], others[s][...])]
            for start in train:
                pieces.append((owns[s][r0 : r0 + LANES, pl.ds(start, width)], owns[s][:, pl.ds(start, width)]))
            for left, right in pieces:
                part = dot_nt(left, right)
                acc = part if acc is None else acc + part
        acc = acc / learning_tally
        for r in range(levels):
            mat_ref[r, r0 : r0 + LANES, 0:height] = acc
            mat_ref[r, r0 : r0 + LANES, height:total] = jnp.zeros((LANES, total - height), F32)
            mat_ref[r, r0 : r0 + LANES, r0 : r0 + LANES] = acc[:, r0 : r0 + LANES] + jnp.where(
                diagonal, shrink_ref[r], 0.0
            )

    def stage(j, carry):
        start = pl.multiple_of(j * LANES, LANES)
        inverses = invert_blocks(
            [mat_ref[r, pl.ds(start, LANES), pl.ds(start, LANES)] for r in range(levels)], ones_ref[...]
        )
        for r in range(levels):
            inv_ref[r] = inverses[r]
        for jj in range(blocks):

            @pl.when(j == jj)
            def _():
                c0 = jj * LANES
                c1 = c0 + LANES
                for r in range(levels):
                    solved = jnp.dot(
                        inv_ref[r], mat_ref[r, c0:c1, c1:total], precision=HIGHEST, preferred_element_type=F32
                    )
                    for lo, hi in ((0, c0), (c1, pad_rows)):
                        if hi > lo:
                            mat_ref[r, lo:hi, c1:total] = mat_ref[r, lo:hi, c1:total] - jnp.dot(
                                mat_ref[r, lo:hi, c0:c1], solved, precision=HIGHEST, preferred_element_type=F32
                            )
                    mat_ref[r, c0:c1, c1:total] = solved

        return carry

    lax.fori_loop(0, blocks, stage, 0)
    for r in range(levels):
        betas = jnp.transpose(mat_ref[r, :, pad_rows : pad_rows + LANES])[0:trait_rows, :].astype(BF16)
        for s in range(sources):
            message_ref[r * trait_rows : (r + 1) * trait_rows, s * width : (s + 1) * width] = jnp.dot(
                betas, owns[s][0:pad_rows, pl.ds(held, width)], preferred_element_type=F32
            ).astype(BF16)
    for s in range(sources):
        message_ref[levels * trait_rows : (levels + 1) * trait_rows, s * width : (s + 1) * width] = owns[s][
            pad_rows : pad_rows + trait_rows, pl.ds(held, width)
        ]


def level_kernel(levels, traits, trait_rows, held_rows, partner_steps, *refs):
    own_count = len(partner_steps)
    n_blocks = (len(refs) - 2) // own_count
    messages = [refs[f * n_blocks : (f + 1) * n_blocks] for f in range(own_count)]
    pred_ref, level_ref = refs[-2:]
    me = lax.axis_index("samples")
    sources = lax.axis_size("samples")
    block = lax.axis_index("blocks")
    pick = lax.rem(me, own_count)
    width = pred_ref.shape[-1]
    lane = lax.broadcasted_iota(jnp.int32, (trait_rows, LANES), 1)
    for f in range(own_count):
        slot = lax.rem(pick + f, own_count)
        partner = me - pick + slot
        mine = messages[f][0]
        where_mine = pl.multiple_of(lax.rem(partner - me + sources, sources) * width, width)
        for r in range(levels):
            pred_ref[slot, r] = mine[r * trait_rows : r * trait_rows + trait_rows, pl.ds(where_mine, width)][0:traits]
        wide = [
            [messages[f][e][s * trait_rows : (s + 1) * trait_rows, :].astype(F32) for s in range(levels)]
            for e in range(n_blocks)
        ]
        trait = mine[levels * trait_rows : (levels + 1) * trait_rows, :].astype(F32)
        for r in range(levels):
            out = jnp.where(lane == n_blocks * levels, jnp.sum(wide[0][r] * trait, axis=1, keepdims=True), 0.0)
            for e in range(n_blocks):
                column = lax.rem(block - e + n_blocks, n_blocks) * levels
                for s in range(levels):
                    total = jnp.sum(wide[0][r] * wide[e][s], axis=1, keepdims=True)
                    out = out + jnp.where(lane == column + s, total, 0.0)
            level_ref[slot, r] = out / held_rows


def per_device(allele_dosage_table, phenotype_values, individual_partition_label, shrink_strengths):
    cores = lax.axis_size("folds")
    sources = lax.axis_size("samples")
    n_blocks = lax.axis_size("blocks")
    own_count = FOLDS // cores
    levels = shrink_strengths.shape[0]
    variants, samples = allele_dosage_table.shape
    traits = phenotype_values.shape[0]
    width = samples // FOLDS
    held_rows = sources * width
    learning_tally = sources * samples - held_rows
    pad_rows = round_up(variants, LANES)
    trait_rows = round_up(traits, 32)
    height = pad_rows + trait_rows
    half = own_count * width
    vmem = pl.BlockSpec(memory_space=pltpu.VMEM)
    smem = pl.BlockSpec(memory_space=pltpu.SMEM)

    other_half, own_half = pl.pallas_call(
        functools.partial(sort_kernel, own_count, variants, traits, pad_rows),
        out_shape=[jax.ShapeDtypeStruct((height, half), BF16)] * 2,
        in_specs=[vmem] * 3,
        out_specs=[vmem] * 2,
        name="sort_samples",
    )(allele_dosage_table, phenotype_values, individual_partition_label.reshape(1, samples))

    others, owns = [other_half], [own_half]
    for shift in range(1, sources):
        others.append(lax.ppermute(other_half, "samples", [(i, (i + shift) % sources) for i in range(sources)]))
    for shift in range(1, sources):
        owns.append(lax.ppermute(others[shift], "folds", [(i, cores - 1 - i) for i in range(cores)]))

    message = pl.pallas_call(
        functools.partial(solve_kernel, sources, own_count, learning_tally, pad_rows, trait_rows),
        out_shape=jax.ShapeDtypeStruct(((levels + 1) * trait_rows, sources * width), BF16),
        in_specs=[smem] + [vmem] * (2 * sources),
        out_specs=vmem,
        scratch_shapes=[
            pltpu.VMEM((levels, pad_rows, pad_rows + LANES), F32),
            pltpu.VMEM((levels, LANES, LANES), F32),
            pltpu.VMEM((8, LANES), F32),
        ],
        name="solve_ridge",
    )(shrink_strengths, *others, *owns)

    messages = []
    for f in range(own_count):
        for e in range(n_blocks):
            if f == 0 and e == 0:
                messages.append(message)
                continue
            pairs = []
            for s in range(sources):
                source = s - s % own_count + (s % own_count + f) % own_count
                for b in range(n_blocks):
                    pairs.append((source * n_blocks + (b - e) % n_blocks, s * n_blocks + b))
            messages.append(lax.ppermute(message, ("samples", "blocks"), pairs))

    preds, level = pl.pallas_call(
        functools.partial(level_kernel, levels, traits, trait_rows, held_rows, tuple(range(own_count))),
        out_shape=[
            jax.ShapeDtypeStruct((own_count, levels, traits, width), BF16),
            jax.ShapeDtypeStruct((own_count, levels, trait_rows, LANES), F32),
        ],
        in_specs=[vmem] * len(messages),
        out_specs=[vmem] * 2,
        name="level_one",
    )(*messages)
    gram = level[:, None, :, :traits, : n_blocks * levels]
    level_gram = gram.reshape(own_count, 1, levels, traits, n_blocks, levels)
    level_cross = level[:, None, :, :traits, n_blocks * levels]
    return (preds[:, None], level_gram, level_cross)


def solution(mesh):
    in_specs = (
        P("blocks", ("groups", "samples")),
        P(None, ("groups", "samples")),
        P(("groups", "samples")),
        P(),
    )
    out_specs = (
        P("folds", "blocks", None, None, ("groups", "samples")),
        P(("groups", "folds"), "blocks", None, None, None, None),
        P(("groups", "folds"), "blocks", None, None),
    )
    return jax.shard_map(
        per_device, mesh=mesh, in_specs=in_specs, out_specs=out_specs, check_vma=False
    )
```

```python
import functools

import jax
import jax.numpy as jnp
from jax import lax
from jax.experimental import pallas as pl
from jax.experimental.pallas import tpu as pltpu
from jax.sharding import PartitionSpec as P

SHRINK_LEVELS = 2
FOLDS = 4
LANES = 128
PANEL = 32
PIVOTS = 8
HIGHEST = lax.Precision.HIGHEST
F32 = jnp.float32
BF16 = jnp.bfloat16


def round_up(value, step):
    return (value + step - 1) // step * step


def dot_nt(left, right):
    return lax.dot_general(left, right, (((1,), (1,)), ((), ())), preferred_element_type=F32)


def spread(value):
    return jnp.broadcast_to(value, (8, LANES))


def sort_kernel(own_count, pad_rows, geno_ref, trait_ref, label_ref, *refs):
    variants, traits = geno_ref.shape[0], trait_ref.shape[0]
    rows = label_ref.shape[1]
    core = lax.axis_index("folds")
    cores = lax.axis_size("folds")
    slot = lax.rem(label_ref[...] + own_count * (cores - 1 - core), FOLDS)
    width = rows // FOLDS
    before = lax.broadcasted_iota(jnp.int32, (rows, rows), 0) < lax.broadcasted_iota(jnp.int32, (rows, rows), 1)
    fold_row = lax.broadcasted_iota(jnp.int32, (16, rows), 0)
    hit = jnp.broadcast_to(slot, (16, rows)) == fold_row
    rank = jnp.dot(
        jnp.where(hit, 1.0, 0.0).astype(BF16),
        jnp.where(before, 1.0, 0.0).astype(BF16),
        preferred_element_type=F32,
    )
    place = jnp.sum(jnp.where(hit, rank + (fold_row * width).astype(F32), 0.0), axis=0, keepdims=True)
    place = place.astype(jnp.int32)
    target = lax.broadcasted_iota(jnp.int32, (rows, rows), 0)
    move = jnp.where(target == jnp.broadcast_to(place, (rows, rows)), 1.0, 0.0).astype(BF16)
    sorted_geno = dot_nt(geno_ref[...], move).astype(BF16)
    sorted_trait = dot_nt(trait_ref[...], move).astype(BF16)
    split = refs[0].shape[0]
    half = refs[0].shape[1]
    height = refs[2].shape[0]
    low = (variants - split) // 16 * 16
    for part in range(2):
        lanes = slice(part * half, (part + 1) * half)
        refs[part][...] = sorted_geno[0:split, lanes]
        ref = refs[2 + part]
        ref[low:height, :] = jnp.zeros((height - low, half), BF16)
        ref[0 : variants - split, :] = sorted_geno[split:variants, lanes]
        ref[pad_rows - split : pad_rows - split + traits, :] = sorted_trait[:, lanes]


def eliminate_panel(panels, first, ones):
    lane = lax.broadcasted_iota(jnp.int32, (8, LANES), 1)
    sub = lax.broadcasted_iota(jnp.int32, (8, LANES), 0)
    systems = range(len(panels))
    count = len(panels[0])
    panels = [list(panel) for panel in panels]
    for b in range(count):
        base_col = first + 8 * b
        in_pivot = (lane >= base_col) & (lane < base_col + 8)
        rest = [(b + 1 + i) % count for i in range(count - 1)]
        cols = [[None] * 8 for _ in systems]
        factors = [{i: [None] * 8 for i in rest} for _ in systems]
        for u in range(8):
            for q in systems:
                cols[q][u] = spread(panels[q][b][:, base_col + u : base_col + u + 1]) * ones
        for u in range(8):
            for q in systems:
                for i in rest:
                    factors[q][i][u] = spread(panels[q][i][:, base_col + u : base_col + u + 1])
        for t in range(8):
            for q in systems:
                inverse = 1.0 / spread(cols[q][t][t : t + 1, :])
                factor = jnp.where(sub == t, -1.0, cols[q][t])
                for u in range(t + 1, 8):
                    row = spread(cols[q][u][t : t + 1, :])
                    cols[q][u] = jnp.where(sub == t, 0.0, cols[q][u]) - (factor * row) * inverse
                row = jnp.where(lane == base_col + t, 1.0, spread(panels[q][b][t : t + 1, :]))
                keep = jnp.where((lane == base_col + t) | (sub == t), 0.0, panels[q][b])
                panels[q][b] = keep - (factor * row) * inverse
        for q in systems:
            rows = [spread(panels[q][b][t : t + 1, :]) for t in range(8)]
            for i in rest:
                parts = [factors[q][i][t] * rows[t] for t in range(8)]
                while len(parts) > 1:
                    parts = [parts[k] + parts[k + 1] for k in range(0, len(parts), 2)]
                panels[q][i] = jnp.where(in_pivot, 0.0, panels[q][i]) - parts[0]
    return panels


def invert_blocks(blocks, ones):
    lane = lax.broadcasted_iota(jnp.int32, (LANES, LANES), 1)
    row = lax.broadcasted_iota(jnp.int32, (LANES, LANES), 0)
    blocks = list(blocks)
    for b in range(LANES // PANEL):
        r0 = PANEL * b
        panels = eliminate_panel(
            [[block[r0 + 8 * i : r0 + 8 * i + 8, :] for i in range(PANEL // 8)] for block in blocks], r0, ones
        )
        for q, block in enumerate(blocks):
            pieces = list(panels[q])
            if r0:
                pieces.insert(0, jnp.zeros((r0, LANES), F32))
            if LANES - PANEL - r0:
                pieces.append(jnp.zeros((LANES - PANEL - r0, LANES), F32))
            wide = jnp.concatenate(pieces, axis=0)
            keep = jnp.where((lane >= r0) & (lane < r0 + PANEL), 0.0, block)
            update = keep - jnp.dot(block, wide, precision=HIGHEST, preferred_element_type=F32)
            blocks[q] = jnp.where((row >= r0) & (row < r0 + PANEL), wide, update)
    return blocks


def dot_f32(left, right):
    return jnp.dot(left, right, precision=HIGHEST, preferred_element_type=F32)


def fold_lanes(own_count, width):
    pick = lax.rem(lax.axis_index("samples"), own_count)
    held = pl.multiple_of(pick * width, width)
    train = [pl.multiple_of(lax.rem(pick + 1 + i, own_count) * width, width) for i in range(own_count - 1)]
    return held, train


def training_product(left, right, train, width, rows):
    acc = None
    for left_other, left_own, right_other, right_own in zip(*left, *right):
        pieces = [(left_other[rows, :], right_other[...])]
        for start in train:
            pieces.append((left_own[rows, pl.ds(start, width)], right_own[:, pl.ds(start, width)]))
        for a, b in pieces:
            part = dot_nt(a, b)
            acc = part if acc is None else acc + part
    return acc


def stages(count, levels, mat_ref, inv_ref, ones_ref, follow):
    def stage(j, carry):
        start = pl.multiple_of(j * LANES, LANES)
        inverses = invert_blocks(
            [mat_ref[r, pl.ds(start, LANES), pl.ds(start, LANES)] for r in range(levels)], ones_ref[...]
        )
        for r in range(levels):
            inv_ref[r] = inverses[r]
        for jj in range(count):

            @pl.when(j == jj)
            def _():
                for r in range(levels):
                    follow(jj, r)

        return carry

    lax.fori_loop(0, count, stage, 0)


def lead_kernel(sources, own_count, learning_tally, *refs):
    shrink_ref = refs[0]
    others, owns = refs[1 : 1 + sources], refs[1 + sources : 1 + 2 * sources]
    out_ref, inv_ref, ones_ref = refs[1 + 2 * sources :]
    levels, size = out_ref.shape[0], out_ref.shape[1]
    width = others[0].shape[1] // own_count
    _, train = fold_lanes(own_count, width)
    ones_ref[...] = jnp.ones((8, LANES), F32)
    diagonal = lax.broadcasted_iota(jnp.int32, (LANES, size), 1) - lax.broadcasted_iota(jnp.int32, (LANES, size), 0)
    for r0 in range(0, size, LANES):
        rows = slice(r0, r0 + LANES)
        acc = training_product((others, owns), (others, owns), train, width, rows) / learning_tally
        for r in range(levels):
            out_ref[r, rows, :] = acc + jnp.where(diagonal == r0, shrink_ref[r], 0.0)

    def follow(j, r):
        c0, c1 = j * LANES, (j + 1) * LANES
        inverse = inv_ref[r]
        spans = [(lo, hi) for lo, hi in ((0, c0), (c1, size)) if hi > lo]
        solved = [dot_f32(inverse, out_ref[r, c0:c1, lo:hi]) for lo, hi in spans]
        for lo, hi in spans:
            column = out_ref[r, lo:hi, c0:c1]
            for (left, right), value in zip(spans, solved):
                out_ref[r, lo:hi, left:right] = out_ref[r, lo:hi, left:right] - dot_f32(column, value)
            out_ref[r, lo:hi, c0:c1] = -dot_f32(column, inverse)
        for (left, right), value in zip(spans, solved):
            out_ref[r, c0:c1, left:right] = value
        out_ref[r, c0:c1, c0:c1] = inverse

    stages(size // LANES, levels, out_ref, inv_ref, ones_ref, follow)


def tail_kernel(sources, own_count, learning_tally, trait_rows, *refs):
    shrink_ref, lead_ref = refs[0:2]
    first = (refs[2 : 2 + sources], refs[2 + sources : 2 + 2 * sources])
    last = (refs[2 + 2 * sources : 2 + 3 * sources], refs[2 + 3 * sources : 2 + 4 * sources])
    message_ref, wide_ref, solved_ref, mat_ref, inv_ref, ones_ref = refs[2 + 4 * sources :]
    levels, lead = lead_ref.shape[0], lead_ref.shape[1]
    size, total = mat_ref.shape[1], mat_ref.shape[2]
    width = first[0][0].shape[1] // own_count
    height = size + trait_rows
    held, train = fold_lanes(own_count, width)
    ones_ref[...] = jnp.ones((8, LANES), F32)
    for r0 in range(0, lead, LANES):
        rows = slice(r0, r0 + LANES)
        wide_ref[rows, 0:height] = training_product(first, last, train, width, rows) / learning_tally
        wide_ref[rows, height:total] = jnp.zeros((LANES, total - height), F32)
    for r in range(levels):
        solved_ref[r] = dot_f32(lead_ref[r], wide_ref[...])
    diagonal = lax.broadcasted_iota(jnp.int32, (LANES, height), 1) - lax.broadcasted_iota(
        jnp.int32, (LANES, height), 0
    )
    for r0 in range(0, size, LANES):
        rows = slice(r0, r0 + LANES)
        side = training_product(last, first, train, width, rows) / learning_tally
        acc = training_product(last, last, train, width, rows) / learning_tally
        for r in range(levels):
            mat_ref[r, rows, 0:height] = acc + jnp.where(diagonal == r0, shrink_ref[r], 0.0)
            mat_ref[r, rows, height:total] = jnp.zeros((LANES, total - height), F32)
            mat_ref[r, rows, :] = mat_ref[r, rows, :] - dot_f32(side, solved_ref[r])

    def follow(j, r):
        c0, c1 = j * LANES, (j + 1) * LANES
        solved = dot_f32(inv_ref[r], mat_ref[r, c0:c1, c1:total])
        for lo, hi in ((0, c0), (c1, size)):
            if hi > lo:
                mat_ref[r, lo:hi, c1:total] = mat_ref[r, lo:hi, c1:total] - dot_f32(mat_ref[r, lo:hi, c0:c1], solved)
        mat_ref[r, c0:c1, c1:total] = solved

    stages(size // LANES, levels, mat_ref, inv_ref, ones_ref, follow)
    for r in range(levels):
        low = mat_ref[r, :, size:total]
        top = solved_ref[r, :, size:total] - dot_f32(solved_ref[r, :, 0:size], low)
        top = jnp.transpose(top)[0:trait_rows, :].astype(BF16)
        low = jnp.transpose(low)[0:trait_rows, :].astype(BF16)
        for s in range(sources):
            value = jnp.dot(top, first[1][s][:, pl.ds(held, width)], preferred_element_type=F32) + jnp.dot(
                low, last[1][s][0:size, pl.ds(held, width)], preferred_element_type=F32
            )
            message_ref[r * trait_rows : (r + 1) * trait_rows, s * width : (s + 1) * width] = value.astype(BF16)
    for s in range(sources):
        message_ref[levels * trait_rows : (levels + 1) * trait_rows, s * width : (s + 1) * width] = last[1][s][
            size : size + trait_rows, pl.ds(held, width)
        ]


def level_kernel(own_count, trait_rows, held_rows, *refs):
    pred_ref, gram_ref, cross_ref = refs[-3:]
    n_blocks = (len(refs) - 3) // own_count
    messages = [refs[f * n_blocks : (f + 1) * n_blocks] for f in range(own_count)]
    levels, traits, width = pred_ref.shape[2:]
    me = lax.axis_index("samples")
    block = lax.axis_index("blocks")
    pick = lax.rem(me, own_count)
    lane = lax.broadcasted_iota(jnp.int32, (trait_rows, LANES), 1)
    for f in range(own_count):
        slot = lax.rem(pick + f, own_count)
        mine = messages[f][0]
        held = pl.multiple_of((me ^ (me - pick + slot)) * width, width)
        for r in range(levels):
            pred_ref[slot, 0, r] = mine[r * trait_rows : (r + 1) * trait_rows, pl.ds(held, width)][0:traits]
        wide = [
            [messages[f][e][s * trait_rows : (s + 1) * trait_rows, :].astype(F32) for s in range(levels)]
            for e in range(n_blocks)
        ]
        trait = mine[levels * trait_rows : (levels + 1) * trait_rows, :].astype(F32)
        columns = [lax.rem(block - e + n_blocks, n_blocks) for e in range(n_blocks)]
        ones = jnp.ones((8, trait.shape[1]), F32)
        for r in range(levels):
            cross = lax.dot_general(
                ones, wide[0][r] * trait, (((1,), (1,)), ((), ())), precision=HIGHEST, preferred_element_type=F32
            )
            cross_ref[slot, 0, r : r + 1, :] = cross[0:1, 0:traits] / held_rows
            sums = [
                [jnp.sum(wide[0][r] * wide[e][s], axis=1, keepdims=True) / held_rows for s in range(levels)]
                for e in range(n_blocks)
            ]
            for c in range(n_blocks):
                out = jnp.zeros((trait_rows, LANES), F32)
                for e in range(n_blocks):
                    for s in range(levels):
                        out = out + jnp.where((lane == s) & (columns[e] == c), sums[e][s], 0.0)
                for p in range(traits):
                    gram_ref[slot, 0, r, p, c : c + 1, :] = out[p : p + 1, 0:levels]


def per_device(allele_dosage_table, phenotype_values, individual_partition_label, shrink_strengths):
    cores = lax.axis_size("folds")
    sources = lax.axis_size("samples")
    n_blocks = lax.axis_size("blocks")
    own_count = FOLDS // cores
    levels = shrink_strengths.shape[0]
    variants, samples = allele_dosage_table.shape
    traits = phenotype_values.shape[0]
    width = samples // FOLDS
    held_rows = sources * width
    learning_tally = sources * samples - held_rows
    pad_rows = round_up(variants, LANES)
    lead = pad_rows // LANES // 2 * LANES
    size = pad_rows - lead
    trait_rows = round_up(traits, 32)
    half = own_count * width
    vmem = pl.BlockSpec(memory_space=pltpu.VMEM)
    smem = pl.BlockSpec(memory_space=pltpu.SMEM)

    other_lead, own_lead, other_tail, own_tail = pl.pallas_call(
        functools.partial(sort_kernel, own_count, pad_rows),
        out_shape=[jax.ShapeDtypeStruct((lead, half), BF16)] * 2
        + [jax.ShapeDtypeStruct((size + trait_rows, half), BF16)] * 2,
        in_specs=[vmem] * 3,
        out_specs=[vmem] * 4,
        name="sort_samples",
    )(allele_dosage_table, phenotype_values, individual_partition_label.reshape(1, samples))

    def fetch(other):
        return [other] + [
            lax.ppermute(other, "samples", [(i, i ^ d) for i in range(sources)]) for d in range(1, sources)
        ]

    def swap(own, others):
        return [own] + [lax.ppermute(x, "folds", [(i, cores - 1 - i) for i in range(cores)]) for x in others[1:]]

    others_lead = fetch(other_lead)
    owns_lead = swap(own_lead, others_lead)
    others_tail = fetch(other_tail)
    lead_inverse = pl.pallas_call(
        functools.partial(lead_kernel, sources, own_count, learning_tally),
        out_shape=jax.ShapeDtypeStruct((levels, lead, lead), F32),
        in_specs=[smem] + [vmem] * (2 * sources),
        out_specs=vmem,
        scratch_shapes=[pltpu.VMEM((levels, LANES, LANES), F32), pltpu.VMEM((8, LANES), F32)],
        name="invert_lead",
    )(shrink_strengths, *others_lead, *owns_lead)
    lead_inverse, *others_tail[1:] = lax.optimization_barrier((lead_inverse, *others_tail[1:]))
    owns_tail = swap(own_tail, others_tail)
    message = pl.pallas_call(
        functools.partial(tail_kernel, sources, own_count, learning_tally, trait_rows),
        out_shape=jax.ShapeDtypeStruct(((levels + 1) * trait_rows, sources * width), BF16),
        in_specs=[smem] + [vmem] * (1 + 4 * sources),
        out_specs=vmem,
        scratch_shapes=[
            pltpu.VMEM((lead, size + LANES), F32),
            pltpu.VMEM((levels, lead, size + LANES), F32),
            pltpu.VMEM((levels, size, size + LANES), F32),
            pltpu.VMEM((levels, LANES, LANES), F32),
            pltpu.VMEM((8, LANES), F32),
        ],
        name="solve_tail",
    )(shrink_strengths, lead_inverse, *others_lead, *owns_lead, *others_tail, *owns_tail)

    messages = []
    for f in range(own_count):
        for e in range(n_blocks):
            if f == 0 and e == 0:
                messages.append(message)
                continue
            pairs = []
            for s in range(sources):
                source = s - s % own_count + (s % own_count + f) % own_count
                for b in range(n_blocks):
                    pairs.append((source * n_blocks + (b - e) % n_blocks, s * n_blocks + b))
            messages.append(lax.ppermute(message, ("samples", "blocks"), pairs))

    return pl.pallas_call(
        functools.partial(level_kernel, own_count, trait_rows, held_rows),
        out_shape=[
            jax.ShapeDtypeStruct((own_count, 1, levels, traits, width), BF16),
            jax.ShapeDtypeStruct((own_count, 1, levels, traits, n_blocks, levels), F32),
            jax.ShapeDtypeStruct((own_count, 1, levels, traits), F32),
        ],
        in_specs=[vmem] * len(messages),
        out_specs=[vmem] * 3,
        name="level_one",
    )(*messages)


def solution(mesh):
    in_specs = (
        P("blocks", ("groups", "samples")),
        P(None, ("groups", "samples")),
        P(("groups", "samples")),
        P(),
    )
    out_specs = (
        P("folds", "blocks", None, None, ("groups", "samples")),
        P(("groups", "folds"), "blocks", None, None, None, None),
        P(("groups", "folds"), "blocks", None, None),
    )
    return jax.shard_map(
        per_device, mesh=mesh, in_specs=in_specs, out_specs=out_specs, check_vma=False
    )
```

```python
import functools

import jax
import jax.numpy as jnp
from jax import lax
from jax.experimental import pallas as pl
from jax.experimental.pallas import tpu as pltpu
from jax.sharding import PartitionSpec as P

SHRINK_LEVELS = 2
FOLDS = 4
LANES = 128
PANEL = 32
PIVOTS = 8
HIGHEST = lax.Precision.HIGHEST
F32 = jnp.float32
BF16 = jnp.bfloat16


def round_up(value, step):
    return (value + step - 1) // step * step


def dot_nt(left, right):
    return lax.dot_general(left, right, (((1,), (1,)), ((), ())), preferred_element_type=F32)


def spread(value):
    return jnp.broadcast_to(value, (8, LANES))


def sort_kernel(own_count, pad_rows, geno_ref, trait_ref, label_ref, *refs):
    variants, traits = geno_ref.shape[0], trait_ref.shape[0]
    rows = label_ref.shape[1]
    core = lax.axis_index("folds")
    cores = lax.axis_size("folds")
    slot = lax.rem(label_ref[...] + own_count * (cores - 1 - core), FOLDS)
    width = rows // FOLDS
    before = lax.broadcasted_iota(jnp.int32, (rows, rows), 0) < lax.broadcasted_iota(jnp.int32, (rows, rows), 1)
    fold_row = lax.broadcasted_iota(jnp.int32, (16, rows), 0)
    hit = jnp.broadcast_to(slot, (16, rows)) == fold_row
    rank = jnp.dot(
        jnp.where(hit, 1.0, 0.0).astype(BF16),
        jnp.where(before, 1.0, 0.0).astype(BF16),
        preferred_element_type=F32,
    )
    place = jnp.sum(jnp.where(hit, rank + (fold_row * width).astype(F32), 0.0), axis=0, keepdims=True)
    place = place.astype(jnp.int32)
    target = lax.broadcasted_iota(jnp.int32, (rows, rows), 0)
    move = jnp.where(target == jnp.broadcast_to(place, (rows, rows)), 1.0, 0.0).astype(BF16)
    sorted_geno = dot_nt(geno_ref[...], move).astype(BF16)
    sorted_trait = dot_nt(trait_ref[...], move).astype(BF16)
    split = refs[0].shape[0]
    half = refs[0].shape[1]
    height = refs[2].shape[0]
    low = (variants - split) // 16 * 16
    for part in range(2):
        lanes = slice(part * half, (part + 1) * half)
        refs[part][...] = sorted_geno[0:split, lanes]
        ref = refs[2 + part]
        ref[low:height, :] = jnp.zeros((height - low, half), BF16)
        ref[0 : variants - split, :] = sorted_geno[split:variants, lanes]
        ref[pad_rows - split : pad_rows - split + traits, :] = sorted_trait[:, lanes]


def eliminate_panel(panels, first, ones):
    lane = lax.broadcasted_iota(jnp.int32, (8, LANES), 1)
    sub = lax.broadcasted_iota(jnp.int32, (8, LANES), 0)
    systems = range(len(panels))
    count = len(panels[0])
    panels = [list(panel) for panel in panels]
    for b in range(count):
        base_col = first + 8 * b
        in_pivot = (lane >= base_col) & (lane < base_col + 8)
        rest = [(b + 1 + i) % count for i in range(count - 1)]
        cols = [[None] * 8 for _ in systems]
        factors = [{i: [None] * 8 for i in rest} for _ in systems]
        for u in range(8):
            for q in systems:
                cols[q][u] = spread(panels[q][b][:, base_col + u : base_col + u + 1]) * ones
        for u in range(8):
            for q in systems:
                for i in rest:
                    factors[q][i][u] = spread(panels[q][i][:, base_col + u : base_col + u + 1])
        for t in range(8):
            for q in systems:
                inverse = 1.0 / spread(cols[q][t][t : t + 1, :])
                factor = jnp.where(sub == t, -1.0, cols[q][t])
                for u in range(t + 1, 8):
                    row = spread(cols[q][u][t : t + 1, :])
                    cols[q][u] = jnp.where(sub == t, 0.0, cols[q][u]) - (factor * row) * inverse
                row = jnp.where(lane == base_col + t, 1.0, spread(panels[q][b][t : t + 1, :]))
                keep = jnp.where((lane == base_col + t) | (sub == t), 0.0, panels[q][b])
                panels[q][b] = keep - (factor * row) * inverse
        for q in systems:
            rows = [spread(panels[q][b][t : t + 1, :]) for t in range(8)]
            for i in rest:
                parts = [factors[q][i][t] * rows[t] for t in range(8)]
                while len(parts) > 1:
                    parts = [parts[k] + parts[k + 1] for k in range(0, len(parts), 2)]
                panels[q][i] = jnp.where(in_pivot, 0.0, panels[q][i]) - parts[0]
    return panels


def invert_blocks(blocks, ones):
    lane = lax.broadcasted_iota(jnp.int32, (LANES, LANES), 1)
    row = lax.broadcasted_iota(jnp.int32, (LANES, LANES), 0)
    blocks = list(blocks)
    for b in range(LANES // PANEL):
        r0 = PANEL * b
        panels = eliminate_panel(
            [[block[r0 + 8 * i : r0 + 8 * i + 8, :] for i in range(PANEL // 8)] for block in blocks], r0, ones
        )
        for q, block in enumerate(blocks):
            pieces = list(panels[q])
            if r0:
                pieces.insert(0, jnp.zeros((r0, LANES), F32))
            if LANES - PANEL - r0:
                pieces.append(jnp.zeros((LANES - PANEL - r0, LANES), F32))
            wide = jnp.concatenate(pieces, axis=0)
            keep = jnp.where((lane >= r0) & (lane < r0 + PANEL), 0.0, block)
            update = keep - jnp.dot(block, wide, precision=HIGHEST, preferred_element_type=F32)
            blocks[q] = jnp.where((row >= r0) & (row < r0 + PANEL), wide, update)
    return blocks


def dot_f32(left, right):
    return jnp.dot(left, right, precision=HIGHEST, preferred_element_type=F32)


def fold_lanes(own_count, width):
    pick = lax.rem(lax.axis_index("samples"), own_count)
    held = pl.multiple_of(pick * width, width)
    train = [pl.multiple_of(lax.rem(pick + 1 + i, own_count) * width, width) for i in range(own_count - 1)]
    return held, train


def training_product(left, right, train, width, rows):
    acc = None
    for left_other, left_own, right_other, right_own in zip(*left, *right):
        pieces = [(left_other[rows, :], right_other[...])]
        for start in train:
            pieces.append((left_own[rows, pl.ds(start, width)], right_own[:, pl.ds(start, width)]))
        for a, b in pieces:
            part = dot_nt(a, b)
            acc = part if acc is None else acc + part
    return acc


def stages(count, levels, mat_ref, inv_ref, ones_ref, follow):
    def stage(j, carry):
        start = pl.multiple_of(j * LANES, LANES)
        inverses = invert_blocks(
            [mat_ref[r, pl.ds(start, LANES), pl.ds(start, LANES)] for r in range(levels)], ones_ref[...]
        )
        for r in range(levels):
            inv_ref[r] = inverses[r]
        for jj in range(count):

            @pl.when(j == jj)
            def _():
                for r in range(levels):
                    follow(jj, r)

        return carry

    lax.fori_loop(0, count, stage, 0)


def lead_kernel(sources, own_count, learning_tally, *refs):
    shrink_ref = refs[0]
    others, owns = refs[1 : 1 + sources], refs[1 + sources : 1 + 2 * sources]
    out_ref, inv_ref, ones_ref = refs[1 + 2 * sources :]
    levels, size = out_ref.shape[0], out_ref.shape[1]
    width = others[0].shape[1] // own_count
    _, train = fold_lanes(own_count, width)
    ones_ref[...] = jnp.ones((8, LANES), F32)
    diagonal = lax.broadcasted_iota(jnp.int32, (LANES, size), 1) - lax.broadcasted_iota(jnp.int32, (LANES, size), 0)
    for r0 in range(0, size, LANES):
        rows = slice(r0, r0 + LANES)
        acc = training_product((others, owns), (others, owns), train, width, rows) / learning_tally
        for r in range(levels):
            out_ref[r, rows, :] = acc + jnp.where(diagonal == r0, shrink_ref[r], 0.0)

    def follow(j, r):
        c0, c1 = j * LANES, (j + 1) * LANES
        inverse = inv_ref[r]
        spans = [(lo, hi) for lo, hi in ((0, c0), (c1, size)) if hi > lo]
        solved = [dot_f32(inverse, out_ref[r, c0:c1, lo:hi]) for lo, hi in spans]
        for lo, hi in spans:
            column = out_ref[r, lo:hi, c0:c1]
            for (left, right), value in zip(spans, solved):
                out_ref[r, lo:hi, left:right] = out_ref[r, lo:hi, left:right] - dot_f32(column, value)
            out_ref[r, lo:hi, c0:c1] = -dot_f32(column, inverse)
        for (left, right), value in zip(spans, solved):
            out_ref[r, c0:c1, left:right] = value
        out_ref[r, c0:c1, c0:c1] = inverse

    stages(size // LANES, levels, out_ref, inv_ref, ones_ref, follow)


def tail_kernel(sources, own_count, learning_tally, trait_rows, *refs):
    shrink_ref, lead_ref = refs[0:2]
    first = (refs[2 : 2 + sources], refs[2 + sources : 2 + 2 * sources])
    last = (refs[2 + 2 * sources : 2 + 3 * sources], refs[2 + 3 * sources : 2 + 4 * sources])
    message_ref, wide_ref, solved_ref, mat_ref, inv_ref, ones_ref = refs[2 + 4 * sources :]
    levels, lead = lead_ref.shape[0], lead_ref.shape[1]
    size, total = mat_ref.shape[1], mat_ref.shape[2]
    width = first[0][0].shape[1] // own_count
    height = size + trait_rows
    held, train = fold_lanes(own_count, width)
    ones_ref[...] = jnp.ones((8, LANES), F32)
    for r0 in range(0, lead, LANES):
        rows = slice(r0, r0 + LANES)
        wide_ref[rows, 0:height] = training_product(first, last, train, width, rows) / learning_tally
        wide_ref[rows, height:total] = jnp.zeros((LANES, total - height), F32)
    for r in range(levels):
        solved_ref[r] = dot_f32(lead_ref[r], wide_ref[...])
    diagonal = lax.broadcasted_iota(jnp.int32, (LANES, height), 1) - lax.broadcasted_iota(
        jnp.int32, (LANES, height), 0
    )
    for r0 in range(0, size, LANES):
        rows = slice(r0, r0 + LANES)
        side = training_product(last, first, train, width, rows) / learning_tally
        acc = training_product(last, last, train, width, rows) / learning_tally
        for r in range(levels):
            mat_ref[r, rows, 0:height] = acc + jnp.where(diagonal == r0, shrink_ref[r], 0.0)
            mat_ref[r, rows, height:total] = jnp.zeros((LANES, total - height), F32)
            mat_ref[r, rows, :] = mat_ref[r, rows, :] - dot_f32(side, solved_ref[r])

    def follow(j, r):
        c0, c1 = j * LANES, (j + 1) * LANES
        solved = dot_f32(inv_ref[r], mat_ref[r, c0:c1, c1:total])
        for lo, hi in ((0, c0), (c1, size)):
            if hi > lo:
                mat_ref[r, lo:hi, c1:total] = mat_ref[r, lo:hi, c1:total] - dot_f32(mat_ref[r, lo:hi, c0:c1], solved)
        mat_ref[r, c0:c1, c1:total] = solved

    stages(size // LANES, levels, mat_ref, inv_ref, ones_ref, follow)
    for r in range(levels):
        low = mat_ref[r, :, size:total]
        top = solved_ref[r, :, size:total] - dot_f32(solved_ref[r, :, 0:size], low)
        top = jnp.transpose(top)[0:trait_rows, :].astype(BF16)
        low = jnp.transpose(low)[0:trait_rows, :].astype(BF16)
        for s in range(sources):
            value = jnp.dot(top, first[1][s][:, pl.ds(held, width)], preferred_element_type=F32) + jnp.dot(
                low, last[1][s][0:size, pl.ds(held, width)], preferred_element_type=F32
            )
            message_ref[r * trait_rows : (r + 1) * trait_rows, s * width : (s + 1) * width] = value.astype(BF16)
    for s in range(sources):
        message_ref[levels * trait_rows : (levels + 1) * trait_rows, s * width : (s + 1) * width] = last[1][s][
            size : size + trait_rows, pl.ds(held, width)
        ]


def level_kernel(own_count, trait_rows, held_rows, *refs):
    pred_ref, gram_ref, cross_ref = refs[-3:]
    n_blocks = (len(refs) - 3) // own_count
    messages = [refs[f * n_blocks : (f + 1) * n_blocks] for f in range(own_count)]
    traits, levels, width = pred_ref.shape[2:]
    me = lax.axis_index("samples")
    block = lax.axis_index("blocks")
    pick = lax.rem(me, own_count)
    lane = lax.broadcasted_iota(jnp.int32, (trait_rows, LANES), 1)
    for f in range(own_count):
        slot = lax.rem(pick + f, own_count)
        mine = messages[f][0]
        held = pl.multiple_of((me ^ (me - pick + slot)) * width, width)
        own = [
            mine[r * trait_rows : (r + 1) * trait_rows, pl.ds(held, width)].astype(F32)[0:traits]
            for r in range(levels)
        ]
        pred_ref[slot, 0] = jnp.stack(own, axis=1).astype(BF16)
        wide = [
            [messages[f][e][s * trait_rows : (s + 1) * trait_rows, :].astype(F32) for s in range(levels)]
            for e in range(n_blocks)
        ]
        trait = mine[levels * trait_rows : (levels + 1) * trait_rows, :].astype(F32)
        for r in range(levels):
            out = jnp.where(lane == n_blocks * levels, jnp.sum(wide[0][r] * trait, axis=1, keepdims=True), 0.0)
            for e in range(n_blocks):
                column = lax.rem(block - e + n_blocks, n_blocks) * levels
                for s in range(levels):
                    total = jnp.sum(wide[0][r] * wide[e][s], axis=1, keepdims=True)
                    out = out + jnp.where(lane == column + s, total, 0.0)
            rows = jnp.transpose(out) / held_rows
            for c in range(n_blocks):
                gram_ref[slot, 0, r, c] = rows[c * levels : (c + 1) * levels, 0:traits]
            cross_ref[slot, 0, r : r + 1, :] = rows[n_blocks * levels : n_blocks * levels + 1, 0:traits]


def per_device(allele_dosage_table, phenotype_values, individual_partition_label, shrink_strengths):
    cores = lax.axis_size("folds")
    sources = lax.axis_size("samples")
    n_blocks = lax.axis_size("blocks")
    own_count = FOLDS // cores
    levels = shrink_strengths.shape[0]
    variants, samples = allele_dosage_table.shape
    traits = phenotype_values.shape[0]
    width = samples // FOLDS
    held_rows = sources * width
    learning_tally = sources * samples - held_rows
    pad_rows = round_up(variants, LANES)
    lead = pad_rows // LANES // 2 * LANES
    size = pad_rows - lead
    trait_rows = round_up(traits, 32)
    half = own_count * width
    vmem = pl.BlockSpec(memory_space=pltpu.VMEM)
    smem = pl.BlockSpec(memory_space=pltpu.SMEM)

    other_lead, own_lead, other_tail, own_tail = pl.pallas_call(
        functools.partial(sort_kernel, own_count, pad_rows),
        out_shape=[jax.ShapeDtypeStruct((lead, half), BF16)] * 2
        + [jax.ShapeDtypeStruct((size + trait_rows, half), BF16)] * 2,
        in_specs=[vmem] * 3,
        out_specs=[vmem] * 4,
        name="sort_samples",
    )(allele_dosage_table, phenotype_values, individual_partition_label.reshape(1, samples))

    def fetch(other):
        return [other] + [
            lax.ppermute(other, "samples", [(i, i ^ d) for i in range(sources)]) for d in range(1, sources)
        ]

    def swap(own, others):
        return [own] + [lax.ppermute(x, "folds", [(i, cores - 1 - i) for i in range(cores)]) for x in others[1:]]

    others_lead = fetch(other_lead)
    owns_lead = swap(own_lead, others_lead)
    other_tail, *others_lead[1:] = lax.optimization_barrier((other_tail, *others_lead[1:]))
    others_tail = fetch(other_tail)
    lead_inverse = pl.pallas_call(
        functools.partial(lead_kernel, sources, own_count, learning_tally),
        out_shape=jax.ShapeDtypeStruct((levels, lead, lead), F32),
        in_specs=[smem] + [vmem] * (2 * sources),
        out_specs=vmem,
        scratch_shapes=[pltpu.VMEM((levels, LANES, LANES), F32), pltpu.VMEM((8, LANES), F32)],
        name="invert_lead",
    )(shrink_strengths, *others_lead, *owns_lead)
    lead_inverse, *others_tail[1:] = lax.optimization_barrier((lead_inverse, *others_tail[1:]))
    owns_tail = swap(own_tail, others_tail)
    message = pl.pallas_call(
        functools.partial(tail_kernel, sources, own_count, learning_tally, trait_rows),
        out_shape=jax.ShapeDtypeStruct(((levels + 1) * trait_rows, sources * width), BF16),
        in_specs=[smem] + [vmem] * (1 + 4 * sources),
        out_specs=vmem,
        scratch_shapes=[
            pltpu.VMEM((lead, size + LANES), F32),
            pltpu.VMEM((levels, lead, size + LANES), F32),
            pltpu.VMEM((levels, size, size + LANES), F32),
            pltpu.VMEM((levels, LANES, LANES), F32),
            pltpu.VMEM((8, LANES), F32),
        ],
        name="solve_tail",
    )(shrink_strengths, lead_inverse, *others_lead, *owns_lead, *others_tail, *owns_tail)

    messages = []
    for f in range(own_count):
        for e in range(n_blocks):
            if f == 0 and e == 0:
                messages.append(message)
                continue
            pairs = []
            for s in range(sources):
                source = s - s % own_count + (s % own_count + f) % own_count
                for b in range(n_blocks):
                    pairs.append((source * n_blocks + (b - e) % n_blocks, s * n_blocks + b))
            messages.append(lax.ppermute(message, ("samples", "blocks"), pairs))

    preds, gram, cross = pl.pallas_call(
        functools.partial(level_kernel, own_count, trait_rows, held_rows),
        out_shape=[
            jax.ShapeDtypeStruct((own_count, 1, traits, levels, width), BF16),
            jax.ShapeDtypeStruct((own_count, 1, levels, n_blocks, levels, traits), F32),
            jax.ShapeDtypeStruct((own_count, 1, levels, traits), F32),
        ],
        in_specs=[vmem] * len(messages),
        out_specs=[vmem] * 3,
        name="level_one",
    )(*messages)
    return jnp.swapaxes(preds, 2, 3), jnp.moveaxis(gram, 5, 3), cross


def solution(mesh):
    in_specs = (
        P("blocks", ("groups", "samples")),
        P(None, ("groups", "samples")),
        P(("groups", "samples")),
        P(),
    )
    out_specs = (
        P("folds", "blocks", None, None, ("groups", "samples")),
        P(("groups", "folds"), "blocks", None, None, None, None),
        P(("groups", "folds"), "blocks", None, None),
    )
    return jax.shard_map(
        per_device, mesh=mesh, in_specs=in_specs, out_specs=out_specs, check_vma=False
    )
```

```python
import functools

import jax
import jax.numpy as jnp
from jax import lax
from jax.experimental import pallas as pl
from jax.experimental.pallas import tpu as pltpu
from jax.sharding import PartitionSpec as P

SHRINK_LEVELS = 2
FOLDS = 4
LANES = 128
PANEL = 32
PIVOTS = 8
HIGHEST = lax.Precision.HIGHEST
VMEM_SHARE = 2 << 20
F32 = jnp.float32
BF16 = jnp.bfloat16


def round_up(value, step):
    return (value + step - 1) // step * step


def dot_nt(left, right):
    return lax.dot_general(left, right, (((1,), (1,)), ((), ())), preferred_element_type=F32)


def spread(value):
    return jnp.broadcast_to(value, (8, LANES))


def sort_kernel(own_count, pad_rows, geno_ref, trait_ref, label_ref, *refs):
    variants, traits = geno_ref.shape[0], trait_ref.shape[0]
    rows = label_ref.shape[1]
    core = lax.axis_index("folds")
    cores = lax.axis_size("folds")
    slot = lax.rem(label_ref[...] + own_count * (cores - 1 - core), FOLDS)
    width = rows // FOLDS
    before = lax.broadcasted_iota(jnp.int32, (rows, rows), 0) < lax.broadcasted_iota(jnp.int32, (rows, rows), 1)
    fold_row = lax.broadcasted_iota(jnp.int32, (16, rows), 0)
    hit = jnp.broadcast_to(slot, (16, rows)) == fold_row
    rank = jnp.dot(
        jnp.where(hit, 1.0, 0.0).astype(BF16),
        jnp.where(before, 1.0, 0.0).astype(BF16),
        preferred_element_type=F32,
    )
    place = jnp.sum(jnp.where(hit, rank + (fold_row * width).astype(F32), 0.0), axis=0, keepdims=True)
    place = place.astype(jnp.int32)
    target = lax.broadcasted_iota(jnp.int32, (rows, rows), 0)
    move = jnp.where(target == jnp.broadcast_to(place, (rows, rows)), 1.0, 0.0).astype(BF16)
    sorted_geno = dot_nt(geno_ref[...], move).astype(BF16)
    sorted_trait = dot_nt(trait_ref[...], move).astype(BF16)
    split = refs[0].shape[0]
    half = refs[0].shape[1]
    height = refs[2].shape[0]
    low = (variants - split) // 16 * 16
    for part in range(2):
        lanes = slice(part * half, (part + 1) * half)
        refs[part][...] = sorted_geno[0:split, lanes]
        ref = refs[2 + part]
        ref[low:height, :] = jnp.zeros((height - low, half), BF16)
        ref[0 : variants - split, :] = sorted_geno[split:variants, lanes]
        ref[pad_rows - split : pad_rows - split + traits, :] = sorted_trait[:, lanes]


def eliminate_panel(panels, first, ones):
    lane = lax.broadcasted_iota(jnp.int32, (8, LANES), 1)
    sub = lax.broadcasted_iota(jnp.int32, (8, LANES), 0)
    systems = range(len(panels))
    count = len(panels[0])
    panels = [list(panel) for panel in panels]
    for b in range(count):
        base_col = first + 8 * b
        in_pivot = (lane >= base_col) & (lane < base_col + 8)
        rest = [(b + 1 + i) % count for i in range(count - 1)]
        cols = [[None] * 8 for _ in systems]
        factors = [{i: [None] * 8 for i in rest} for _ in systems]
        for u in range(8):
            for q in systems:
                cols[q][u] = spread(panels[q][b][:, base_col + u : base_col + u + 1]) * ones
        for u in range(8):
            for q in systems:
                for i in rest:
                    factors[q][i][u] = spread(panels[q][i][:, base_col + u : base_col + u + 1])
        for t in range(8):
            for q in systems:
                inverse = 1.0 / spread(cols[q][t][t : t + 1, :])
                factor = jnp.where(sub == t, -1.0, cols[q][t])
                for u in range(t + 1, 8):
                    row = spread(cols[q][u][t : t + 1, :])
                    cols[q][u] = jnp.where(sub == t, 0.0, cols[q][u]) - (factor * row) * inverse
                row = jnp.where(lane == base_col + t, 1.0, spread(panels[q][b][t : t + 1, :]))
                keep = jnp.where((lane == base_col + t) | (sub == t), 0.0, panels[q][b])
                panels[q][b] = keep - (factor * row) * inverse
        for q in systems:
            rows = [spread(panels[q][b][t : t + 1, :]) for t in range(8)]
            for i in rest:
                parts = [factors[q][i][t] * rows[t] for t in range(8)]
                while len(parts) > 1:
                    parts = [parts[k] + parts[k + 1] for k in range(0, len(parts), 2)]
                panels[q][i] = jnp.where(in_pivot, 0.0, panels[q][i]) - parts[0]
    return panels


def invert_blocks(blocks, ones):
    lane = lax.broadcasted_iota(jnp.int32, (LANES, LANES), 1)
    row = lax.broadcasted_iota(jnp.int32, (LANES, LANES), 0)
    blocks = list(blocks)
    for b in range(LANES // PANEL):
        r0 = PANEL * b
        panels = eliminate_panel(
            [[block[r0 + 8 * i : r0 + 8 * i + 8, :] for i in range(PANEL // 8)] for block in blocks], r0, ones
        )
        for q, block in enumerate(blocks):
            pieces = list(panels[q])
            if r0:
                pieces.insert(0, jnp.zeros((r0, LANES), F32))
            if LANES - PANEL - r0:
                pieces.append(jnp.zeros((LANES - PANEL - r0, LANES), F32))
            wide = jnp.concatenate(pieces, axis=0)
            keep = jnp.where((lane >= r0) & (lane < r0 + PANEL), 0.0, block)
            update = keep - jnp.dot(block, wide, precision=HIGHEST, preferred_element_type=F32)
            blocks[q] = jnp.where((row >= r0) & (row < r0 + PANEL), wide, update)
    return blocks


def dot_f32(left, right):
    return jnp.dot(left, right, precision=HIGHEST, preferred_element_type=F32)


def fold_lanes(own_count, width):
    pick = lax.rem(lax.axis_index("samples"), own_count)
    held = pl.multiple_of(pick * width, width)
    train = [pl.multiple_of(lax.rem(pick + 1 + i, own_count) * width, width) for i in range(own_count - 1)]
    return held, train


def training_product(left, right, train, width, rows):
    acc = None
    for left_other, left_own, right_other, right_own in zip(*left, *right):
        pieces = [(left_other[rows, :], right_other[...])]
        for start in train:
            pieces.append((left_own[rows, pl.ds(start, width)], right_own[:, pl.ds(start, width)]))
        for a, b in pieces:
            part = dot_nt(a, b)
            acc = part if acc is None else acc + part
    return acc


def stages(count, levels, mat_ref, inv_ref, ones_ref, follow):
    def stage(j, carry):
        start = pl.multiple_of(j * LANES, LANES)
        inverses = invert_blocks(
            [mat_ref[r, pl.ds(start, LANES), pl.ds(start, LANES)] for r in range(levels)], ones_ref[...]
        )
        for r in range(levels):
            inv_ref[r] = inverses[r]
        for jj in range(count):

            @pl.when(j == jj)
            def _():
                for r in range(levels):
                    follow(jj, r)

        return carry

    lax.fori_loop(0, count, stage, 0)


def lead_kernel(sources, own_count, learning_tally, *refs):
    shrink_ref = refs[0]
    others, owns = refs[1 : 1 + sources], refs[1 + sources : 1 + 2 * sources]
    out_ref, inv_ref, ones_ref = refs[1 + 2 * sources :]
    levels, size = out_ref.shape[0], out_ref.shape[1]
    width = others[0].shape[1] // own_count
    _, train = fold_lanes(own_count, width)
    ones_ref[...] = jnp.ones((8, LANES), F32)
    diagonal = lax.broadcasted_iota(jnp.int32, (LANES, size), 1) - lax.broadcasted_iota(jnp.int32, (LANES, size), 0)
    for r0 in range(0, size, LANES):
        rows = slice(r0, r0 + LANES)
        acc = training_product((others, owns), (others, owns), train, width, rows) / learning_tally
        for r in range(levels):
            out_ref[r, rows, :] = acc + jnp.where(diagonal == r0, shrink_ref[r], 0.0)

    def follow(j, r):
        c0, c1 = j * LANES, (j + 1) * LANES
        inverse = inv_ref[r]
        spans = [(lo, hi) for lo, hi in ((0, c0), (c1, size)) if hi > lo]
        solved = [dot_f32(inverse, out_ref[r, c0:c1, lo:hi]) for lo, hi in spans]
        for lo, hi in spans:
            column = out_ref[r, lo:hi, c0:c1]
            for (left, right), value in zip(spans, solved):
                out_ref[r, lo:hi, left:right] = out_ref[r, lo:hi, left:right] - dot_f32(column, value)
            out_ref[r, lo:hi, c0:c1] = -dot_f32(column, inverse)
        for (left, right), value in zip(spans, solved):
            out_ref[r, c0:c1, left:right] = value
        out_ref[r, c0:c1, c0:c1] = inverse

    stages(size // LANES, levels, out_ref, inv_ref, ones_ref, follow)


def tail_kernel(sources, own_count, learning_tally, trait_rows, *refs):
    shrink_ref, lead_ref = refs[0:2]
    first = (refs[2 : 2 + sources], refs[2 + sources : 2 + 2 * sources])
    last = (refs[2 + 2 * sources : 2 + 3 * sources], refs[2 + 3 * sources : 2 + 4 * sources])
    message_ref, wide_ref, solved_ref, mat_ref, inv_ref, ones_ref = refs[2 + 4 * sources :]
    levels, lead = lead_ref.shape[0], lead_ref.shape[1]
    size, total = mat_ref.shape[1], mat_ref.shape[2]
    width = first[0][0].shape[1] // own_count
    height = size + trait_rows
    held, train = fold_lanes(own_count, width)
    ones_ref[...] = jnp.ones((8, LANES), F32)
    for r0 in range(0, lead, LANES):
        rows = slice(r0, r0 + LANES)
        wide_ref[rows, 0:height] = training_product(first, last, train, width, rows) / learning_tally
        wide_ref[rows, height:total] = jnp.zeros((LANES, total - height), F32)
    for r in range(levels):
        solved_ref[r] = dot_f32(lead_ref[r], wide_ref[...])
    diagonal = lax.broadcasted_iota(jnp.int32, (LANES, height), 1) - lax.broadcasted_iota(
        jnp.int32, (LANES, height), 0
    )
    for r0 in range(0, size, LANES):
        rows = slice(r0, r0 + LANES)
        side = training_product(last, first, train, width, rows) / learning_tally
        acc = training_product(last, last, train, width, rows) / learning_tally
        for r in range(levels):
            mat_ref[r, rows, 0:height] = acc + jnp.where(diagonal == r0, shrink_ref[r], 0.0)
            mat_ref[r, rows, height:total] = jnp.zeros((LANES, total - height), F32)
            mat_ref[r, rows, :] = mat_ref[r, rows, :] - dot_f32(side, solved_ref[r])

    def follow(j, r):
        c0, c1 = j * LANES, (j + 1) * LANES
        solved = dot_f32(inv_ref[r], mat_ref[r, c0:c1, c1:total])
        for lo, hi in ((0, c0), (c1, size)):
            if hi > lo:
                mat_ref[r, lo:hi, c1:total] = mat_ref[r, lo:hi, c1:total] - dot_f32(mat_ref[r, lo:hi, c0:c1], solved)
        mat_ref[r, c0:c1, c1:total] = solved

    stages(size // LANES, levels, mat_ref, inv_ref, ones_ref, follow)
    for r in range(levels):
        low = mat_ref[r, :, size:total]
        top = solved_ref[r, :, size:total] - dot_f32(solved_ref[r, :, 0:size], low)
        top = jnp.transpose(top)[0:trait_rows, :].astype(BF16)
        low = jnp.transpose(low)[0:trait_rows, :].astype(BF16)
        for s in range(sources):
            value = jnp.dot(top, first[1][s][:, pl.ds(held, width)], preferred_element_type=F32) + jnp.dot(
                low, last[1][s][0:size, pl.ds(held, width)], preferred_element_type=F32
            )
            message_ref[r * trait_rows : (r + 1) * trait_rows, s * width : (s + 1) * width] = value.astype(BF16)
    for s in range(sources):
        message_ref[levels * trait_rows : (levels + 1) * trait_rows, s * width : (s + 1) * width] = last[1][s][
            size : size + trait_rows, pl.ds(held, width)
        ]


def level_kernel(own_count, trait_rows, held_rows, *refs):
    pred_ref, gram_ref, cross_ref = refs[-3:]
    n_blocks = (len(refs) - 3) // own_count
    messages = [refs[f * n_blocks : (f + 1) * n_blocks] for f in range(own_count)]
    traits, levels, width = pred_ref.shape[2:]
    me = lax.axis_index("samples")
    block = lax.axis_index("blocks")
    pick = lax.rem(me, own_count)
    lane = lax.broadcasted_iota(jnp.int32, (trait_rows, LANES), 1)
    for f in range(own_count):
        slot = lax.rem(pick + f, own_count)
        mine = messages[f][0]
        held = pl.multiple_of((me ^ (me - pick + slot)) * width, width)
        own = [
            mine[r * trait_rows : (r + 1) * trait_rows, pl.ds(held, width)].astype(F32)[0:traits]
            for r in range(levels)
        ]
        pred_ref[slot, 0] = jnp.stack(own, axis=1).astype(BF16)
        wide = [
            [messages[f][e][s * trait_rows : (s + 1) * trait_rows, :].astype(F32) for s in range(levels)]
            for e in range(n_blocks)
        ]
        trait = mine[levels * trait_rows : (levels + 1) * trait_rows, :].astype(F32)
        for r in range(levels):
            out = jnp.where(lane == n_blocks * levels, jnp.sum(wide[0][r] * trait, axis=1, keepdims=True), 0.0)
            for e in range(n_blocks):
                column = lax.rem(block - e + n_blocks, n_blocks) * levels
                for s in range(levels):
                    total = jnp.sum(wide[0][r] * wide[e][s], axis=1, keepdims=True)
                    out = out + jnp.where(lane == column + s, total, 0.0)
            rows = jnp.transpose(out) / held_rows
            for c in range(n_blocks):
                gram_ref[slot, 0, r, c] = rows[c * levels : (c + 1) * levels, 0:traits]
            cross_ref[slot, 0, r : r + 1, :] = rows[n_blocks * levels : n_blocks * levels + 1, 0:traits]


def land(value, copies):
    if copies * value.size * value.dtype.itemsize > VMEM_SHARE:
        return value
    return pltpu.with_memory_space_constraint(value, pltpu.VMEM)


def per_device(allele_dosage_table, phenotype_values, individual_partition_label, shrink_strengths):
    cores = lax.axis_size("folds")
    sources = lax.axis_size("samples")
    n_blocks = lax.axis_size("blocks")
    own_count = FOLDS // cores
    levels = shrink_strengths.shape[0]
    variants, samples = allele_dosage_table.shape
    traits = phenotype_values.shape[0]
    width = samples // FOLDS
    held_rows = sources * width
    learning_tally = sources * samples - held_rows
    pad_rows = round_up(variants, LANES)
    lead = pad_rows // LANES // 2 * LANES
    size = pad_rows - lead
    trait_rows = round_up(traits, 32)
    half = own_count * width
    vmem = pl.BlockSpec(memory_space=pltpu.VMEM)
    smem = pl.BlockSpec(memory_space=pltpu.SMEM)

    other_lead, own_lead, other_tail, own_tail = pl.pallas_call(
        functools.partial(sort_kernel, own_count, pad_rows),
        out_shape=[jax.ShapeDtypeStruct((lead, half), BF16)] * 2
        + [jax.ShapeDtypeStruct((size + trait_rows, half), BF16)] * 2,
        in_specs=[vmem] * 3,
        out_specs=[vmem] * 4,
        name="sort_samples",
    )(allele_dosage_table, phenotype_values, individual_partition_label.reshape(1, samples))

    def fetch(other):
        return [other] + [
            land(lax.ppermute(other, "samples", [(i, i ^ d) for i in range(sources)]), 2 * sources) for d in range(1, sources)
        ]

    def swap(own, others):
        return [own] + [land(lax.ppermute(x, "folds", [(i, cores - 1 - i) for i in range(cores)]), 2 * sources) for x in others[1:]]

    others_lead = fetch(other_lead)
    owns_lead = swap(own_lead, others_lead)
    other_tail, *others_lead[1:] = lax.optimization_barrier((other_tail, *others_lead[1:]))
    others_tail = fetch(other_tail)
    lead_inverse = pl.pallas_call(
        functools.partial(lead_kernel, sources, own_count, learning_tally),
        out_shape=jax.ShapeDtypeStruct((levels, lead, lead), F32),
        in_specs=[smem] + [vmem] * (2 * sources),
        out_specs=vmem,
        scratch_shapes=[pltpu.VMEM((levels, LANES, LANES), F32), pltpu.VMEM((8, LANES), F32)],
        name="invert_lead",
    )(shrink_strengths, *others_lead, *owns_lead)
    lead_inverse, *others_tail[1:] = lax.optimization_barrier((land(lead_inverse, 1), *others_tail[1:]))
    owns_tail = swap(own_tail, others_tail)
    message = pl.pallas_call(
        functools.partial(tail_kernel, sources, own_count, learning_tally, trait_rows),
        out_shape=jax.ShapeDtypeStruct(((levels + 1) * trait_rows, sources * width), BF16),
        in_specs=[smem] + [vmem] * (1 + 4 * sources),
        out_specs=vmem,
        scratch_shapes=[
            pltpu.VMEM((lead, size + LANES), F32),
            pltpu.VMEM((levels, lead, size + LANES), F32),
            pltpu.VMEM((levels, size, size + LANES), F32),
            pltpu.VMEM((levels, LANES, LANES), F32),
            pltpu.VMEM((8, LANES), F32),
        ],
        name="solve_tail",
    )(shrink_strengths, lead_inverse, *others_lead, *owns_lead, *others_tail, *owns_tail)

    messages = []
    for f in range(own_count):
        for e in range(n_blocks):
            if f == 0 and e == 0:
                messages.append(message)
                continue
            pairs = []
            for s in range(sources):
                source = s - s % own_count + (s % own_count + f) % own_count
                for b in range(n_blocks):
                    pairs.append((source * n_blocks + (b - e) % n_blocks, s * n_blocks + b))
            messages.append(land(lax.ppermute(message, ("samples", "blocks"), pairs), own_count * n_blocks))

    preds, gram, cross = pl.pallas_call(
        functools.partial(level_kernel, own_count, trait_rows, held_rows),
        out_shape=[
            jax.ShapeDtypeStruct((own_count, 1, traits, levels, width), BF16),
            jax.ShapeDtypeStruct((own_count, 1, levels, n_blocks, levels, traits), F32),
            jax.ShapeDtypeStruct((own_count, 1, levels, traits), F32),
        ],
        in_specs=[vmem] * len(messages),
        out_specs=[vmem] * 3,
        name="level_one",
    )(*messages)
    return jnp.swapaxes(preds, 2, 3), jnp.moveaxis(gram, 5, 3), cross


def solution(mesh):
    in_specs = (
        P("blocks", ("groups", "samples")),
        P(None, ("groups", "samples")),
        P(("groups", "samples")),
        P(),
    )
    out_specs = (
        P("folds", "blocks", None, None, ("groups", "samples")),
        P(("groups", "folds"), "blocks", None, None, None, None),
        P(("groups", "folds"), "blocks", None, None),
    )
    return jax.shard_map(
        per_device, mesh=mesh, in_specs=in_specs, out_specs=out_specs, check_vma=False
    )
```

```python
import functools

import jax
import jax.numpy as jnp
from jax import lax
from jax.experimental import pallas as pl
from jax.experimental.pallas import tpu as pltpu
from jax.sharding import PartitionSpec as P

SHRINK_LEVELS = 2
FOLDS = 4
LANES = 128
PANEL = 32
PIVOTS = 8
HIGHEST = lax.Precision.HIGHEST
VMEM_SHARE = 2 << 20
F32 = jnp.float32
BF16 = jnp.bfloat16


def round_up(value, step):
    return (value + step - 1) // step * step


def dot_nt(left, right):
    return lax.dot_general(left, right, (((1,), (1,)), ((), ())), preferred_element_type=F32)


def spread(value):
    return jnp.broadcast_to(value, (8, LANES))


def sort_kernel(own_count, pad_rows, geno_ref, trait_ref, label_ref, *refs):
    variants, traits = geno_ref.shape[0], trait_ref.shape[0]
    rows = label_ref.shape[1]
    core = lax.axis_index("folds")
    cores = lax.axis_size("folds")
    slot = lax.rem(label_ref[...] + own_count * (cores - 1 - core), FOLDS)
    width = rows // FOLDS
    before = lax.broadcasted_iota(jnp.int32, (rows, rows), 0) < lax.broadcasted_iota(jnp.int32, (rows, rows), 1)
    fold_row = lax.broadcasted_iota(jnp.int32, (16, rows), 0)
    hit = jnp.broadcast_to(slot, (16, rows)) == fold_row
    rank = jnp.dot(
        jnp.where(hit, 1.0, 0.0).astype(BF16),
        jnp.where(before, 1.0, 0.0).astype(BF16),
        preferred_element_type=F32,
    )
    place = jnp.sum(jnp.where(hit, rank + (fold_row * width).astype(F32), 0.0), axis=0, keepdims=True)
    place = place.astype(jnp.int32)
    target = lax.broadcasted_iota(jnp.int32, (rows, rows), 0)
    move = jnp.where(target == jnp.broadcast_to(place, (rows, rows)), 1.0, 0.0).astype(BF16)
    sorted_geno = dot_nt(geno_ref[...], move).astype(BF16)
    sorted_trait = dot_nt(trait_ref[...], move).astype(BF16)
    split = refs[0].shape[0]
    half = refs[0].shape[1]
    height = refs[2].shape[0]
    low = (variants - split) // 16 * 16
    for part in range(2):
        lanes = slice(part * half, (part + 1) * half)
        refs[part][...] = sorted_geno[0:split, lanes]
        ref = refs[2 + part]
        ref[low:height, :] = jnp.zeros((height - low, half), BF16)
        ref[0 : variants - split, :] = sorted_geno[split:variants, lanes]
        ref[pad_rows - split : pad_rows - split + traits, :] = sorted_trait[:, lanes]


def eliminate_panel(panels, first, ones):
    lane = lax.broadcasted_iota(jnp.int32, (8, LANES), 1)
    sub = lax.broadcasted_iota(jnp.int32, (8, LANES), 0)
    systems = range(len(panels))
    count = len(panels[0])
    panels = [list(panel) for panel in panels]
    for b in range(count):
        base_col = first + 8 * b
        in_pivot = (lane >= base_col) & (lane < base_col + 8)
        rest = [(b + 1 + i) % count for i in range(count - 1)]
        cols = [[None] * 8 for _ in systems]
        factors = [{i: [None] * 8 for i in rest} for _ in systems]
        for u in range(8):
            for q in systems:
                cols[q][u] = spread(panels[q][b][:, base_col + u : base_col + u + 1]) * ones
        for u in range(8):
            for q in systems:
                for i in rest:
                    factors[q][i][u] = spread(panels[q][i][:, base_col + u : base_col + u + 1])
        for t in range(8):
            for q in systems:
                inverse = 1.0 / spread(cols[q][t][t : t + 1, :])
                factor = jnp.where(sub == t, -1.0, cols[q][t])
                for u in range(t + 1, 8):
                    row = spread(cols[q][u][t : t + 1, :])
                    cols[q][u] = jnp.where(sub == t, 0.0, cols[q][u]) - (factor * row) * inverse
                row = jnp.where(lane == base_col + t, 1.0, spread(panels[q][b][t : t + 1, :]))
                keep = jnp.where((lane == base_col + t) | (sub == t), 0.0, panels[q][b])
                panels[q][b] = keep - (factor * row) * inverse
        for q in systems:
            rows = [spread(panels[q][b][t : t + 1, :]) for t in range(8)]
            for i in rest:
                parts = [factors[q][i][t] * rows[t] for t in range(8)]
                while len(parts) > 1:
                    parts = [parts[k] + parts[k + 1] for k in range(0, len(parts), 2)]
                panels[q][i] = jnp.where(in_pivot, 0.0, panels[q][i]) - parts[0]
    return panels


def invert_blocks(blocks, ones):
    lane = lax.broadcasted_iota(jnp.int32, (LANES, LANES), 1)
    row = lax.broadcasted_iota(jnp.int32, (LANES, LANES), 0)
    blocks = list(blocks)
    for b in range(LANES // PANEL):
        r0 = PANEL * b
        panels = eliminate_panel(
            [[block[r0 + 8 * i : r0 + 8 * i + 8, :] for i in range(PANEL // 8)] for block in blocks], r0, ones
        )
        for q, block in enumerate(blocks):
            pieces = list(panels[q])
            if r0:
                pieces.insert(0, jnp.zeros((r0, LANES), F32))
            if LANES - PANEL - r0:
                pieces.append(jnp.zeros((LANES - PANEL - r0, LANES), F32))
            wide = jnp.concatenate(pieces, axis=0)
            keep = jnp.where((lane >= r0) & (lane < r0 + PANEL), 0.0, block)
            update = keep - jnp.dot(block, wide, precision=HIGHEST, preferred_element_type=F32)
            blocks[q] = jnp.where((row >= r0) & (row < r0 + PANEL), wide, update)
    return blocks


def dot_f32(left, right):
    return jnp.dot(left, right, precision=HIGHEST, preferred_element_type=F32)


def fold_lanes(own_count, width):
    pick = lax.rem(lax.axis_index("samples"), own_count)
    held = pl.multiple_of(pick * width, width)
    train = [pl.multiple_of(lax.rem(pick + 1 + i, own_count) * width, width) for i in range(own_count - 1)]
    return held, train


def training_product(left, right, train, width, rows):
    lefts, rights = [], []
    for left_other, left_own, right_other, right_own in zip(*left, *right):
        lefts.append(left_other[rows, :])
        rights.append(right_other[...])
        for start in train:
            lefts.append(left_own[rows, pl.ds(start, width)])
            rights.append(right_own[:, pl.ds(start, width)])
    return dot_nt(jnp.concatenate(lefts, axis=1), jnp.concatenate(rights, axis=1))


def stages(count, levels, mat_ref, inv_ref, ones_ref, follow):
    def stage(j, carry):
        start = pl.multiple_of(j * LANES, LANES)
        inverses = invert_blocks(
            [mat_ref[r, pl.ds(start, LANES), pl.ds(start, LANES)] for r in range(levels)], ones_ref[...]
        )
        for r in range(levels):
            inv_ref[r] = inverses[r]
        for jj in range(count):

            @pl.when(j == jj)
            def _():
                for r in range(levels):
                    follow(jj, r)

        return carry

    lax.fori_loop(0, count, stage, 0)


def lead_kernel(sources, own_count, learning_tally, *refs):
    shrink_ref = refs[0]
    others, owns = refs[1 : 1 + sources], refs[1 + sources : 1 + 2 * sources]
    out_ref, inv_ref, ones_ref = refs[1 + 2 * sources :]
    levels, size = out_ref.shape[0], out_ref.shape[1]
    width = others[0].shape[1] // own_count
    _, train = fold_lanes(own_count, width)
    ones_ref[...] = jnp.ones((8, LANES), F32)
    diagonal = lax.broadcasted_iota(jnp.int32, (LANES, size), 1) - lax.broadcasted_iota(jnp.int32, (LANES, size), 0)
    for r0 in range(0, size, LANES):
        rows = slice(r0, r0 + LANES)
        acc = training_product((others, owns), (others, owns), train, width, rows) / learning_tally
        for r in range(levels):
            out_ref[r, rows, :] = acc + jnp.where(diagonal == r0, shrink_ref[r], 0.0)

    def follow(j, r):
        c0, c1 = j * LANES, (j + 1) * LANES
        inverse = inv_ref[r]
        spans = [(lo, hi) for lo, hi in ((0, c0), (c1, size)) if hi > lo]
        solved = [dot_f32(inverse, out_ref[r, c0:c1, lo:hi]) for lo, hi in spans]
        for lo, hi in spans:
            column = out_ref[r, lo:hi, c0:c1]
            for (left, right), value in zip(spans, solved):
                out_ref[r, lo:hi, left:right] = out_ref[r, lo:hi, left:right] - dot_f32(column, value)
            out_ref[r, lo:hi, c0:c1] = -dot_f32(column, inverse)
        for (left, right), value in zip(spans, solved):
            out_ref[r, c0:c1, left:right] = value
        out_ref[r, c0:c1, c0:c1] = inverse

    stages(size // LANES, levels, out_ref, inv_ref, ones_ref, follow)


def tail_kernel(sources, own_count, learning_tally, trait_rows, *refs):
    shrink_ref, lead_ref = refs[0:2]
    first = (refs[2 : 2 + sources], refs[2 + sources : 2 + 2 * sources])
    last = (refs[2 + 2 * sources : 2 + 3 * sources], refs[2 + 3 * sources : 2 + 4 * sources])
    message_ref, wide_ref, solved_ref, mat_ref, inv_ref, ones_ref = refs[2 + 4 * sources :]
    levels, lead = lead_ref.shape[0], lead_ref.shape[1]
    size, total = mat_ref.shape[1], mat_ref.shape[2]
    width = first[0][0].shape[1] // own_count
    height = size + trait_rows
    held, train = fold_lanes(own_count, width)
    ones_ref[...] = jnp.ones((8, LANES), F32)
    for r0 in range(0, lead, LANES):
        rows = slice(r0, r0 + LANES)
        wide_ref[rows, 0:height] = training_product(first, last, train, width, rows) / learning_tally
        wide_ref[rows, height:total] = jnp.zeros((LANES, total - height), F32)
    for r in range(levels):
        solved_ref[r] = dot_f32(lead_ref[r], wide_ref[...])
    diagonal = lax.broadcasted_iota(jnp.int32, (LANES, height), 1) - lax.broadcasted_iota(
        jnp.int32, (LANES, height), 0
    )
    for r0 in range(0, size, LANES):
        rows = slice(r0, r0 + LANES)
        side = training_product(last, first, train, width, rows) / learning_tally
        acc = training_product(last, last, train, width, rows) / learning_tally
        for r in range(levels):
            mat_ref[r, rows, 0:height] = acc + jnp.where(diagonal == r0, shrink_ref[r], 0.0)
            mat_ref[r, rows, height:total] = jnp.zeros((LANES, total - height), F32)
            mat_ref[r, rows, :] = mat_ref[r, rows, :] - dot_f32(side, solved_ref[r])

    def follow(j, r):
        c0, c1 = j * LANES, (j + 1) * LANES
        solved = dot_f32(inv_ref[r], mat_ref[r, c0:c1, c1:total])
        for lo, hi in ((0, c0), (c1, size)):
            if hi > lo:
                mat_ref[r, lo:hi, c1:total] = mat_ref[r, lo:hi, c1:total] - dot_f32(mat_ref[r, lo:hi, c0:c1], solved)
        mat_ref[r, c0:c1, c1:total] = solved

    stages(size // LANES, levels, mat_ref, inv_ref, ones_ref, follow)
    for r in range(levels):
        low = mat_ref[r, :, size:total]
        top = solved_ref[r, :, size:total] - dot_f32(solved_ref[r, :, 0:size], low)
        top = jnp.transpose(top)[0:trait_rows, :].astype(BF16)
        low = jnp.transpose(low)[0:trait_rows, :].astype(BF16)
        for s in range(sources):
            value = jnp.dot(top, first[1][s][:, pl.ds(held, width)], preferred_element_type=F32) + jnp.dot(
                low, last[1][s][0:size, pl.ds(held, width)], preferred_element_type=F32
            )
            message_ref[r * trait_rows : (r + 1) * trait_rows, s * width : (s + 1) * width] = value.astype(BF16)
    for s in range(sources):
        message_ref[levels * trait_rows : (levels + 1) * trait_rows, s * width : (s + 1) * width] = last[1][s][
            size : size + trait_rows, pl.ds(held, width)
        ]


def level_kernel(own_count, trait_rows, held_rows, *refs):
    pred_ref, gram_ref, cross_ref = refs[-3:]
    n_blocks = (len(refs) - 3) // own_count
    messages = [refs[f * n_blocks : (f + 1) * n_blocks] for f in range(own_count)]
    traits, levels, width = pred_ref.shape[2:]
    me = lax.axis_index("samples")
    block = lax.axis_index("blocks")
    pick = lax.rem(me, own_count)
    lane = lax.broadcasted_iota(jnp.int32, (trait_rows, LANES), 1)
    for f in range(own_count):
        slot = lax.rem(pick + f, own_count)
        mine = messages[f][0]
        held = pl.multiple_of((me ^ (me - pick + slot)) * width, width)
        own = [
            mine[r * trait_rows : (r + 1) * trait_rows, pl.ds(held, width)].astype(F32)[0:traits]
            for r in range(levels)
        ]
        pred_ref[slot, 0] = jnp.stack(own, axis=1).astype(BF16)
        wide = [
            [messages[f][e][s * trait_rows : (s + 1) * trait_rows, :].astype(F32) for s in range(levels)]
            for e in range(n_blocks)
        ]
        trait = mine[levels * trait_rows : (levels + 1) * trait_rows, :].astype(F32)
        for r in range(levels):
            out = jnp.where(lane == n_blocks * levels, jnp.sum(wide[0][r] * trait, axis=1, keepdims=True), 0.0)
            for e in range(n_blocks):
                column = lax.rem(block - e + n_blocks, n_blocks) * levels
                for s in range(levels):
                    total = jnp.sum(wide[0][r] * wide[e][s], axis=1, keepdims=True)
                    out = out + jnp.where(lane == column + s, total, 0.0)
            rows = jnp.transpose(out) / held_rows
            for c in range(n_blocks):
                gram_ref[slot, 0, r, c] = rows[c * levels : (c + 1) * levels, 0:traits]
            cross_ref[slot, 0, r : r + 1, :] = rows[n_blocks * levels : n_blocks * levels + 1, 0:traits]


def land(value, copies):
    if copies * value.size * value.dtype.itemsize > VMEM_SHARE:
        return value
    return pltpu.with_memory_space_constraint(value, pltpu.VMEM)


def per_device(allele_dosage_table, phenotype_values, individual_partition_label, shrink_strengths):
    cores = lax.axis_size("folds")
    sources = lax.axis_size("samples")
    n_blocks = lax.axis_size("blocks")
    own_count = FOLDS // cores
    levels = shrink_strengths.shape[0]
    variants, samples = allele_dosage_table.shape
    traits = phenotype_values.shape[0]
    width = samples // FOLDS
    held_rows = sources * width
    learning_tally = sources * samples - held_rows
    pad_rows = round_up(variants, LANES)
    lead = pad_rows // LANES // 2 * LANES
    size = pad_rows - lead
    trait_rows = round_up(traits, 32)
    half = own_count * width
    vmem = pl.BlockSpec(memory_space=pltpu.VMEM)
    smem = pl.BlockSpec(memory_space=pltpu.SMEM)

    other_lead, own_lead, other_tail, own_tail = pl.pallas_call(
        functools.partial(sort_kernel, own_count, pad_rows),
        out_shape=[jax.ShapeDtypeStruct((lead, half), BF16)] * 2
        + [jax.ShapeDtypeStruct((size + trait_rows, half), BF16)] * 2,
        in_specs=[vmem] * 3,
        out_specs=[vmem] * 4,
        name="sort_samples",
    )(allele_dosage_table, phenotype_values, individual_partition_label.reshape(1, samples))

    def fetch(other):
        return [other] + [
            land(lax.ppermute(other, "samples", [(i, i ^ d) for i in range(sources)]), 2 * sources) for d in range(1, sources)
        ]

    def swap(own, others):
        return [own] + [land(lax.ppermute(x, "folds", [(i, cores - 1 - i) for i in range(cores)]), 2 * sources) for x in others[1:]]

    others_lead = fetch(other_lead)
    owns_lead = swap(own_lead, others_lead)
    other_tail, *others_lead[1:] = lax.optimization_barrier((other_tail, *others_lead[1:]))
    others_tail = fetch(other_tail)
    lead_inverse = pl.pallas_call(
        functools.partial(lead_kernel, sources, own_count, learning_tally),
        out_shape=jax.ShapeDtypeStruct((levels, lead, lead), F32),
        in_specs=[smem] + [vmem] * (2 * sources),
        out_specs=vmem,
        scratch_shapes=[pltpu.VMEM((levels, LANES, LANES), F32), pltpu.VMEM((8, LANES), F32)],
        name="invert_lead",
    )(shrink_strengths, *others_lead, *owns_lead)
    lead_inverse, *others_tail[1:] = lax.optimization_barrier((lead_inverse, *others_tail[1:]))
    owns_tail = swap(own_tail, others_tail)
    message = pl.pallas_call(
        functools.partial(tail_kernel, sources, own_count, learning_tally, trait_rows),
        out_shape=jax.ShapeDtypeStruct(((levels + 1) * trait_rows, sources * width), BF16),
        in_specs=[smem] + [vmem] * (1 + 4 * sources),
        out_specs=vmem,
        scratch_shapes=[
            pltpu.VMEM((lead, size + LANES), F32),
            pltpu.VMEM((levels, lead, size + LANES), F32),
            pltpu.VMEM((levels, size, size + LANES), F32),
            pltpu.VMEM((levels, LANES, LANES), F32),
            pltpu.VMEM((8, LANES), F32),
        ],
        name="solve_tail",
    )(shrink_strengths, lead_inverse, *others_lead, *owns_lead, *others_tail, *owns_tail)

    messages = []
    for f in range(own_count):
        for e in range(n_blocks):
            if f == 0 and e == 0:
                messages.append(message)
                continue
            pairs = []
            for s in range(sources):
                source = s - s % own_count + (s % own_count + f) % own_count
                for b in range(n_blocks):
                    pairs.append((source * n_blocks + (b - e) % n_blocks, s * n_blocks + b))
            messages.append(land(lax.ppermute(message, ("samples", "blocks"), pairs), own_count * n_blocks))

    preds, gram, cross = pl.pallas_call(
        functools.partial(level_kernel, own_count, trait_rows, held_rows),
        out_shape=[
            jax.ShapeDtypeStruct((own_count, 1, traits, levels, width), BF16),
            jax.ShapeDtypeStruct((own_count, 1, levels, n_blocks, levels, traits), F32),
            jax.ShapeDtypeStruct((own_count, 1, levels, traits), F32),
        ],
        in_specs=[vmem] * len(messages),
        out_specs=[vmem] * 3,
        name="level_one",
    )(*messages)
    return jnp.swapaxes(preds, 2, 3), jnp.moveaxis(gram, 5, 3), cross


def solution(mesh):
    in_specs = (
        P("blocks", ("groups", "samples")),
        P(None, ("groups", "samples")),
        P(("groups", "samples")),
        P(),
    )
    out_specs = (
        P("folds", "blocks", None, None, ("groups", "samples")),
        P(("groups", "folds"), "blocks", None, None, None, None),
        P(("groups", "folds"), "blocks", None, None),
    )
    return jax.shard_map(
        per_device, mesh=mesh, in_specs=in_specs, out_specs=out_specs, check_vma=False
    )
```

```python
import functools

import jax
import jax.numpy as jnp
from jax import lax
from jax.experimental import pallas as pl
from jax.experimental.pallas import tpu as pltpu
from jax.sharding import PartitionSpec as P

SHRINK_LEVELS = 2
FOLDS = 4
LANES = 128
PANEL = 32
PIVOTS = 8
HIGHEST = lax.Precision.HIGHEST
VMEM_SHARE = 2 << 20
F32 = jnp.float32
BF16 = jnp.bfloat16


def round_up(value, step):
    return (value + step - 1) // step * step


def dot_nt(left, right):
    return lax.dot_general(left, right, (((1,), (1,)), ((), ())), preferred_element_type=F32)


def spread(value):
    return jnp.broadcast_to(value, (8, LANES))


def sort_kernel(own_count, pad_rows, geno_ref, trait_ref, label_ref, *refs):
    variants, traits = geno_ref.shape[0], trait_ref.shape[0]
    rows = label_ref.shape[1]
    core = lax.axis_index("folds")
    cores = lax.axis_size("folds")
    slot = lax.rem(label_ref[...] + own_count * (cores - 1 - core), FOLDS)
    width = rows // FOLDS
    before = lax.broadcasted_iota(jnp.int32, (rows, rows), 0) < lax.broadcasted_iota(jnp.int32, (rows, rows), 1)
    fold_row = lax.broadcasted_iota(jnp.int32, (16, rows), 0)
    hit = jnp.broadcast_to(slot, (16, rows)) == fold_row
    rank = jnp.dot(
        jnp.where(hit, 1.0, 0.0).astype(BF16),
        jnp.where(before, 1.0, 0.0).astype(BF16),
        preferred_element_type=F32,
    )
    place = jnp.sum(jnp.where(hit, rank + (fold_row * width).astype(F32), 0.0), axis=0, keepdims=True)
    place = place.astype(jnp.int32)
    target = lax.broadcasted_iota(jnp.int32, (rows, rows), 0)
    move = jnp.where(target == jnp.broadcast_to(place, (rows, rows)), 1.0, 0.0).astype(BF16)
    sorted_geno = dot_nt(geno_ref[...], move).astype(BF16)
    sorted_trait = dot_nt(trait_ref[...], move).astype(BF16)
    split = refs[0].shape[0]
    half = refs[0].shape[1]
    height = refs[2].shape[0]
    low = (variants - split) // 16 * 16
    for part in range(2):
        lanes = slice(part * half, (part + 1) * half)
        refs[part][...] = sorted_geno[0:split, lanes]
        ref = refs[2 + part]
        ref[low:height, :] = jnp.zeros((height - low, half), BF16)
        ref[0 : variants - split, :] = sorted_geno[split:variants, lanes]
        ref[pad_rows - split : pad_rows - split + traits, :] = sorted_trait[:, lanes]


def eliminate_panel(panels, first, ones):
    lane = lax.broadcasted_iota(jnp.int32, (8, LANES), 1)
    sub = lax.broadcasted_iota(jnp.int32, (8, LANES), 0)
    systems = range(len(panels))
    count = len(panels[0])
    panels = [list(panel) for panel in panels]
    for b in range(count):
        base_col = first + 8 * b
        in_pivot = (lane >= base_col) & (lane < base_col + 8)
        rest = [(b + 1 + i) % count for i in range(count - 1)]
        cols = [[None] * 8 for _ in systems]
        factors = [{i: [None] * 8 for i in rest} for _ in systems]
        for u in range(8):
            for q in systems:
                cols[q][u] = spread(panels[q][b][:, base_col + u : base_col + u + 1]) * ones
        for u in range(8):
            for q in systems:
                for i in rest:
                    factors[q][i][u] = spread(panels[q][i][:, base_col + u : base_col + u + 1])
        for t in range(0, 8, 2):
            first_lane, second_lane = lane == base_col + t, lane == base_col + t + 1
            first_row, second_row = sub == t, sub == t + 1
            for q in systems:
                left, right, panel = cols[q][t], cols[q][t + 1], panels[q][b]
                corner = spread(left[t : t + 1, :])
                upper = spread(right[t : t + 1, :])
                lower = spread(left[t + 1 : t + 2, :])
                other = spread(right[t + 1 : t + 2, :])
                inverse = 1.0 / corner
                second = corner * (1.0 / (corner * other - upper * lower))
                ratio = lower * inverse
                factor = jnp.where(first_row, -1.0, left) * inverse
                after = jnp.where(first_row, 0.0, right) - factor * upper
                after = jnp.where(second_row, -1.0, after) * second
                factor = jnp.where(second_row, 0.0, factor)
                pair = first_row | second_row
                for u in range(t + 2, 8):
                    col = cols[q][u]
                    row = spread(col[t : t + 1, :])
                    next_row = spread(col[t + 1 : t + 2, :]) - ratio * row
                    cols[q][u] = jnp.where(pair, 0.0, col) - factor * row - after * next_row
                row = jnp.where(first_lane, 1.0, jnp.where(second_lane, 0.0, spread(panel[t : t + 1, :])))
                next_row = jnp.where(first_lane, 0.0, spread(panel[t + 1 : t + 2, :])) - ratio * row
                next_row = jnp.where(second_lane, 1.0, next_row)
                keep = jnp.where(pair | first_lane | second_lane, 0.0, panel)
                panels[q][b] = keep - factor * row - after * next_row
        for q in systems:
            rows = [spread(panels[q][b][t : t + 1, :]) for t in range(8)]
            for i in rest:
                parts = [factors[q][i][t] * rows[t] for t in range(8)]
                while len(parts) > 1:
                    parts = [parts[k] + parts[k + 1] for k in range(0, len(parts), 2)]
                panels[q][i] = jnp.where(in_pivot, 0.0, panels[q][i]) - parts[0]
    return panels


def invert_blocks(blocks, ones):
    lane = lax.broadcasted_iota(jnp.int32, (LANES, LANES), 1)
    row = lax.broadcasted_iota(jnp.int32, (LANES, LANES), 0)
    blocks = list(blocks)
    for b in range(LANES // PANEL):
        r0 = PANEL * b
        panels = eliminate_panel(
            [[block[r0 + 8 * i : r0 + 8 * i + 8, :] for i in range(PANEL // 8)] for block in blocks], r0, ones
        )
        for q, block in enumerate(blocks):
            pieces = list(panels[q])
            if r0:
                pieces.insert(0, jnp.zeros((r0, LANES), F32))
            if LANES - PANEL - r0:
                pieces.append(jnp.zeros((LANES - PANEL - r0, LANES), F32))
            wide = jnp.concatenate(pieces, axis=0)
            keep = jnp.where((lane >= r0) & (lane < r0 + PANEL), 0.0, block)
            update = keep - jnp.dot(block, wide, precision=HIGHEST, preferred_element_type=F32)
            blocks[q] = jnp.where((row >= r0) & (row < r0 + PANEL), wide, update)
    return blocks


def dot_f32(left, right):
    return jnp.dot(left, right, precision=HIGHEST, preferred_element_type=F32)


def fold_lanes(own_count, width):
    pick = lax.rem(lax.axis_index("samples"), own_count)
    held = pl.multiple_of(pick * width, width)
    train = [pl.multiple_of((pick ^ f) * width, width) for f in range(1, own_count)]
    return held, train


def training_product(left, right, train, width, rows):
    lefts, rights = [], []
    for left_other, left_own, right_other, right_own in zip(*left, *right):
        lefts.append(left_other[rows, :])
        rights.append(right_other[...])
        for start in train:
            lefts.append(left_own[rows, pl.ds(start, width)])
            rights.append(right_own[:, pl.ds(start, width)])
    return dot_nt(jnp.concatenate(lefts, axis=1), jnp.concatenate(rights, axis=1))


def stages(count, levels, mat_ref, inv_ref, ones_ref, follow):
    def stage(j, carry):
        start = pl.multiple_of(j * LANES, LANES)
        inverses = invert_blocks(
            [mat_ref[r, pl.ds(start, LANES), pl.ds(start, LANES)] for r in range(levels)], ones_ref[...]
        )
        for r in range(levels):
            inv_ref[r] = inverses[r]
        for jj in range(count):

            @pl.when(j == jj)
            def _():
                for r in range(levels):
                    follow(jj, r)

        return carry

    lax.fori_loop(0, count, stage, 0)


def lead_kernel(sources, own_count, learning_tally, *refs):
    shrink_ref = refs[0]
    others, owns = refs[1 : 1 + sources], refs[1 + sources : 1 + 2 * sources]
    out_ref, inv_ref, ones_ref = refs[1 + 2 * sources :]
    levels, size = out_ref.shape[0], out_ref.shape[1]
    width = others[0].shape[1] // own_count
    _, train = fold_lanes(own_count, width)
    ones_ref[...] = jnp.ones((8, LANES), F32)
    diagonal = lax.broadcasted_iota(jnp.int32, (LANES, size), 1) - lax.broadcasted_iota(jnp.int32, (LANES, size), 0)
    for r0 in range(0, size, LANES):
        rows = slice(r0, r0 + LANES)
        acc = training_product((others, owns), (others, owns), train, width, rows) / learning_tally
        for r in range(levels):
            out_ref[r, rows, :] = acc + jnp.where(diagonal == r0, shrink_ref[r], 0.0)

    def follow(j, r):
        c0, c1 = j * LANES, (j + 1) * LANES
        inverse = inv_ref[r]
        spans = [(lo, hi) for lo, hi in ((0, c0), (c1, size)) if hi > lo]
        solved = [dot_f32(inverse, out_ref[r, c0:c1, lo:hi]) for lo, hi in spans]
        for lo, hi in spans:
            column = out_ref[r, lo:hi, c0:c1]
            for (left, right), value in zip(spans, solved):
                out_ref[r, lo:hi, left:right] = out_ref[r, lo:hi, left:right] - dot_f32(column, value)
            out_ref[r, lo:hi, c0:c1] = -dot_f32(column, inverse)
        for (left, right), value in zip(spans, solved):
            out_ref[r, c0:c1, left:right] = value
        out_ref[r, c0:c1, c0:c1] = inverse

    stages(size // LANES, levels, out_ref, inv_ref, ones_ref, follow)


def tail_kernel(sources, own_count, learning_tally, traits, trait_rows, *refs):
    shrink_ref, lead_ref = refs[0:2]
    first = (refs[2 : 2 + sources], refs[2 + sources : 2 + 2 * sources])
    last = (refs[2 + 2 * sources : 2 + 3 * sources], refs[2 + 3 * sources : 2 + 4 * sources])
    message_ref, trait_ref, wide_ref, solved_ref, mat_ref, inv_ref, ones_ref, beta_ref = refs[2 + 4 * sources :]
    levels, lead = lead_ref.shape[0], lead_ref.shape[1]
    size, total = mat_ref.shape[1], mat_ref.shape[2]
    width = first[0][0].shape[1] // own_count
    height = size + trait_rows
    held, train = fold_lanes(own_count, width)
    ones_ref[...] = jnp.ones((8, LANES), F32)
    for r0 in range(0, lead, LANES):
        rows = slice(r0, r0 + LANES)
        wide_ref[rows, 0:height] = training_product(first, last, train, width, rows) / learning_tally
        wide_ref[rows, height:total] = jnp.zeros((LANES, total - height), F32)
    for r in range(levels):
        solved_ref[r] = dot_f32(lead_ref[r], wide_ref[...])
    diagonal = lax.broadcasted_iota(jnp.int32, (LANES, height), 1) - lax.broadcasted_iota(
        jnp.int32, (LANES, height), 0
    )
    for r0 in range(0, size, LANES):
        rows = slice(r0, r0 + LANES)
        side = training_product(last, first, train, width, rows) / learning_tally
        acc = training_product(last, last, train, width, rows) / learning_tally
        for r in range(levels):
            mat_ref[r, rows, 0:height] = acc + jnp.where(diagonal == r0, shrink_ref[r], 0.0)
            mat_ref[r, rows, height:total] = jnp.zeros((LANES, total - height), F32)
            mat_ref[r, rows, :] = mat_ref[r, rows, :] - dot_f32(side, solved_ref[r])

    def follow(j, r):
        c0, c1 = j * LANES, (j + 1) * LANES
        solved = dot_f32(inv_ref[r], mat_ref[r, c0:c1, c1:total])
        for lo, hi in ((0, c0), (c1, size)):
            if hi > lo:
                mat_ref[r, lo:hi, c1:total] = mat_ref[r, lo:hi, c1:total] - dot_f32(mat_ref[r, lo:hi, c0:c1], solved)
        mat_ref[r, c0:c1, c1:total] = solved

    stages(size // LANES, levels, mat_ref, inv_ref, ones_ref, follow)
    beta_ref[...] = jnp.zeros(beta_ref.shape, F32)
    for r in range(levels):
        low = mat_ref[r, :, size:total]
        top = solved_ref[r, :, size:total] - dot_f32(solved_ref[r, :, 0:size], low)
        beta_ref[r * traits : (r + 1) * traits, 0:lead] = jnp.transpose(top)[0:traits, :]
        beta_ref[r * traits : (r + 1) * traits, lead : lead + size] = jnp.transpose(low)[0:traits, :]
    betas = beta_ref[...].astype(BF16)
    for s in range(sources):
        lanes = slice(s * width, (s + 1) * width)
        held_geno = jnp.concatenate(
            [first[1][s][:, pl.ds(held, width)], last[1][s][0:size, pl.ds(held, width)]], axis=0
        )
        message_ref[:, lanes] = jnp.dot(betas, held_geno, preferred_element_type=F32).astype(BF16)
        for f, start in enumerate([held] + train):
            trait_ref[f, :, lanes] = last[1][s ^ f][size : size + trait_rows, pl.ds(start, width)]


def level_kernel(own_count, trait_rows, held_rows, trait_ref, *refs):
    pred_ref, gram_ref, cross_ref, wide_ref = refs[-4:]
    n_blocks = (len(refs) - 4) // own_count
    traits, levels, width = pred_ref.shape[2:]
    rows = round_up(traits, 8)
    me = lax.axis_index("samples")
    block = lax.axis_index("blocks")
    pick = lax.rem(me, own_count)
    lane = lax.broadcasted_iota(jnp.int32, (rows, LANES), 1)
    for f in range(own_count):
        slot = pick ^ f
        for e in range(n_blocks):
            wide_ref[e] = refs[f * n_blocks + e][...].astype(F32)
        pred_ref[slot, 0] = jnp.stack(
            [wide_ref[0, r * traits : (r + 1) * traits, f * width : (f + 1) * width] for r in range(levels)], axis=1
        ).astype(BF16)
        wide = [[wide_ref[e, s * traits : s * traits + rows, :] for s in range(levels)] for e in range(n_blocks)]
        trait = trait_ref[f].astype(F32)[0:rows]
        for r in range(levels):
            out = jnp.where(lane == n_blocks * levels, jnp.sum(wide[0][r] * trait, axis=1, keepdims=True), 0.0)
            for e in range(n_blocks):
                column = lax.rem(block - e + n_blocks, n_blocks) * levels
                for s in range(levels):
                    total = jnp.sum(wide[0][r] * wide[e][s], axis=1, keepdims=True)
                    out = out + jnp.where(lane == column + s, total, 0.0)
            turned = jnp.transpose(out) / held_rows
            for c in range(n_blocks):
                gram_ref[slot, 0, r, c] = turned[c * levels : (c + 1) * levels, 0:traits]
            cross_ref[slot, 0, r : r + 1, :] = turned[n_blocks * levels : n_blocks * levels + 1, 0:traits]


def land(value, copies):
    if copies * value.size * value.dtype.itemsize > VMEM_SHARE:
        return value
    return pltpu.with_memory_space_constraint(value, pltpu.VMEM)


def per_device(allele_dosage_table, phenotype_values, individual_partition_label, shrink_strengths):
    cores = lax.axis_size("folds")
    sources = lax.axis_size("samples")
    n_blocks = lax.axis_size("blocks")
    own_count = FOLDS // cores
    levels = shrink_strengths.shape[0]
    variants, samples = allele_dosage_table.shape
    traits = phenotype_values.shape[0]
    width = samples // FOLDS
    held_rows = sources * width
    learning_tally = sources * samples - held_rows
    pad_rows = round_up(variants, LANES)
    lead = pad_rows // LANES // 2 * LANES
    size = pad_rows - lead
    trait_rows = round_up(traits, 32)
    half = own_count * width
    vmem = pl.BlockSpec(memory_space=pltpu.VMEM)
    smem = pl.BlockSpec(memory_space=pltpu.SMEM)

    other_lead, own_lead, other_tail, own_tail = pl.pallas_call(
        functools.partial(sort_kernel, own_count, pad_rows),
        out_shape=[jax.ShapeDtypeStruct((lead, half), BF16)] * 2
        + [jax.ShapeDtypeStruct((size + trait_rows, half), BF16)] * 2,
        in_specs=[vmem] * 3,
        out_specs=[vmem] * 4,
        name="sort_samples",
    )(allele_dosage_table, phenotype_values, individual_partition_label.reshape(1, samples))

    def fetch(other):
        return [other] + [
            land(lax.ppermute(other, "samples", [(i, i ^ d) for i in range(sources)]), 2 * sources) for d in range(1, sources)
        ]

    def swap(own, others):
        return [own] + [land(lax.ppermute(x, "folds", [(i, cores - 1 - i) for i in range(cores)]), 2 * sources) for x in others[1:]]

    others_lead = fetch(other_lead)
    owns_lead = swap(own_lead, others_lead)
    other_tail, *others_lead[1:] = lax.optimization_barrier((other_tail, *others_lead[1:]))
    others_tail = fetch(other_tail)
    lead_inverse = pl.pallas_call(
        functools.partial(lead_kernel, sources, own_count, learning_tally),
        out_shape=jax.ShapeDtypeStruct((levels, lead, lead), F32),
        in_specs=[smem] + [vmem] * (2 * sources),
        out_specs=vmem,
        scratch_shapes=[pltpu.VMEM((levels, LANES, LANES), F32), pltpu.VMEM((8, LANES), F32)],
        name="invert_lead",
    )(shrink_strengths, *others_lead, *owns_lead)
    lead_inverse, *others_tail[1:] = lax.optimization_barrier((lead_inverse, *others_tail[1:]))
    owns_tail = swap(own_tail, others_tail)
    message_rows = round_up((levels - 1) * traits + round_up(traits, 8), 16)
    message, trait_rows_held = pl.pallas_call(
        functools.partial(tail_kernel, sources, own_count, learning_tally, traits, trait_rows),
        out_shape=[
            jax.ShapeDtypeStruct((message_rows, sources * width), BF16),
            jax.ShapeDtypeStruct((own_count, trait_rows, sources * width), BF16),
        ],
        in_specs=[smem] + [vmem] * (1 + 4 * sources),
        out_specs=[vmem] * 2,
        scratch_shapes=[
            pltpu.VMEM((lead, size + LANES), F32),
            pltpu.VMEM((levels, lead, size + LANES), F32),
            pltpu.VMEM((levels, size, size + LANES), F32),
            pltpu.VMEM((levels, LANES, LANES), F32),
            pltpu.VMEM((8, LANES), F32),
            pltpu.VMEM((message_rows, pad_rows), F32),
        ],
        name="solve_tail",
    )(shrink_strengths, lead_inverse, *others_lead, *owns_lead, *others_tail, *owns_tail)

    messages = []
    for f in range(own_count):
        for e in range(n_blocks):
            if f == 0 and e == 0:
                messages.append(message)
                continue
            pairs = []
            for s in range(sources):
                for b in range(n_blocks):
                    pairs.append(((s ^ f) * n_blocks + (b - e) % n_blocks, s * n_blocks + b))
            messages.append(land(lax.ppermute(message, ("samples", "blocks"), pairs), own_count * n_blocks))

    preds, gram, cross = pl.pallas_call(
        functools.partial(level_kernel, own_count, trait_rows, held_rows),
        out_shape=[
            jax.ShapeDtypeStruct((own_count, 1, traits, levels, width), BF16),
            jax.ShapeDtypeStruct((own_count, 1, levels, n_blocks, levels, traits), F32),
            jax.ShapeDtypeStruct((own_count, 1, levels, traits), F32),
        ],
        in_specs=[vmem] * (1 + len(messages)),
        out_specs=[vmem] * 3,
        scratch_shapes=[pltpu.VMEM((n_blocks, message_rows, sources * width), F32)],
        name="level_one",
    )(trait_rows_held, *messages)
    return jnp.swapaxes(preds, 2, 3), jnp.moveaxis(gram, 5, 3), cross


def solution(mesh):
    in_specs = (
        P("blocks", ("groups", "samples")),
        P(None, ("groups", "samples")),
        P(("groups", "samples")),
        P(),
    )
    out_specs = (
        P("folds", "blocks", None, None, ("groups", "samples")),
        P(("groups", "folds"), "blocks", None, None, None, None),
        P(("groups", "folds"), "blocks", None, None),
    )
    return jax.shard_map(
        per_device, mesh=mesh, in_specs=in_specs, out_specs=out_specs, check_vma=False
    )
```

```python
import functools

import jax
import jax.numpy as jnp
from jax import lax
from jax.experimental import pallas as pl
from jax.experimental.pallas import tpu as pltpu
from jax.sharding import PartitionSpec as P

SHRINK_LEVELS = 2
FOLDS = 4
LANES = 128
PANEL = 32
PIVOTS = 8
HIGHEST = lax.Precision.HIGHEST
VMEM_SHARE = 2 << 20
F32 = jnp.float32
BF16 = jnp.bfloat16


def round_up(value, step):
    return (value + step - 1) // step * step


def dot_nt(left, right):
    return lax.dot_general(left, right, (((1,), (1,)), ((), ())), preferred_element_type=F32)


def spread(value):
    return jnp.broadcast_to(value, (8, LANES))


def sort_kernel(own_count, offset, variants, geno_ref, trait_ref, label_ref, other_ref, own_ref):
    rows = label_ref.shape[1]
    core = lax.axis_index("folds")
    cores = lax.axis_size("folds")
    slot = lax.rem(label_ref[...] + own_count * (cores - 1 - core), FOLDS)
    width = rows // FOLDS
    before = lax.broadcasted_iota(jnp.int32, (rows, rows), 0) < lax.broadcasted_iota(jnp.int32, (rows, rows), 1)
    fold_row = lax.broadcasted_iota(jnp.int32, (16, rows), 0)
    hit = jnp.broadcast_to(slot, (16, rows)) == fold_row
    rank = jnp.dot(
        jnp.where(hit, 1.0, 0.0).astype(BF16),
        jnp.where(before, 1.0, 0.0).astype(BF16),
        preferred_element_type=F32,
    )
    place = jnp.sum(jnp.where(hit, rank + (fold_row * width).astype(F32), 0.0), axis=0, keepdims=True)
    place = place.astype(jnp.int32)
    target = lax.broadcasted_iota(jnp.int32, (rows, rows), 0)
    move = jnp.where(target == jnp.broadcast_to(place, (rows, rows)), 1.0, 0.0).astype(BF16)
    sorted_geno = dot_nt(geno_ref[offset : offset + variants, :], move).astype(BF16)
    height, half = other_ref.shape
    size = height if trait_ref is None else height - round_up(trait_ref.shape[0], 32)
    for part, ref in enumerate((other_ref, own_ref)):
        lanes = slice(part * half, (part + 1) * half)
        low = variants // 16 * 16
        if low < height:
            ref[low:height, :] = jnp.zeros((height - low, half), BF16)
        ref[0:variants, :] = sorted_geno[:, lanes]
        if trait_ref is not None:
            ref[size : size + trait_ref.shape[0], :] = dot_nt(trait_ref[...], move)[:, lanes].astype(BF16)


def eliminate_panel(panels, first, ones):
    lane = lax.broadcasted_iota(jnp.int32, (8, LANES), 1)
    sub = lax.broadcasted_iota(jnp.int32, (8, LANES), 0)
    systems = range(len(panels))
    count = len(panels[0])
    panels = [list(panel) for panel in panels]
    for b in range(count):
        base_col = first + 8 * b
        in_pivot = (lane >= base_col) & (lane < base_col + 8)
        rest = [(b + 1 + i) % count for i in range(count - 1)]
        cols = [[None] * 8 for _ in systems]
        factors = [{i: [None] * 8 for i in rest} for _ in systems]
        for u in range(8):
            for q in systems:
                cols[q][u] = spread(panels[q][b][:, base_col + u : base_col + u + 1]) * ones
        for u in range(8):
            for q in systems:
                for i in rest:
                    factors[q][i][u] = spread(panels[q][i][:, base_col + u : base_col + u + 1])
        for t in range(0, 8, 2):
            first_lane, second_lane = lane == base_col + t, lane == base_col + t + 1
            first_row, second_row = sub == t, sub == t + 1
            for q in systems:
                left, right, panel = cols[q][t], cols[q][t + 1], panels[q][b]
                corner = spread(left[t : t + 1, :])
                upper = spread(right[t : t + 1, :])
                lower = spread(left[t + 1 : t + 2, :])
                other = spread(right[t + 1 : t + 2, :])
                inverse = 1.0 / corner
                second = corner * (1.0 / (corner * other - upper * lower))
                ratio = lower * inverse
                factor = jnp.where(first_row, -1.0, left) * inverse
                after = jnp.where(first_row, 0.0, right) - factor * upper
                after = jnp.where(second_row, -1.0, after) * second
                factor = jnp.where(second_row, 0.0, factor)
                pair = first_row | second_row
                for u in range(t + 2, 8):
                    col = cols[q][u]
                    row = spread(col[t : t + 1, :])
                    next_row = spread(col[t + 1 : t + 2, :]) - ratio * row
                    cols[q][u] = jnp.where(pair, 0.0, col) - factor * row - after * next_row
                row = jnp.where(first_lane, 1.0, jnp.where(second_lane, 0.0, spread(panel[t : t + 1, :])))
                next_row = jnp.where(first_lane, 0.0, spread(panel[t + 1 : t + 2, :])) - ratio * row
                next_row = jnp.where(second_lane, 1.0, next_row)
                keep = jnp.where(pair | first_lane | second_lane, 0.0, panel)
                panels[q][b] = keep - factor * row - after * next_row
        for q in systems:
            rows = [spread(panels[q][b][t : t + 1, :]) for t in range(8)]
            for i in rest:
                parts = [factors[q][i][t] * rows[t] for t in range(8)]
                while len(parts) > 1:
                    parts = [parts[k] + parts[k + 1] for k in range(0, len(parts), 2)]
                panels[q][i] = jnp.where(in_pivot, 0.0, panels[q][i]) - parts[0]
    return panels


def invert_blocks(blocks, ones):
    lane = lax.broadcasted_iota(jnp.int32, (LANES, LANES), 1)
    row = lax.broadcasted_iota(jnp.int32, (LANES, LANES), 0)
    blocks = list(blocks)
    for b in range(LANES // PANEL):
        r0 = PANEL * b
        panels = eliminate_panel(
            [[block[r0 + 8 * i : r0 + 8 * i + 8, :] for i in range(PANEL // 8)] for block in blocks], r0, ones
        )
        for q, block in enumerate(blocks):
            pieces = list(panels[q])
            if r0:
                pieces.insert(0, jnp.zeros((r0, LANES), F32))
            if LANES - PANEL - r0:
                pieces.append(jnp.zeros((LANES - PANEL - r0, LANES), F32))
            wide = jnp.concatenate(pieces, axis=0)
            keep = jnp.where((lane >= r0) & (lane < r0 + PANEL), 0.0, block)
            update = keep - jnp.dot(block, wide, precision=HIGHEST, preferred_element_type=F32)
            blocks[q] = jnp.where((row >= r0) & (row < r0 + PANEL), wide, update)
    return blocks


def dot_f32(left, right):
    return jnp.dot(left, right, precision=HIGHEST, preferred_element_type=F32)


def fold_lanes(own_count, width):
    pick = lax.rem(lax.axis_index("samples"), own_count)
    held = pl.multiple_of(pick * width, width)
    train = [pl.multiple_of((pick ^ f) * width, width) for f in range(1, own_count)]
    return held, train


def training_product(left, right, train, width, rows):
    lefts, rights = [], []
    for left_other, left_own, right_other, right_own in zip(*left, *right):
        lefts.append(left_other[rows, :])
        rights.append(right_other[...])
        for start in train:
            lefts.append(left_own[rows, pl.ds(start, width)])
            rights.append(right_own[:, pl.ds(start, width)])
    return dot_nt(jnp.concatenate(lefts, axis=1), jnp.concatenate(rights, axis=1))


def stages(count, levels, mat_ref, inv_ref, ones_ref, follow):
    def stage(j, carry):
        start = pl.multiple_of(j * LANES, LANES)
        inverses = invert_blocks(
            [mat_ref[r, pl.ds(start, LANES), pl.ds(start, LANES)] for r in range(levels)], ones_ref[...]
        )
        for r in range(levels):
            inv_ref[r] = inverses[r]
        for jj in range(count):

            @pl.when(j == jj)
            def _():
                for r in range(levels):
                    follow(jj, r)

        return carry

    lax.fori_loop(0, count, stage, 0)


def lead_kernel(sources, own_count, learning_tally, *refs):
    shrink_ref = refs[0]
    others, owns = refs[1 : 1 + sources], refs[1 + sources : 1 + 2 * sources]
    out_ref, inv_ref, ones_ref = refs[1 + 2 * sources :]
    levels, size = out_ref.shape[0], out_ref.shape[1]
    width = others[0].shape[1] // own_count
    _, train = fold_lanes(own_count, width)
    ones_ref[...] = jnp.ones((8, LANES), F32)
    diagonal = lax.broadcasted_iota(jnp.int32, (LANES, size), 1) - lax.broadcasted_iota(jnp.int32, (LANES, size), 0)
    for r0 in range(0, size, LANES):
        rows = slice(r0, r0 + LANES)
        acc = training_product((others, owns), (others, owns), train, width, rows) / learning_tally
        for r in range(levels):
            out_ref[r, rows, :] = acc + jnp.where(diagonal == r0, shrink_ref[r], 0.0)

    def follow(j, r):
        c0, c1 = j * LANES, (j + 1) * LANES
        inverse = inv_ref[r]
        spans = [(lo, hi) for lo, hi in ((0, c0), (c1, size)) if hi > lo]
        solved = [dot_f32(inverse, out_ref[r, c0:c1, lo:hi]) for lo, hi in spans]
        for lo, hi in spans:
            column = out_ref[r, lo:hi, c0:c1]
            for (left, right), value in zip(spans, solved):
                out_ref[r, lo:hi, left:right] = out_ref[r, lo:hi, left:right] - dot_f32(column, value)
            out_ref[r, lo:hi, c0:c1] = -dot_f32(column, inverse)
        for (left, right), value in zip(spans, solved):
            out_ref[r, c0:c1, left:right] = value
        out_ref[r, c0:c1, c0:c1] = inverse

    stages(size // LANES, levels, out_ref, inv_ref, ones_ref, follow)


def tail_kernel(sources, own_count, learning_tally, traits, trait_rows, *refs):
    shrink_ref, lead_ref = refs[0:2]
    first = (refs[2 : 2 + sources], refs[2 + sources : 2 + 2 * sources])
    last = (refs[2 + 2 * sources : 2 + 3 * sources], refs[2 + 3 * sources : 2 + 4 * sources])
    message_ref, trait_ref, wide_ref, solved_ref, mat_ref, inv_ref, ones_ref, beta_ref = refs[2 + 4 * sources :]
    levels, lead = lead_ref.shape[0], lead_ref.shape[1]
    size, total = mat_ref.shape[1], mat_ref.shape[2]
    width = first[0][0].shape[1] // own_count
    height = size + trait_rows
    held, train = fold_lanes(own_count, width)
    ones_ref[...] = jnp.ones((8, LANES), F32)
    for r0 in range(0, lead, LANES):
        rows = slice(r0, r0 + LANES)
        wide_ref[rows, 0:height] = training_product(first, last, train, width, rows) / learning_tally
        wide_ref[rows, height:total] = jnp.zeros((LANES, total - height), F32)
    for r in range(levels):
        solved_ref[:, r * total : (r + 1) * total] = dot_f32(lead_ref[r], wide_ref[...])
    diagonal = lax.broadcasted_iota(jnp.int32, (LANES, height), 1) - lax.broadcasted_iota(
        jnp.int32, (LANES, height), 0
    )
    for r0 in range(0, size, LANES):
        rows = slice(r0, r0 + LANES)
        side = training_product(last, first, train, width, rows) / learning_tally
        acc = training_product(last, last, train, width, rows) / learning_tally
        known = dot_f32(side, solved_ref[...])
        for r in range(levels):
            mat_ref[r, rows, 0:height] = (
                acc + jnp.where(diagonal == r0, shrink_ref[r], 0.0) - known[:, r * total : r * total + height]
            )
            mat_ref[r, rows, height:total] = jnp.zeros((LANES, total - height), F32)

    def follow(j, r):
        c0, c1 = j * LANES, (j + 1) * LANES
        solved = dot_f32(inv_ref[r], mat_ref[r, c0:c1, c1:total])
        for lo, hi in ((0, c0), (c1, size)):
            if hi > lo:
                mat_ref[r, lo:hi, c1:total] = mat_ref[r, lo:hi, c1:total] - dot_f32(mat_ref[r, lo:hi, c0:c1], solved)
        mat_ref[r, c0:c1, c1:total] = solved

    stages(size // LANES, levels, mat_ref, inv_ref, ones_ref, follow)
    beta_ref[...] = jnp.zeros(beta_ref.shape, F32)
    for r in range(levels):
        low = mat_ref[r, :, size:total]
        top = solved_ref[:, r * total + size : (r + 1) * total] - dot_f32(
            solved_ref[:, r * total : r * total + size], low
        )
        beta_ref[r * traits : (r + 1) * traits, 0:lead] = jnp.transpose(top)[0:traits, :]
        beta_ref[r * traits : (r + 1) * traits, lead : lead + size] = jnp.transpose(low)[0:traits, :]
    betas = beta_ref[...].astype(BF16)
    for s in range(sources):
        lanes = slice(s * width, (s + 1) * width)
        held_geno = jnp.concatenate(
            [first[1][s][:, pl.ds(held, width)], last[1][s][0:size, pl.ds(held, width)]], axis=0
        )
        message_ref[:, lanes] = jnp.dot(betas, held_geno, preferred_element_type=F32).astype(BF16)
        for f, start in enumerate([held] + train):
            trait_ref[f, :, lanes] = last[1][s ^ f][size : size + trait_rows, pl.ds(start, width)]


def level_kernel(own_count, trait_rows, held_rows, trait_ref, *refs):
    pred_ref, gram_ref, cross_ref, wide_ref = refs[-4:]
    n_blocks = (len(refs) - 4) // own_count
    traits, levels, width = pred_ref.shape[2:]
    rows = round_up(traits, 8)
    me = lax.axis_index("samples")
    block = lax.axis_index("blocks")
    pick = lax.rem(me, own_count)
    lane = lax.broadcasted_iota(jnp.int32, (rows, LANES), 1)
    for f in range(own_count):
        slot = pick ^ f
        for e in range(n_blocks):
            wide_ref[e] = refs[f * n_blocks + e][...].astype(F32)
        pred_ref[slot, 0] = jnp.stack(
            [wide_ref[0, r * traits : (r + 1) * traits, f * width : (f + 1) * width] for r in range(levels)], axis=1
        ).astype(BF16)
        wide = [[wide_ref[e, s * traits : s * traits + rows, :] for s in range(levels)] for e in range(n_blocks)]
        trait = trait_ref[f].astype(F32)[0:rows]
        for r in range(levels):
            out = jnp.where(lane == n_blocks * levels, jnp.sum(wide[0][r] * trait, axis=1, keepdims=True), 0.0)
            for e in range(n_blocks):
                column = lax.rem(block - e + n_blocks, n_blocks) * levels
                for s in range(levels):
                    total = jnp.sum(wide[0][r] * wide[e][s], axis=1, keepdims=True)
                    out = out + jnp.where(lane == column + s, total, 0.0)
            turned = jnp.transpose(out) / held_rows
            for c in range(n_blocks):
                gram_ref[slot, 0, r, c] = turned[c * levels : (c + 1) * levels, 0:traits]
            cross_ref[slot, 0, r : r + 1, :] = turned[n_blocks * levels : n_blocks * levels + 1, 0:traits]


def land(value, copies):
    if copies * value.size * value.dtype.itemsize > VMEM_SHARE:
        return value
    return pltpu.with_memory_space_constraint(value, pltpu.VMEM)


def per_device(allele_dosage_table, phenotype_values, individual_partition_label, shrink_strengths):
    cores = lax.axis_size("folds")
    sources = lax.axis_size("samples")
    n_blocks = lax.axis_size("blocks")
    own_count = FOLDS // cores
    levels = shrink_strengths.shape[0]
    variants, samples = allele_dosage_table.shape
    traits = phenotype_values.shape[0]
    width = samples // FOLDS
    held_rows = sources * width
    learning_tally = sources * samples - held_rows
    pad_rows = round_up(variants, LANES)
    lead = pad_rows // LANES // 2 * LANES
    size = pad_rows - lead
    trait_rows = round_up(traits, 32)
    half = own_count * width
    vmem = pl.BlockSpec(memory_space=pltpu.VMEM)
    smem = pl.BlockSpec(memory_space=pltpu.SMEM)

    def sort(offset, height, with_traits):
        count = min(variants - offset, height)
        inputs = [allele_dosage_table, phenotype_values, individual_partition_label.reshape(1, samples)]
        block = lead if lead == size else variants
        specs = [
            pl.BlockSpec((block, samples), lambda i: (offset // block, 0)),
            pl.BlockSpec((traits, samples), lambda i: (0, 0)),
            pl.BlockSpec((1, samples), lambda i: (0, 0)),
        ]
        kernel = functools.partial(sort_kernel, own_count, offset % block, count)
        if not with_traits:
            del inputs[1], specs[1]

            def kernel(geno_ref, label_ref, *outs):
                sort_kernel(own_count, offset % block, count, geno_ref, None, label_ref, *outs)

        return pl.pallas_call(
            kernel,
            grid=(1,),
            out_shape=[jax.ShapeDtypeStruct((height, half), BF16)] * 2,
            in_specs=specs,
            out_specs=[pl.BlockSpec((height, half), lambda i: (0, 0))] * 2,
            name="sort_samples",
        )(*inputs)

    other_lead, own_lead = sort(0, lead, False)
    other_tail, own_tail = sort(lead, size + trait_rows, True)

    def fetch(other):
        return [other] + [
            land(lax.ppermute(other, "samples", [(i, i ^ d) for i in range(sources)]), 2 * sources) for d in range(1, sources)
        ]

    def swap(own, others):
        return [own] + [land(lax.ppermute(x, "folds", [(i, cores - 1 - i) for i in range(cores)]), 2 * sources) for x in others[1:]]

    others_lead = fetch(other_lead)
    owns_lead = swap(own_lead, others_lead)
    other_tail, *others_lead[1:] = lax.optimization_barrier((other_tail, *others_lead[1:]))
    others_tail = fetch(other_tail)
    lead_inverse = pl.pallas_call(
        functools.partial(lead_kernel, sources, own_count, learning_tally),
        out_shape=jax.ShapeDtypeStruct((levels, lead, lead), F32),
        in_specs=[smem] + [vmem] * (2 * sources),
        out_specs=vmem,
        scratch_shapes=[pltpu.VMEM((levels, LANES, LANES), F32), pltpu.VMEM((8, LANES), F32)],
        name="invert_lead",
    )(shrink_strengths, *others_lead, *owns_lead)
    lead_inverse, *others_tail[1:] = lax.optimization_barrier((lead_inverse, *others_tail[1:]))
    owns_tail = swap(own_tail, others_tail)
    message_rows = round_up((levels - 1) * traits + round_up(traits, 8), 16)
    message, trait_rows_held = pl.pallas_call(
        functools.partial(tail_kernel, sources, own_count, learning_tally, traits, trait_rows),
        out_shape=[
            jax.ShapeDtypeStruct((message_rows, sources * width), BF16),
            jax.ShapeDtypeStruct((own_count, trait_rows, sources * width), BF16),
        ],
        in_specs=[smem] + [vmem] * (1 + 4 * sources),
        out_specs=[vmem] * 2,
        scratch_shapes=[
            pltpu.VMEM((lead, size + LANES), F32),
            pltpu.VMEM((lead, levels * (size + LANES)), F32),
            pltpu.VMEM((levels, size, size + LANES), F32),
            pltpu.VMEM((levels, LANES, LANES), F32),
            pltpu.VMEM((8, LANES), F32),
            pltpu.VMEM((message_rows, pad_rows), F32),
        ],
        name="solve_tail",
    )(shrink_strengths, lead_inverse, *others_lead, *owns_lead, *others_tail, *owns_tail)

    messages = []
    for f in range(own_count):
        for e in range(n_blocks):
            if f == 0 and e == 0:
                messages.append(message)
                continue
            pairs = []
            for s in range(sources):
                for b in range(n_blocks):
                    pairs.append(((s ^ f) * n_blocks + (b - e) % n_blocks, s * n_blocks + b))
            messages.append(land(lax.ppermute(message, ("samples", "blocks"), pairs), own_count * n_blocks))

    preds, gram, cross = pl.pallas_call(
        functools.partial(level_kernel, own_count, trait_rows, held_rows),
        out_shape=[
            jax.ShapeDtypeStruct((own_count, 1, traits, levels, width), BF16),
            jax.ShapeDtypeStruct((own_count, 1, levels, n_blocks, levels, traits), F32),
            jax.ShapeDtypeStruct((own_count, 1, levels, traits), F32),
        ],
        in_specs=[vmem] * (1 + len(messages)),
        out_specs=[vmem] * 3,
        scratch_shapes=[pltpu.VMEM((n_blocks, message_rows, sources * width), F32)],
        name="level_one",
    )(trait_rows_held, *messages)
    return jnp.swapaxes(preds, 2, 3), jnp.moveaxis(gram, 5, 3), cross


def solution(mesh):
    in_specs = (
        P("blocks", ("groups", "samples")),
        P(None, ("groups", "samples")),
        P(("groups", "samples")),
        P(),
    )
    out_specs = (
        P("folds", "blocks", None, None, ("groups", "samples")),
        P(("groups", "folds"), "blocks", None, None, None, None),
        P(("groups", "folds"), "blocks", None, None),
    )
    return jax.shard_map(
        per_device, mesh=mesh, in_specs=in_specs, out_specs=out_specs, check_vma=False
    )
```

```python
import functools

import jax
import jax.numpy as jnp
from jax import lax
from jax.experimental import pallas as pl
from jax.experimental.pallas import tpu as pltpu
from jax.sharding import PartitionSpec as P

SHRINK_LEVELS = 2
FOLDS = 4
LANES = 128
PANEL = 32
PIVOTS = 8
HIGHEST = lax.Precision.HIGHEST
VMEM_SHARE = 2 << 20
F32 = jnp.float32
BF16 = jnp.bfloat16


def round_up(value, step):
    return (value + step - 1) // step * step


def dot_nt(left, right):
    return lax.dot_general(left, right, (((1,), (1,)), ((), ())), preferred_element_type=F32)


def spread(value):
    return jnp.broadcast_to(value, (8, LANES))


def sort_kernel(own_count, offset, variants, geno_ref, trait_ref, label_ref, other_ref, own_ref):
    rows = label_ref.shape[1]
    core = lax.axis_index("folds")
    cores = lax.axis_size("folds")
    slot = lax.rem(label_ref[...] + own_count * (cores - 1 - core), FOLDS)
    width = rows // FOLDS
    before = lax.broadcasted_iota(jnp.int32, (rows, rows), 0) < lax.broadcasted_iota(jnp.int32, (rows, rows), 1)
    fold_row = lax.broadcasted_iota(jnp.int32, (16, rows), 0)
    hit = jnp.broadcast_to(slot, (16, rows)) == fold_row
    rank = jnp.dot(
        jnp.where(hit, 1.0, 0.0).astype(BF16),
        jnp.where(before, 1.0, 0.0).astype(BF16),
        preferred_element_type=F32,
    )
    place = jnp.sum(jnp.where(hit, rank + (fold_row * width).astype(F32), 0.0), axis=0, keepdims=True)
    place = place.astype(jnp.int32)
    target = lax.broadcasted_iota(jnp.int32, (rows, rows), 0)
    move = jnp.where(target == jnp.broadcast_to(place, (rows, rows)), 1.0, 0.0).astype(BF16)
    sorted_geno = dot_nt(geno_ref[offset : offset + variants, :], move).astype(BF16)
    height, half = other_ref.shape
    size = height if trait_ref is None else height - round_up(trait_ref.shape[0], 32)
    for part, ref in enumerate((other_ref, own_ref)):
        lanes = slice(part * half, (part + 1) * half)
        low = variants // 16 * 16
        if low < height:
            ref[low:height, :] = jnp.zeros((height - low, half), BF16)
        ref[0:variants, :] = sorted_geno[:, lanes]
        if trait_ref is not None:
            ref[size : size + trait_ref.shape[0], :] = dot_nt(trait_ref[...], move)[:, lanes].astype(BF16)


def eliminate_panel(panels, first, ones):
    lane = lax.broadcasted_iota(jnp.int32, (8, LANES), 1)
    sub = lax.broadcasted_iota(jnp.int32, (8, LANES), 0)
    systems = range(len(panels))
    count = len(panels[0])
    panels = [list(panel) for panel in panels]
    for b in range(count):
        base_col = first + 8 * b
        in_pivot = (lane >= base_col) & (lane < base_col + 8)
        rest = [(b + 1 + i) % count for i in range(count - 1)]
        cols = [[None] * 8 for _ in systems]
        factors = [{i: [None] * 8 for i in rest} for _ in systems]
        for u in range(8):
            for q in systems:
                cols[q][u] = spread(panels[q][b][:, base_col + u : base_col + u + 1]) * ones
        for u in range(8):
            for q in systems:
                for i in rest:
                    factors[q][i][u] = spread(panels[q][i][:, base_col + u : base_col + u + 1])
        for t in range(0, 8, 2):
            first_lane, second_lane = lane == base_col + t, lane == base_col + t + 1
            first_row, second_row = sub == t, sub == t + 1
            for q in systems:
                left, right, panel = cols[q][t], cols[q][t + 1], panels[q][b]
                corner = spread(left[t : t + 1, :])
                upper = spread(right[t : t + 1, :])
                lower = spread(left[t + 1 : t + 2, :])
                other = spread(right[t + 1 : t + 2, :])
                inverse = 1.0 / corner
                second = corner * (1.0 / (corner * other - upper * lower))
                ratio = lower * inverse
                factor = jnp.where(first_row, -1.0, left) * inverse
                after = jnp.where(first_row, 0.0, right) - factor * upper
                after = jnp.where(second_row, -1.0, after) * second
                factor = jnp.where(second_row, 0.0, factor)
                pair = first_row | second_row
                for u in range(t + 2, 8):
                    col = cols[q][u]
                    row = spread(col[t : t + 1, :])
                    next_row = spread(col[t + 1 : t + 2, :]) - ratio * row
                    cols[q][u] = jnp.where(pair, 0.0, col) - factor * row - after * next_row
                row = jnp.where(first_lane, 1.0, jnp.where(second_lane, 0.0, spread(panel[t : t + 1, :])))
                next_row = jnp.where(first_lane, 0.0, spread(panel[t + 1 : t + 2, :])) - ratio * row
                next_row = jnp.where(second_lane, 1.0, next_row)
                keep = jnp.where(pair | first_lane | second_lane, 0.0, panel)
                panels[q][b] = keep - factor * row - after * next_row
        for q in systems:
            rows = [spread(panels[q][b][t : t + 1, :]) for t in range(8)]
            for i in rest:
                parts = [factors[q][i][t] * rows[t] for t in range(8)]
                while len(parts) > 1:
                    parts = [parts[k] + parts[k + 1] for k in range(0, len(parts), 2)]
                panels[q][i] = jnp.where(in_pivot, 0.0, panels[q][i]) - parts[0]
    return panels


def invert_blocks(blocks, ones):
    lane = lax.broadcasted_iota(jnp.int32, (LANES, LANES), 1)
    row = lax.broadcasted_iota(jnp.int32, (LANES, LANES), 0)
    blocks = list(blocks)
    for b in range(LANES // PANEL):
        r0 = PANEL * b
        panels = eliminate_panel(
            [[block[r0 + 8 * i : r0 + 8 * i + 8, :] for i in range(PANEL // 8)] for block in blocks], r0, ones
        )
        for q, block in enumerate(blocks):
            pieces = list(panels[q])
            if r0:
                pieces.insert(0, jnp.zeros((r0, LANES), F32))
            if LANES - PANEL - r0:
                pieces.append(jnp.zeros((LANES - PANEL - r0, LANES), F32))
            wide = jnp.concatenate(pieces, axis=0)
            keep = jnp.where((lane >= r0) & (lane < r0 + PANEL), 0.0, block)
            update = keep - jnp.dot(block, wide, precision=HIGHEST, preferred_element_type=F32)
            blocks[q] = jnp.where((row >= r0) & (row < r0 + PANEL), wide, update)
    return blocks


def dot_f32(left, right):
    return jnp.dot(left, right, precision=HIGHEST, preferred_element_type=F32)


def fold_lanes(own_count, width):
    pick = lax.rem(lax.axis_index("samples"), own_count)
    held = pl.multiple_of(pick * width, width)
    train = [pl.multiple_of((pick ^ f) * width, width) for f in range(1, own_count)]
    return held, train


def training_product(left, right, train, width, rows):
    lefts, rights = [], []
    for left_other, left_own, right_other, right_own in zip(*left, *right):
        lefts.append(left_other[rows, :])
        rights.append(right_other[...])
        for start in train:
            lefts.append(left_own[rows, pl.ds(start, width)])
            rights.append(right_own[:, pl.ds(start, width)])
    return dot_nt(jnp.concatenate(lefts, axis=1), jnp.concatenate(rights, axis=1))


def stages(count, levels, mat_ref, inv_ref, ones_ref, follow):
    def stage(j, carry):
        start = pl.multiple_of(j * LANES, LANES)
        inverses = invert_blocks(
            [mat_ref[r, pl.ds(start, LANES), pl.ds(start, LANES)] for r in range(levels)], ones_ref[...]
        )
        for r in range(levels):
            inv_ref[r] = inverses[r]
        for jj in range(count):

            @pl.when(j == jj)
            def _():
                for r in range(levels):
                    follow(jj, r)

        return carry

    lax.fori_loop(0, count, stage, 0)


def lead_kernel(sources, own_count, learning_tally, *refs):
    shrink_ref = refs[0]
    others, owns = refs[1 : 1 + sources], refs[1 + sources : 1 + 2 * sources]
    out_ref, inv_ref, ones_ref = refs[1 + 2 * sources :]
    levels, size = out_ref.shape[0], out_ref.shape[1]
    width = others[0].shape[1] // own_count
    _, train = fold_lanes(own_count, width)
    ones_ref[...] = jnp.ones((8, LANES), F32)
    diagonal = lax.broadcasted_iota(jnp.int32, (LANES, size), 1) - lax.broadcasted_iota(jnp.int32, (LANES, size), 0)
    for r0 in range(0, size, LANES):
        rows = slice(r0, r0 + LANES)
        acc = training_product((others, owns), (others, owns), train, width, rows) / learning_tally
        for r in range(levels):
            out_ref[r, rows, :] = acc + jnp.where(diagonal == r0, shrink_ref[r], 0.0)

    def follow(j, r):
        c0, c1 = j * LANES, (j + 1) * LANES
        inverse = inv_ref[r]
        spans = [(lo, hi) for lo, hi in ((0, c0), (c1, size)) if hi > lo]
        solved = [dot_f32(inverse, out_ref[r, c0:c1, lo:hi]) for lo, hi in spans]
        for lo, hi in spans:
            column = out_ref[r, lo:hi, c0:c1]
            for (left, right), value in zip(spans, solved):
                out_ref[r, lo:hi, left:right] = out_ref[r, lo:hi, left:right] - dot_f32(column, value)
            out_ref[r, lo:hi, c0:c1] = -dot_f32(column, inverse)
        for (left, right), value in zip(spans, solved):
            out_ref[r, c0:c1, left:right] = value
        out_ref[r, c0:c1, c0:c1] = inverse

    stages(size // LANES, levels, out_ref, inv_ref, ones_ref, follow)


def tail_kernel(sources, own_count, learning_tally, traits, trait_rows, *refs):
    shrink_ref, lead_ref = refs[0:2]
    first = (refs[2 : 2 + sources], refs[2 + sources : 2 + 2 * sources])
    last = (refs[2 + 2 * sources : 2 + 3 * sources], refs[2 + 3 * sources : 2 + 4 * sources])
    message_ref, trait_ref, wide_ref, solved_ref, mat_ref, inv_ref, ones_ref, beta_ref = refs[2 + 4 * sources :]
    levels, lead = lead_ref.shape[0], lead_ref.shape[1]
    size, total = mat_ref.shape[1], mat_ref.shape[2]
    width = first[0][0].shape[1] // own_count
    height = size + trait_rows
    held, train = fold_lanes(own_count, width)
    ones_ref[...] = jnp.ones((8, LANES), F32)
    for r0 in range(0, lead, LANES):
        rows = slice(r0, r0 + LANES)
        wide_ref[rows, 0:height] = training_product(first, last, train, width, rows) / learning_tally
        wide_ref[rows, height:total] = jnp.zeros((LANES, total - height), F32)
    for r in range(levels):
        solved_ref[:, r * total : (r + 1) * total] = dot_f32(lead_ref[r], wide_ref[...])
    diagonal = lax.broadcasted_iota(jnp.int32, (LANES, height), 1) - lax.broadcasted_iota(
        jnp.int32, (LANES, height), 0
    )
    for r0 in range(0, size, LANES):
        rows = slice(r0, r0 + LANES)
        side = training_product(last, first, train, width, rows) / learning_tally
        acc = training_product(last, last, train, width, rows) / learning_tally
        known = dot_f32(side, solved_ref[...])
        for r in range(levels):
            mat_ref[r, rows, 0:height] = (
                acc + jnp.where(diagonal == r0, shrink_ref[r], 0.0) - known[:, r * total : r * total + height]
            )
            mat_ref[r, rows, height:total] = jnp.zeros((LANES, total - height), F32)

    def follow(j, r):
        c0, c1 = j * LANES, (j + 1) * LANES
        solved = dot_f32(inv_ref[r], mat_ref[r, c0:c1, c1:total])
        for lo, hi in ((0, c0), (c1, size)):
            if hi > lo:
                mat_ref[r, lo:hi, c1:total] = mat_ref[r, lo:hi, c1:total] - dot_f32(mat_ref[r, lo:hi, c0:c1], solved)
        mat_ref[r, c0:c1, c1:total] = solved

    stages(size // LANES, levels, mat_ref, inv_ref, ones_ref, follow)
    beta_ref[...] = jnp.zeros(beta_ref.shape, F32)
    for r in range(levels):
        low = mat_ref[r, :, size:total]
        top = solved_ref[:, r * total + size : (r + 1) * total] - dot_f32(
            solved_ref[:, r * total : r * total + size], low
        )
        beta_ref[r * traits : (r + 1) * traits, 0:lead] = jnp.transpose(top)[0:traits, :]
        beta_ref[r * traits : (r + 1) * traits, lead : lead + size] = jnp.transpose(low)[0:traits, :]
    betas = beta_ref[...].astype(BF16)
    for s in range(sources):
        lanes = slice(s * width, (s + 1) * width)
        held_geno = jnp.concatenate(
            [first[1][s][:, pl.ds(held, width)], last[1][s][0:size, pl.ds(held, width)]], axis=0
        )
        message_ref[:, lanes] = jnp.dot(betas, held_geno, preferred_element_type=F32).astype(BF16)
        for f, start in enumerate([held] + train):
            trait_ref[f, :, lanes] = last[1][s ^ f][size : size + trait_rows, pl.ds(start, width)]


def level_kernel(own_count, trait_rows, held_rows, trait_ref, *refs):
    pred_ref, gram_ref, cross_ref, wide_ref = refs[-4:]
    n_blocks = (len(refs) - 4) // own_count
    traits, levels, width = pred_ref.shape[2:]
    rows = round_up(traits, 8)
    me = lax.axis_index("samples")
    block = lax.axis_index("blocks")
    pick = lax.rem(me, own_count)
    lane = lax.broadcasted_iota(jnp.int32, (rows, LANES), 1)
    for f in range(own_count):
        slot = pick ^ f
        for e in range(n_blocks):
            wide_ref[e] = refs[f * n_blocks + e][...].astype(F32)
        pred_ref[slot, 0] = jnp.stack(
            [wide_ref[0, r * traits : (r + 1) * traits, f * width : (f + 1) * width] for r in range(levels)], axis=1
        ).astype(BF16)
        wide = [[wide_ref[e, s * traits : s * traits + rows, :] for s in range(levels)] for e in range(n_blocks)]
        trait = trait_ref[f].astype(F32)[0:rows]
        for r in range(levels):
            out = jnp.where(lane == n_blocks * levels, jnp.sum(wide[0][r] * trait, axis=1, keepdims=True), 0.0)
            for e in range(n_blocks):
                column = lax.rem(block - e + n_blocks, n_blocks) * levels
                for s in range(levels):
                    total = jnp.sum(wide[0][r] * wide[e][s], axis=1, keepdims=True)
                    out = out + jnp.where(lane == column + s, total, 0.0)
            turned = jnp.transpose(out) / held_rows
            for c in range(n_blocks):
                gram_ref[slot, 0, r, c] = turned[c * levels : (c + 1) * levels, 0:traits]
            cross_ref[slot, 0, r : r + 1, :] = turned[n_blocks * levels : n_blocks * levels + 1, 0:traits]


def land(value, copies):
    if copies * value.size * value.dtype.itemsize > VMEM_SHARE:
        return value
    return pltpu.with_memory_space_constraint(value, pltpu.VMEM)


def kept(shape, dtype, copies):
    struct = jax.ShapeDtypeStruct(shape, dtype)
    if copies * struct.size * struct.dtype.itemsize > VMEM_SHARE:
        return struct
    return pltpu.VMEM(shape, dtype)


def per_device(allele_dosage_table, phenotype_values, individual_partition_label, shrink_strengths):
    cores = lax.axis_size("folds")
    sources = lax.axis_size("samples")
    n_blocks = lax.axis_size("blocks")
    own_count = FOLDS // cores
    levels = shrink_strengths.shape[0]
    variants, samples = allele_dosage_table.shape
    traits = phenotype_values.shape[0]
    width = samples // FOLDS
    held_rows = sources * width
    learning_tally = sources * samples - held_rows
    pad_rows = round_up(variants, LANES)
    lead = pad_rows // LANES // 2 * LANES
    size = pad_rows - lead
    trait_rows = round_up(traits, 32)
    half = own_count * width
    vmem = pl.BlockSpec(memory_space=pltpu.VMEM)
    smem = pl.BlockSpec(memory_space=pltpu.SMEM)

    def sort(offset, height, with_traits):
        count = min(variants - offset, height)
        inputs = [allele_dosage_table, phenotype_values, individual_partition_label.reshape(1, samples)]
        block = lead if lead == size else variants
        specs = [
            pl.BlockSpec((block, samples), lambda i: (offset // block, 0)),
            pl.BlockSpec((traits, samples), lambda i: (0, 0)),
            pl.BlockSpec((1, samples), lambda i: (0, 0)),
        ]
        kernel = functools.partial(sort_kernel, own_count, offset % block, count)
        if not with_traits:
            del inputs[1], specs[1]

            def kernel(geno_ref, label_ref, *outs):
                sort_kernel(own_count, offset % block, count, geno_ref, None, label_ref, *outs)

        return pl.pallas_call(
            kernel,
            grid=(1,),
            out_shape=[kept((height, half), BF16, 2 * sources)] * 2,
            in_specs=specs,
            out_specs=[pl.BlockSpec((height, half), lambda i: (0, 0))] * 2,
            name="sort_samples",
        )(*inputs)

    other_lead, own_lead = sort(0, lead, False)
    other_tail, own_tail = sort(lead, size + trait_rows, True)

    def fetch(other):
        return [land(other, 2 * sources)] + [
            land(lax.ppermute(other, "samples", [(i, i ^ d) for i in range(sources)]), 2 * sources) for d in range(1, sources)
        ]

    def swap(own, others):
        return [land(own, 2 * sources)] + [land(lax.ppermute(x, "folds", [(i, cores - 1 - i) for i in range(cores)]), 2 * sources) for x in others[1:]]

    others_lead = fetch(other_lead)
    owns_lead = swap(own_lead, others_lead)
    other_tail, *others_lead[1:] = lax.optimization_barrier((other_tail, *others_lead[1:]))
    others_tail = fetch(other_tail)
    lead_inverse = pl.pallas_call(
        functools.partial(lead_kernel, sources, own_count, learning_tally),
        out_shape=kept((levels, lead, lead), F32, sources // 2),
        in_specs=[smem] + [vmem] * (2 * sources),
        out_specs=vmem,
        scratch_shapes=[pltpu.VMEM((levels, LANES, LANES), F32), pltpu.VMEM((8, LANES), F32)],
        name="invert_lead",
    )(shrink_strengths, *others_lead, *owns_lead)
    lead_inverse, *others_tail[1:] = lax.optimization_barrier((lead_inverse, *others_tail[1:]))
    lead_inverse = land(lead_inverse, sources // 2)
    owns_tail = swap(own_tail, others_tail)
    message_rows = round_up((levels - 1) * traits + round_up(traits, 8), 16)
    message, trait_rows_held = pl.pallas_call(
        functools.partial(tail_kernel, sources, own_count, learning_tally, traits, trait_rows),
        out_shape=[
            kept((message_rows, sources * width), BF16, sources),
            kept((own_count, trait_rows, sources * width), BF16, sources),
        ],
        in_specs=[smem] + [vmem] * (1 + 4 * sources),
        out_specs=[vmem] * 2,
        scratch_shapes=[
            pltpu.VMEM((lead, size + LANES), F32),
            pltpu.VMEM((lead, levels * (size + LANES)), F32),
            pltpu.VMEM((levels, size, size + LANES), F32),
            pltpu.VMEM((levels, LANES, LANES), F32),
            pltpu.VMEM((8, LANES), F32),
            pltpu.VMEM((message_rows, pad_rows), F32),
        ],
        name="solve_tail",
    )(shrink_strengths, lead_inverse, *others_lead, *owns_lead, *others_tail, *owns_tail)

    messages = []
    for f in range(own_count):
        for e in range(n_blocks):
            if f == 0 and e == 0:
                messages.append(land(message, own_count * n_blocks))
                continue
            pairs = []
            for s in range(sources):
                for b in range(n_blocks):
                    pairs.append(((s ^ f) * n_blocks + (b - e) % n_blocks, s * n_blocks + b))
            messages.append(land(lax.ppermute(message, ("samples", "blocks"), pairs), own_count * n_blocks))

    preds, gram, cross = pl.pallas_call(
        functools.partial(level_kernel, own_count, trait_rows, held_rows),
        out_shape=[
            jax.ShapeDtypeStruct((own_count, 1, traits, levels, width), BF16),
            jax.ShapeDtypeStruct((own_count, 1, levels, n_blocks, levels, traits), F32),
            jax.ShapeDtypeStruct((own_count, 1, levels, traits), F32),
        ],
        in_specs=[vmem] * (1 + len(messages)),
        out_specs=[vmem] * 3,
        scratch_shapes=[pltpu.VMEM((n_blocks, message_rows, sources * width), F32)],
        name="level_one",
    )(land(trait_rows_held, sources), *messages)
    return jnp.swapaxes(preds, 2, 3), jnp.moveaxis(gram, 5, 3), cross


def solution(mesh):
    in_specs = (
        P("blocks", ("groups", "samples")),
        P(None, ("groups", "samples")),
        P(("groups", "samples")),
        P(),
    )
    out_specs = (
        P("folds", "blocks", None, None, ("groups", "samples")),
        P(("groups", "folds"), "blocks", None, None, None, None),
        P(("groups", "folds"), "blocks", None, None),
    )
    return jax.shard_map(
        per_device, mesh=mesh, in_specs=in_specs, out_specs=out_specs, check_vma=False
    )
```

```python
import functools

import jax
import jax.numpy as jnp
from jax import lax
from jax.experimental import pallas as pl
from jax.experimental.pallas import tpu as pltpu
from jax.sharding import PartitionSpec as P

SHRINK_LEVELS = 2
FOLDS = 4
LANES = 128
PANEL = 32
PIVOTS = 8
HIGHEST = lax.Precision.HIGHEST
VMEM_SHARE = 2 << 20
F32 = jnp.float32
BF16 = jnp.bfloat16


def round_up(value, step):
    return (value + step - 1) // step * step


def dot_nt(left, right):
    return lax.dot_general(left, right, (((1,), (1,)), ((), ())), preferred_element_type=F32)


def spread(value):
    return jnp.broadcast_to(value, (8, LANES))


def sort_kernel(own_count, offset, variants, geno_ref, trait_ref, label_ref, other_ref, own_ref):
    rows = label_ref.shape[1]
    core = lax.axis_index("folds")
    cores = lax.axis_size("folds")
    slot = lax.rem(label_ref[...] + own_count * (cores - 1 - core), FOLDS)
    width = rows // FOLDS
    before = lax.broadcasted_iota(jnp.int32, (rows, rows), 0) < lax.broadcasted_iota(jnp.int32, (rows, rows), 1)
    fold_row = lax.broadcasted_iota(jnp.int32, (16, rows), 0)
    hit = jnp.broadcast_to(slot, (16, rows)) == fold_row
    rank = jnp.dot(
        jnp.where(hit, 1.0, 0.0).astype(BF16),
        jnp.where(before, 1.0, 0.0).astype(BF16),
        preferred_element_type=F32,
    )
    place = jnp.sum(jnp.where(hit, rank + (fold_row * width).astype(F32), 0.0), axis=0, keepdims=True)
    place = place.astype(jnp.int32)
    target = lax.broadcasted_iota(jnp.int32, (rows, rows), 0)
    move = jnp.where(target == jnp.broadcast_to(place, (rows, rows)), 1.0, 0.0).astype(BF16)
    sorted_geno = dot_nt(geno_ref[offset : offset + variants, :], move).astype(BF16)
    height, half = other_ref.shape
    size = height if trait_ref is None else height - round_up(trait_ref.shape[0], 32)
    for part, ref in enumerate((other_ref, own_ref)):
        lanes = slice(part * half, (part + 1) * half)
        low = variants // 16 * 16
        if low < height:
            ref[low:height, :] = jnp.zeros((height - low, half), BF16)
        ref[0:variants, :] = sorted_geno[:, lanes]
        if trait_ref is not None:
            ref[size : size + trait_ref.shape[0], :] = dot_nt(trait_ref[...], move)[:, lanes].astype(BF16)


def eliminate_panel(panels, first, ones):
    lane = lax.broadcasted_iota(jnp.int32, (8, LANES), 1)
    sub = lax.broadcasted_iota(jnp.int32, (8, LANES), 0)
    systems = range(len(panels))
    count = len(panels[0])
    panels = [list(panel) for panel in panels]
    for b in range(count):
        base_col = first + 8 * b
        in_pivot = (lane >= base_col) & (lane < base_col + 8)
        rest = [(b + 1 + i) % count for i in range(count - 1)]
        cols = [[None] * 8 for _ in systems]
        factors = [{i: [None] * 8 for i in rest} for _ in systems]
        for u in range(8):
            for q in systems:
                cols[q][u] = spread(panels[q][b][:, base_col + u : base_col + u + 1]) * ones
        for u in range(8):
            for q in systems:
                for i in rest:
                    factors[q][i][u] = spread(panels[q][i][:, base_col + u : base_col + u + 1])
        for t in range(0, 8, 2):
            first_lane, second_lane = lane == base_col + t, lane == base_col + t + 1
            first_row, second_row = sub == t, sub == t + 1
            for q in systems:
                left, right, panel = cols[q][t], cols[q][t + 1], panels[q][b]
                corner = spread(left[t : t + 1, :])
                upper = spread(right[t : t + 1, :])
                lower = spread(left[t + 1 : t + 2, :])
                other = spread(right[t + 1 : t + 2, :])
                inverse = 1.0 / corner
                second = corner * (1.0 / (corner * other - upper * lower))
                ratio = lower * inverse
                factor = jnp.where(first_row, -1.0, left) * inverse
                after = jnp.where(first_row, 0.0, right) - factor * upper
                after = jnp.where(second_row, -1.0, after) * second
                factor = jnp.where(second_row, 0.0, factor)
                pair = first_row | second_row
                for u in range(t + 2, 8):
                    col = cols[q][u]
                    row = spread(col[t : t + 1, :])
                    next_row = spread(col[t + 1 : t + 2, :]) - ratio * row
                    cols[q][u] = jnp.where(pair, 0.0, col) - factor * row - after * next_row
                row = jnp.where(first_lane, 1.0, jnp.where(second_lane, 0.0, spread(panel[t : t + 1, :])))
                next_row = jnp.where(first_lane, 0.0, spread(panel[t + 1 : t + 2, :])) - ratio * row
                next_row = jnp.where(second_lane, 1.0, next_row)
                keep = jnp.where(pair | first_lane | second_lane, 0.0, panel)
                panels[q][b] = keep - factor * row - after * next_row
        for q in systems:
            rows = [spread(panels[q][b][t : t + 1, :]) for t in range(8)]
            for i in rest:
                parts = [factors[q][i][t] * rows[t] for t in range(8)]
                while len(parts) > 1:
                    parts = [parts[k] + parts[k + 1] for k in range(0, len(parts), 2)]
                panels[q][i] = jnp.where(in_pivot, 0.0, panels[q][i]) - parts[0]
    return panels


def invert_blocks(blocks, ones):
    lane = lax.broadcasted_iota(jnp.int32, (LANES, LANES), 1)
    row = lax.broadcasted_iota(jnp.int32, (LANES, LANES), 0)
    blocks = list(blocks)
    for b in range(LANES // PANEL):
        r0 = PANEL * b
        panels = eliminate_panel(
            [[block[r0 + 8 * i : r0 + 8 * i + 8, :] for i in range(PANEL // 8)] for block in blocks], r0, ones
        )
        for q, block in enumerate(blocks):
            pieces = list(panels[q])
            if r0:
                pieces.insert(0, jnp.zeros((r0, LANES), F32))
            if LANES - PANEL - r0:
                pieces.append(jnp.zeros((LANES - PANEL - r0, LANES), F32))
            wide = jnp.concatenate(pieces, axis=0)
            keep = jnp.where((lane >= r0) & (lane < r0 + PANEL), 0.0, block)
            update = keep - jnp.dot(block, wide, precision=HIGHEST, preferred_element_type=F32)
            blocks[q] = jnp.where((row >= r0) & (row < r0 + PANEL), wide, update)
    return blocks


def dot_f32(left, right):
    return jnp.dot(left, right, precision=HIGHEST, preferred_element_type=F32)


def fold_lanes(own_count, width):
    pick = lax.rem(lax.axis_index("samples"), own_count)
    held = pl.multiple_of(pick * width, width)
    train = [pl.multiple_of((pick ^ f) * width, width) for f in range(1, own_count)]
    return held, train


def training_product(left, right, train, width, rows):
    lefts, rights = [], []
    for left_other, left_own, right_other, right_own in zip(*left, *right):
        lefts.append(left_other[rows, :])
        rights.append(right_other[...])
        for start in train:
            lefts.append(left_own[rows, pl.ds(start, width)])
            rights.append(right_own[:, pl.ds(start, width)])
    return dot_nt(jnp.concatenate(lefts, axis=1), jnp.concatenate(rights, axis=1))


def stages(count, levels, mat_ref, inv_ref, ones_ref, follow):
    def stage(j, carry):
        start = pl.multiple_of(j * LANES, LANES)
        inverses = invert_blocks(
            [mat_ref[r, pl.ds(start, LANES), pl.ds(start, LANES)] for r in range(levels)], ones_ref[...]
        )
        for r in range(levels):
            inv_ref[r] = inverses[r]
        for jj in range(count):

            @pl.when(j == jj)
            def _():
                for r in range(levels):
                    follow(jj, r)

        return carry

    lax.fori_loop(0, count, stage, 0)


def lead_kernel(sources, own_count, learning_tally, *refs):
    shrink_ref = refs[0]
    others, owns = refs[1 : 1 + sources], refs[1 + sources : 1 + 2 * sources]
    out_ref, inv_ref, ones_ref = refs[1 + 2 * sources :]
    levels, size = out_ref.shape[0], out_ref.shape[1]
    width = others[0].shape[1] // own_count
    _, train = fold_lanes(own_count, width)
    ones_ref[...] = jnp.ones((8, LANES), F32)
    diagonal = lax.broadcasted_iota(jnp.int32, (size, size), 1) == lax.broadcasted_iota(jnp.int32, (size, size), 0)
    acc = training_product((others, owns), (others, owns), train, width, slice(0, size)) / learning_tally
    for r in range(levels):
        out_ref[r] = acc + jnp.where(diagonal, shrink_ref[r], 0.0)

    def follow(j, r):
        c0, c1 = j * LANES, (j + 1) * LANES
        inverse = inv_ref[r]
        spans = [(lo, hi) for lo, hi in ((0, c0), (c1, size)) if hi > lo]
        solved = [dot_f32(inverse, out_ref[r, c0:c1, lo:hi]) for lo, hi in spans]
        for lo, hi in spans:
            column = out_ref[r, lo:hi, c0:c1]
            for (left, right), value in zip(spans, solved):
                out_ref[r, lo:hi, left:right] = out_ref[r, lo:hi, left:right] - dot_f32(column, value)
            out_ref[r, lo:hi, c0:c1] = -dot_f32(column, inverse)
        for (left, right), value in zip(spans, solved):
            out_ref[r, c0:c1, left:right] = value
        out_ref[r, c0:c1, c0:c1] = inverse

    stages(size // LANES, levels, out_ref, inv_ref, ones_ref, follow)


def tail_kernel(sources, own_count, learning_tally, traits, trait_rows, *refs):
    shrink_ref, lead_ref = refs[0:2]
    first = (refs[2 : 2 + sources], refs[2 + sources : 2 + 2 * sources])
    last = (refs[2 + 2 * sources : 2 + 3 * sources], refs[2 + 3 * sources : 2 + 4 * sources])
    message_ref, trait_ref, wide_ref, solved_ref, mat_ref, inv_ref, ones_ref, beta_ref = refs[2 + 4 * sources :]
    levels, lead = lead_ref.shape[0], lead_ref.shape[1]
    size, total = mat_ref.shape[1], mat_ref.shape[2]
    width = first[0][0].shape[1] // own_count
    height = size + trait_rows
    held, train = fold_lanes(own_count, width)
    ones_ref[...] = jnp.ones((8, LANES), F32)
    wide_ref[:, 0:height] = training_product(first, last, train, width, slice(0, lead)) / learning_tally
    wide_ref[:, height:total] = jnp.zeros((lead, total - height), F32)
    solved = dot_f32(lead_ref[...].reshape(levels * lead, lead), wide_ref[...])
    for r in range(levels):
        solved_ref[:, r * total : (r + 1) * total] = solved[r * lead : (r + 1) * lead]
    diagonal = lax.broadcasted_iota(jnp.int32, (size, height), 1) == lax.broadcasted_iota(
        jnp.int32, (size, height), 0
    )
    rows = slice(0, size)
    side = training_product(last, first, train, width, rows) / learning_tally
    acc = training_product(last, last, train, width, rows) / learning_tally
    known = dot_f32(side, solved_ref[...])
    for r in range(levels):
        mat_ref[r, :, 0:height] = (
            acc + jnp.where(diagonal, shrink_ref[r], 0.0) - known[:, r * total : r * total + height]
        )
        mat_ref[r, :, height:total] = jnp.zeros((size, total - height), F32)

    def follow(j, r):
        c0, c1 = j * LANES, (j + 1) * LANES
        solved = dot_f32(inv_ref[r], mat_ref[r, c0:c1, c1:total])
        for lo, hi in ((0, c0), (c1, size)):
            if hi > lo:
                mat_ref[r, lo:hi, c1:total] = mat_ref[r, lo:hi, c1:total] - dot_f32(mat_ref[r, lo:hi, c0:c1], solved)
        mat_ref[r, c0:c1, c1:total] = solved

    stages(size // LANES, levels, mat_ref, inv_ref, ones_ref, follow)
    beta_ref[...] = jnp.zeros(beta_ref.shape, F32)
    for r in range(levels):
        low = mat_ref[r, :, size:total]
        top = solved_ref[:, r * total + size : (r + 1) * total] - dot_f32(
            solved_ref[:, r * total : r * total + size], low
        )
        beta_ref[r * traits : (r + 1) * traits, 0:lead] = jnp.transpose(top)[0:traits, :]
        beta_ref[r * traits : (r + 1) * traits, lead : lead + size] = jnp.transpose(low)[0:traits, :]
    betas = beta_ref[...].astype(BF16)
    for s in range(sources):
        lanes = slice(s * width, (s + 1) * width)
        held_geno = jnp.concatenate(
            [first[1][s][:, pl.ds(held, width)], last[1][s][0:size, pl.ds(held, width)]], axis=0
        )
        message_ref[:, lanes] = jnp.dot(betas, held_geno, preferred_element_type=F32).astype(BF16)
        for f, start in enumerate([held] + train):
            trait_ref[f, :, lanes] = last[1][s ^ f][size : size + trait_rows, pl.ds(start, width)]


def level_kernel(own_count, trait_rows, held_rows, trait_ref, *refs):
    pred_ref, gram_ref, cross_ref, wide_ref = refs[-4:]
    n_blocks = (len(refs) - 4) // own_count
    traits, levels, width = pred_ref.shape[2:]
    rows = round_up(traits, 8)
    me = lax.axis_index("samples")
    block = lax.axis_index("blocks")
    pick = lax.rem(me, own_count)
    lane = lax.broadcasted_iota(jnp.int32, (rows, LANES), 1)
    for f in range(own_count):
        slot = pick ^ f
        for e in range(n_blocks):
            wide_ref[e] = refs[f * n_blocks + e][...].astype(F32)
        pred_ref[slot, 0] = jnp.stack(
            [wide_ref[0, r * traits : (r + 1) * traits, f * width : (f + 1) * width] for r in range(levels)], axis=1
        ).astype(BF16)
        wide = [[wide_ref[e, s * traits : s * traits + rows, :] for s in range(levels)] for e in range(n_blocks)]
        trait = trait_ref[f].astype(F32)[0:rows]
        for r in range(levels):
            out = jnp.where(lane == n_blocks * levels, jnp.sum(wide[0][r] * trait, axis=1, keepdims=True), 0.0)
            for e in range(n_blocks):
                column = lax.rem(block - e + n_blocks, n_blocks) * levels
                for s in range(levels):
                    total = jnp.sum(wide[0][r] * wide[e][s], axis=1, keepdims=True)
                    out = out + jnp.where(lane == column + s, total, 0.0)
            turned = jnp.transpose(out) / held_rows
            for c in range(n_blocks):
                gram_ref[slot, 0, r, c] = turned[c * levels : (c + 1) * levels, 0:traits]
            cross_ref[slot, 0, r : r + 1, :] = turned[n_blocks * levels : n_blocks * levels + 1, 0:traits]


def land(value, copies):
    if copies * value.size * value.dtype.itemsize > VMEM_SHARE:
        return value
    return pltpu.with_memory_space_constraint(value, pltpu.VMEM)


def kept(shape, dtype, copies):
    struct = jax.ShapeDtypeStruct(shape, dtype)
    if copies * struct.size * struct.dtype.itemsize > VMEM_SHARE:
        return struct
    return pltpu.VMEM(shape, dtype)


def per_device(allele_dosage_table, phenotype_values, individual_partition_label, shrink_strengths):
    cores = lax.axis_size("folds")
    sources = lax.axis_size("samples")
    n_blocks = lax.axis_size("blocks")
    own_count = FOLDS // cores
    levels = shrink_strengths.shape[0]
    variants, samples = allele_dosage_table.shape
    traits = phenotype_values.shape[0]
    width = samples // FOLDS
    held_rows = sources * width
    learning_tally = sources * samples - held_rows
    pad_rows = round_up(variants, LANES)
    lead = pad_rows // LANES // 2 * LANES
    size = pad_rows - lead
    trait_rows = round_up(traits, 32)
    half = own_count * width
    vmem = pl.BlockSpec(memory_space=pltpu.VMEM)
    smem = pl.BlockSpec(memory_space=pltpu.SMEM)

    def sort(offset, height, with_traits):
        count = min(variants - offset, height)
        inputs = [allele_dosage_table, phenotype_values, individual_partition_label.reshape(1, samples)]
        block = lead if lead == size else variants
        specs = [
            pl.BlockSpec((block, samples), lambda i: (offset // block, 0)),
            pl.BlockSpec((traits, samples), lambda i: (0, 0)),
            pl.BlockSpec((1, samples), lambda i: (0, 0)),
        ]
        kernel = functools.partial(sort_kernel, own_count, offset % block, count)
        if not with_traits:
            del inputs[1], specs[1]

            def kernel(geno_ref, label_ref, *outs):
                sort_kernel(own_count, offset % block, count, geno_ref, None, label_ref, *outs)

        return pl.pallas_call(
            kernel,
            grid=(1,),
            out_shape=[kept((height, half), BF16, 2 * sources)] * 2,
            in_specs=specs,
            out_specs=[pl.BlockSpec((height, half), lambda i: (0, 0))] * 2,
            name="sort_samples",
        )(*inputs)

    other_lead, own_lead = sort(0, lead, False)
    other_tail, own_tail = sort(lead, size + trait_rows, True)

    def fetch(other):
        return [land(other, 2 * sources)] + [
            land(lax.ppermute(other, "samples", [(i, i ^ d) for i in range(sources)]), 2 * sources) for d in range(1, sources)
        ]

    def swap(own, others):
        return [land(own, 2 * sources)] + [land(lax.ppermute(x, "folds", [(i, cores - 1 - i) for i in range(cores)]), 2 * sources) for x in others[1:]]

    others_lead = fetch(other_lead)
    owns_lead = swap(own_lead, others_lead)
    other_tail, *others_lead[1:] = lax.optimization_barrier((other_tail, *others_lead[1:]))
    others_tail = fetch(other_tail)
    lead_inverse = pl.pallas_call(
        functools.partial(lead_kernel, sources, own_count, learning_tally),
        out_shape=kept((levels, lead, lead), F32, sources // 2),
        in_specs=[smem] + [vmem] * (2 * sources),
        out_specs=vmem,
        scratch_shapes=[pltpu.VMEM((levels, LANES, LANES), F32), pltpu.VMEM((8, LANES), F32)],
        name="invert_lead",
    )(shrink_strengths, *others_lead, *owns_lead)
    lead_inverse, *others_tail[1:] = lax.optimization_barrier((lead_inverse, *others_tail[1:]))
    lead_inverse = land(lead_inverse, sources // 2)
    owns_tail = swap(own_tail, others_tail)
    message_rows = round_up((levels - 1) * traits + round_up(traits, 8), 16)
    message, trait_rows_held = pl.pallas_call(
        functools.partial(tail_kernel, sources, own_count, learning_tally, traits, trait_rows),
        out_shape=[
            kept((message_rows, sources * width), BF16, sources),
            kept((own_count, trait_rows, sources * width), BF16, sources),
        ],
        in_specs=[smem] + [vmem] * (1 + 4 * sources),
        out_specs=[vmem] * 2,
        scratch_shapes=[
            pltpu.VMEM((lead, size + LANES), F32),
            pltpu.VMEM((lead, levels * (size + LANES)), F32),
            pltpu.VMEM((levels, size, size + LANES), F32),
            pltpu.VMEM((levels, LANES, LANES), F32),
            pltpu.VMEM((8, LANES), F32),
            pltpu.VMEM((message_rows, pad_rows), F32),
        ],
        name="solve_tail",
    )(shrink_strengths, lead_inverse, *others_lead, *owns_lead, *others_tail, *owns_tail)

    messages = []
    for f in range(own_count):
        for e in range(n_blocks):
            if f == 0 and e == 0:
                messages.append(land(message, own_count * n_blocks))
                continue
            pairs = []
            for s in range(sources):
                for b in range(n_blocks):
                    pairs.append(((s ^ f) * n_blocks + (b - e) % n_blocks, s * n_blocks + b))
            messages.append(land(lax.ppermute(message, ("samples", "blocks"), pairs), own_count * n_blocks))

    preds, gram, cross = pl.pallas_call(
        functools.partial(level_kernel, own_count, trait_rows, held_rows),
        out_shape=[
            jax.ShapeDtypeStruct((own_count, 1, traits, levels, width), BF16),
            jax.ShapeDtypeStruct((own_count, 1, levels, n_blocks, levels, traits), F32),
            jax.ShapeDtypeStruct((own_count, 1, levels, traits), F32),
        ],
        in_specs=[vmem] * (1 + len(messages)),
        out_specs=[vmem] * 3,
        scratch_shapes=[pltpu.VMEM((n_blocks, message_rows, sources * width), F32)],
        name="level_one",
    )(land(trait_rows_held, sources), *messages)
    return jnp.swapaxes(preds, 2, 3), jnp.moveaxis(gram, 5, 3), cross


def solution(mesh):
    in_specs = (
        P("blocks", ("groups", "samples")),
        P(None, ("groups", "samples")),
        P(("groups", "samples")),
        P(),
    )
    out_specs = (
        P("folds", "blocks", None, None, ("groups", "samples")),
        P(("groups", "folds"), "blocks", None, None, None, None),
        P(("groups", "folds"), "blocks", None, None),
    )
    return jax.shard_map(
        per_device, mesh=mesh, in_specs=in_specs, out_specs=out_specs, check_vma=False
    )
```

```python
import functools

import jax
import jax.numpy as jnp
from jax import lax
from jax.experimental import pallas as pl
from jax.experimental.pallas import tpu as pltpu
from jax.sharding import PartitionSpec as P

SHRINK_LEVELS = 2
FOLDS = 4
LANES = 128
PANEL = 32
PIVOTS = 8
HIGHEST = lax.Precision.HIGHEST
VMEM_SHARE = 2 << 20
F32 = jnp.float32
BF16 = jnp.bfloat16


def round_up(value, step):
    return (value + step - 1) // step * step


def dot_nt(left, right):
    return lax.dot_general(left, right, (((1,), (1,)), ((), ())), preferred_element_type=F32)


def spread(value):
    return jnp.broadcast_to(value, (8, LANES))


def sort_kernel(own_count, offset, variants, geno_ref, trait_ref, label_ref, other_ref, own_ref):
    rows = label_ref.shape[1]
    core = lax.axis_index("folds")
    cores = lax.axis_size("folds")
    slot = lax.rem(label_ref[...] + own_count * (cores - 1 - core), FOLDS)
    width = rows // FOLDS
    before = lax.broadcasted_iota(jnp.int32, (rows, rows), 0) < lax.broadcasted_iota(jnp.int32, (rows, rows), 1)
    fold_row = lax.broadcasted_iota(jnp.int32, (16, rows), 0)
    hit = jnp.broadcast_to(slot, (16, rows)) == fold_row
    rank = jnp.dot(
        jnp.where(hit, 1.0, 0.0).astype(BF16),
        jnp.where(before, 1.0, 0.0).astype(BF16),
        preferred_element_type=F32,
    )
    place = jnp.sum(jnp.where(hit, rank + (fold_row * width).astype(F32), 0.0), axis=0, keepdims=True)
    place = place.astype(jnp.int32)
    target = lax.broadcasted_iota(jnp.int32, (rows, rows), 0)
    move = jnp.where(target == jnp.broadcast_to(place, (rows, rows)), 1.0, 0.0).astype(BF16)
    sorted_geno = dot_nt(geno_ref[offset : offset + variants, :], move).astype(BF16)
    height, half = other_ref.shape
    size = height if trait_ref is None else height - round_up(trait_ref.shape[0], 32)
    for part, ref in enumerate((other_ref, own_ref)):
        lanes = slice(part * half, (part + 1) * half)
        low = variants // 16 * 16
        if low < height:
            ref[low:height, :] = jnp.zeros((height - low, half), BF16)
        ref[0:variants, :] = sorted_geno[:, lanes]
        if trait_ref is not None:
            ref[size : size + trait_ref.shape[0], :] = dot_nt(trait_ref[...], move)[:, lanes].astype(BF16)


def eliminate_panel(panels, first, ones):
    lane = lax.broadcasted_iota(jnp.int32, (8, LANES), 1)
    sub = lax.broadcasted_iota(jnp.int32, (8, LANES), 0)
    systems = range(len(panels))
    count = len(panels[0])
    panels = [list(panel) for panel in panels]
    for b in range(count):
        base_col = first + 8 * b
        in_pivot = (lane >= base_col) & (lane < base_col + 8)
        rest = [(b + 1 + i) % count for i in range(count - 1)]
        cols = [[None] * 8 for _ in systems]
        factors = [{i: [None] * 8 for i in rest} for _ in systems]
        for u in range(8):
            for q in systems:
                cols[q][u] = spread(panels[q][b][:, base_col + u : base_col + u + 1]) * ones
        for u in range(8):
            for q in systems:
                for i in rest:
                    factors[q][i][u] = spread(panels[q][i][:, base_col + u : base_col + u + 1])
        for t in range(0, 8, 2):
            first_lane, second_lane = lane == base_col + t, lane == base_col + t + 1
            first_row, second_row = sub == t, sub == t + 1
            for q in systems:
                left, right, panel = cols[q][t], cols[q][t + 1], panels[q][b]
                corner = spread(left[t : t + 1, :])
                upper = spread(right[t : t + 1, :])
                lower = spread(left[t + 1 : t + 2, :])
                other = spread(right[t + 1 : t + 2, :])
                inverse = 1.0 / corner
                second = corner * (1.0 / (corner * other - upper * lower))
                ratio = lower * inverse
                factor = jnp.where(first_row, -1.0, left) * inverse
                after = jnp.where(first_row, 0.0, right) - factor * upper
                after = jnp.where(second_row, -1.0, after) * second
                factor = jnp.where(second_row, 0.0, factor)
                pair = first_row | second_row
                for u in range(t + 2, 8):
                    col = cols[q][u]
                    row = spread(col[t : t + 1, :])
                    next_row = spread(col[t + 1 : t + 2, :]) - ratio * row
                    cols[q][u] = jnp.where(pair, 0.0, col) - factor * row - after * next_row
                row = jnp.where(first_lane, 1.0, jnp.where(second_lane, 0.0, spread(panel[t : t + 1, :])))
                next_row = jnp.where(first_lane, 0.0, spread(panel[t + 1 : t + 2, :])) - ratio * row
                next_row = jnp.where(second_lane, 1.0, next_row)
                keep = jnp.where(pair | first_lane | second_lane, 0.0, panel)
                panels[q][b] = keep - factor * row - after * next_row
        for q in systems:
            rows = [spread(panels[q][b][t : t + 1, :]) for t in range(8)]
            for i in rest:
                parts = [factors[q][i][t] * rows[t] for t in range(8)]
                while len(parts) > 1:
                    parts = [parts[k] + parts[k + 1] for k in range(0, len(parts), 2)]
                panels[q][i] = jnp.where(in_pivot, 0.0, panels[q][i]) - parts[0]
    return panels


def invert_blocks(blocks, ones):
    lane = lax.broadcasted_iota(jnp.int32, (LANES, LANES), 1)
    row = lax.broadcasted_iota(jnp.int32, (LANES, LANES), 0)
    blocks = list(blocks)
    for b in range(LANES // PANEL):
        r0 = PANEL * b
        panels = eliminate_panel(
            [[block[r0 + 8 * i : r0 + 8 * i + 8, :] for i in range(PANEL // 8)] for block in blocks], r0, ones
        )
        for q, block in enumerate(blocks):
            pieces = list(panels[q])
            if r0:
                pieces.insert(0, jnp.zeros((r0, LANES), F32))
            if LANES - PANEL - r0:
                pieces.append(jnp.zeros((LANES - PANEL - r0, LANES), F32))
            wide = jnp.concatenate(pieces, axis=0)
            keep = jnp.where((lane >= r0) & (lane < r0 + PANEL), 0.0, block)
            update = keep - jnp.dot(block, wide, precision=HIGHEST, preferred_element_type=F32)
            blocks[q] = jnp.where((row >= r0) & (row < r0 + PANEL), wide, update)
    return blocks


def dot_f32(left, right):
    return jnp.dot(left, right, precision=HIGHEST, preferred_element_type=F32)


def fold_lanes(own_count, width):
    pick = lax.rem(lax.axis_index("samples"), own_count)
    held = pl.multiple_of(pick * width, width)
    train = [pl.multiple_of((pick ^ f) * width, width) for f in range(1, own_count)]
    return held, train


def training_product(left, right, train, width, rows):
    lefts, rights = [], []
    for left_other, left_own, right_other, right_own in zip(*left, *right):
        lefts.append(left_other[rows, :])
        rights.append(right_other[...])
        for start in train:
            lefts.append(left_own[rows, pl.ds(start, width)])
            rights.append(right_own[:, pl.ds(start, width)])
    return dot_nt(jnp.concatenate(lefts, axis=1), jnp.concatenate(rights, axis=1))


def stages(count, levels, mat_ref, inv_ref, ones_ref, follow):
    def stage(j, carry):
        start = pl.multiple_of(j * LANES, LANES)
        inverses = invert_blocks(
            [mat_ref[r, pl.ds(start, LANES), pl.ds(start, LANES)] for r in range(levels)], ones_ref[...]
        )
        for r in range(levels):
            inv_ref[r] = inverses[r]
        for jj in range(count):

            @pl.when(j == jj)
            def _():
                for r in range(levels):
                    follow(jj, r)

        return carry

    lax.fori_loop(0, count, stage, 0)


def lead_kernel(sources, own_count, learning_tally, *refs):
    shrink_ref = refs[0]
    others, owns = refs[1 : 1 + sources], refs[1 + sources : 1 + 2 * sources]
    out_ref, inv_ref, ones_ref = refs[1 + 2 * sources :]
    levels, size = out_ref.shape[0], out_ref.shape[1]
    width = others[0].shape[1] // own_count
    _, train = fold_lanes(own_count, width)
    ones_ref[...] = jnp.ones((8, LANES), F32)
    diagonal = lax.broadcasted_iota(jnp.int32, (size, size), 1) == lax.broadcasted_iota(jnp.int32, (size, size), 0)
    acc = training_product((others, owns), (others, owns), train, width, slice(0, size)) / learning_tally
    for r in range(levels):
        out_ref[r] = acc + jnp.where(diagonal, shrink_ref[r], 0.0)

    def follow(j, r):
        c0, c1 = j * LANES, (j + 1) * LANES
        inverse = inv_ref[r]
        spans = [(lo, hi) for lo, hi in ((0, c0), (c1, size)) if hi > lo]
        solved = [dot_f32(inverse, out_ref[r, c0:c1, lo:hi]) for lo, hi in spans]
        for lo, hi in spans:
            column = out_ref[r, lo:hi, c0:c1]
            for (left, right), value in zip(spans, solved):
                out_ref[r, lo:hi, left:right] = out_ref[r, lo:hi, left:right] - dot_f32(column, value)
            out_ref[r, lo:hi, c0:c1] = -dot_f32(column, inverse)
        for (left, right), value in zip(spans, solved):
            out_ref[r, c0:c1, left:right] = value
        out_ref[r, c0:c1, c0:c1] = inverse

    stages(size // LANES, levels, out_ref, inv_ref, ones_ref, follow)


def tail_kernel(sources, own_count, learning_tally, traits, trait_rows, *refs):
    shrink_ref, lead_ref = refs[0:2]
    first = (refs[2 : 2 + sources], refs[2 + sources : 2 + 2 * sources])
    last = (refs[2 + 2 * sources : 2 + 3 * sources], refs[2 + 3 * sources : 2 + 4 * sources])
    message_ref, trait_ref, wide_ref, solved_ref, mat_ref, inv_ref, ones_ref, beta_ref = refs[2 + 4 * sources :]
    levels, lead = lead_ref.shape[0], lead_ref.shape[1]
    size, total = mat_ref.shape[1], mat_ref.shape[2]
    width = first[0][0].shape[1] // own_count
    height = size + trait_rows
    held, train = fold_lanes(own_count, width)
    ones_ref[...] = jnp.ones((8, LANES), F32)
    wide_ref[:, 0:height] = training_product(first, last, train, width, slice(0, lead)) / learning_tally
    wide_ref[:, height:total] = jnp.zeros((lead, total - height), F32)
    solved = dot_f32(lead_ref[...].reshape(levels * lead, lead), wide_ref[...])
    for r in range(levels):
        solved_ref[:, r * total : (r + 1) * total] = solved[r * lead : (r + 1) * lead]
    diagonal = lax.broadcasted_iota(jnp.int32, (size, height), 1) == lax.broadcasted_iota(
        jnp.int32, (size, height), 0
    )
    rows = slice(0, size)
    side = training_product(last, first, train, width, rows) / learning_tally
    acc = training_product(last, last, train, width, rows) / learning_tally
    known = dot_f32(side, solved_ref[...])
    for r in range(levels):
        mat_ref[r, :, 0:height] = (
            acc + jnp.where(diagonal, shrink_ref[r], 0.0) - known[:, r * total : r * total + height]
        )
        mat_ref[r, :, height:total] = jnp.zeros((size, total - height), F32)

    def follow(j, r):
        c0, c1 = j * LANES, (j + 1) * LANES
        solved = dot_f32(inv_ref[r], mat_ref[r, c0:c1, c1:total])
        for lo, hi in ((0, c0), (c1, size)):
            if hi > lo:
                mat_ref[r, lo:hi, c1:total] = mat_ref[r, lo:hi, c1:total] - dot_f32(mat_ref[r, lo:hi, c0:c1], solved)
        mat_ref[r, c0:c1, c1:total] = solved

    stages(size // LANES, levels, mat_ref, inv_ref, ones_ref, follow)
    beta_ref[...] = jnp.zeros(beta_ref.shape, F32)
    for r in range(levels):
        low = mat_ref[r, :, size:total]
        top = solved_ref[:, r * total + size : (r + 1) * total] - dot_f32(
            solved_ref[:, r * total : r * total + size], low
        )
        beta_ref[r * traits : (r + 1) * traits, 0:lead] = jnp.transpose(top)[0:traits, :]
        beta_ref[r * traits : (r + 1) * traits, lead : lead + size] = jnp.transpose(low)[0:traits, :]
    betas = beta_ref[...].astype(BF16)
    for s in range(sources):
        lanes = slice(s * width, (s + 1) * width)
        held_geno = jnp.concatenate(
            [first[1][s][:, pl.ds(held, width)], last[1][s][0:size, pl.ds(held, width)]], axis=0
        )
        message_ref[:, lanes] = jnp.dot(betas, held_geno, preferred_element_type=F32).astype(BF16)
        for f, start in enumerate([held] + train):
            trait_ref[f, :, lanes] = last[1][s ^ f][size : size + trait_rows, pl.ds(start, width)]


def level_kernel(own_count, trait_rows, held_rows, trait_ref, *refs):
    pred_ref, gram_ref, cross_ref, wide_ref = refs[-4:]
    n_blocks = (len(refs) - 4) // own_count
    traits, levels, width = pred_ref.shape[2:]
    rows = round_up(traits, 8)
    me = lax.axis_index("samples")
    block = lax.axis_index("blocks")
    pick = lax.rem(me, own_count)
    lane = lax.broadcasted_iota(jnp.int32, (rows, LANES), 1)
    for f in range(own_count):
        slot = pick ^ f
        for e in range(n_blocks):
            wide_ref[e] = refs[f * n_blocks + e][...].astype(F32)
        pred_ref[slot, 0] = jnp.stack(
            [wide_ref[0, r * traits : (r + 1) * traits, f * width : (f + 1) * width] for r in range(levels)], axis=1
        ).astype(BF16)
        wide = [[wide_ref[e, s * traits : s * traits + rows, :] for s in range(levels)] for e in range(n_blocks)]
        trait = trait_ref[f].astype(F32)[0:rows]
        for r in range(levels):
            out = jnp.where(lane == n_blocks * levels, jnp.sum(wide[0][r] * trait, axis=1, keepdims=True), 0.0)
            for e in range(n_blocks):
                column = lax.rem(block - e + n_blocks, n_blocks) * levels
                for s in range(levels):
                    total = jnp.sum(wide[0][r] * wide[e][s], axis=1, keepdims=True)
                    out = out + jnp.where(lane == column + s, total, 0.0)
            turned = jnp.transpose(out) / held_rows
            for c in range(n_blocks):
                gram_ref[slot, 0, r, c] = turned[c * levels : (c + 1) * levels, 0:traits]
            cross_ref[slot, 0, r : r + 1, :] = turned[n_blocks * levels : n_blocks * levels + 1, 0:traits]


def land(value, copies):
    if copies * value.size * value.dtype.itemsize > VMEM_SHARE:
        return value
    return pltpu.with_memory_space_constraint(value, pltpu.VMEM)


def kept(shape, dtype, copies):
    struct = jax.ShapeDtypeStruct(shape, dtype)
    if copies * struct.size * struct.dtype.itemsize > VMEM_SHARE:
        return struct
    return pltpu.VMEM(shape, dtype)


def per_device(allele_dosage_table, phenotype_values, individual_partition_label, shrink_strengths):
    cores = lax.axis_size("folds")
    sources = lax.axis_size("samples")
    n_blocks = lax.axis_size("blocks")
    own_count = FOLDS // cores
    levels = shrink_strengths.shape[0]
    variants, samples = allele_dosage_table.shape
    traits = phenotype_values.shape[0]
    width = samples // FOLDS
    held_rows = sources * width
    learning_tally = sources * samples - held_rows
    pad_rows = round_up(variants, LANES)
    lead = pad_rows // LANES // 2 * LANES
    size = pad_rows - lead
    trait_rows = round_up(traits, 32)
    half = own_count * width
    vmem = pl.BlockSpec(memory_space=pltpu.VMEM)
    smem = pl.BlockSpec(memory_space=pltpu.SMEM)

    def sort(offset, height, with_traits):
        count = min(variants - offset, height)
        inputs = [allele_dosage_table, phenotype_values, individual_partition_label.reshape(1, samples)]
        block = lead if lead == size else variants
        specs = [
            pl.BlockSpec((block, samples), lambda i: (offset // block, 0)),
            pl.BlockSpec((traits, samples), lambda i: (0, 0)),
            pl.BlockSpec((1, samples), lambda i: (0, 0)),
        ]
        kernel = functools.partial(sort_kernel, own_count, offset % block, count)
        if not with_traits:
            del inputs[1], specs[1]

            def kernel(geno_ref, label_ref, *outs):
                sort_kernel(own_count, offset % block, count, geno_ref, None, label_ref, *outs)

        return pl.pallas_call(
            kernel,
            grid=(1,),
            out_shape=[kept((height, half), BF16, 2 * sources)] * 2,
            in_specs=specs,
            out_specs=[pl.BlockSpec((height, half), lambda i: (0, 0))] * 2,
            name="sort_samples",
        )(*inputs)

    other_lead, own_lead = sort(0, lead, False)
    other_tail, own_tail = sort(lead, size + trait_rows, True)

    def move(other, d):
        return land(lax.ppermute(other, "samples", [(i, i ^ d) for i in range(sources)]), 2 * sources)

    def fetch(other, first, last):
        return [move(other, d) for d in range(first, last)]

    def swap(own, others):
        return [land(own, 2 * sources)] + [land(lax.ppermute(x, "folds", [(i, cores - 1 - i) for i in range(cores)]), 2 * sources) for x in others[1:]]

    others_lead = [land(other_lead, 2 * sources)] + fetch(other_lead, 1, sources)
    owns_lead = swap(own_lead, others_lead)
    others_tail = [land(other_tail, 2 * sources)] + fetch(other_tail, 1, 2)
    other_tail, *others_lead[1:] = lax.optimization_barrier((other_tail, *others_lead[1:]))
    others_tail += fetch(other_tail, 2, sources)
    lead_inverse = pl.pallas_call(
        functools.partial(lead_kernel, sources, own_count, learning_tally),
        out_shape=kept((levels, lead, lead), F32, sources // 2),
        in_specs=[smem] + [vmem] * (2 * sources),
        out_specs=vmem,
        scratch_shapes=[pltpu.VMEM((levels, LANES, LANES), F32), pltpu.VMEM((8, LANES), F32)],
        name="invert_lead",
    )(shrink_strengths, *others_lead, *owns_lead)
    lead_inverse, *others_tail[1:] = lax.optimization_barrier((lead_inverse, *others_tail[1:]))
    lead_inverse = land(lead_inverse, sources // 2)
    owns_tail = swap(own_tail, others_tail)
    message_rows = round_up((levels - 1) * traits + round_up(traits, 8), 16)
    message, trait_rows_held = pl.pallas_call(
        functools.partial(tail_kernel, sources, own_count, learning_tally, traits, trait_rows),
        out_shape=[
            kept((message_rows, sources * width), BF16, sources),
            kept((own_count, trait_rows, sources * width), BF16, sources),
        ],
        in_specs=[smem] + [vmem] * (1 + 4 * sources),
        out_specs=[vmem] * 2,
        scratch_shapes=[
            pltpu.VMEM((lead, size + LANES), F32),
            pltpu.VMEM((lead, levels * (size + LANES)), F32),
            pltpu.VMEM((levels, size, size + LANES), F32),
            pltpu.VMEM((levels, LANES, LANES), F32),
            pltpu.VMEM((8, LANES), F32),
            pltpu.VMEM((message_rows, pad_rows), F32),
        ],
        name="solve_tail",
    )(shrink_strengths, lead_inverse, *others_lead, *owns_lead, *others_tail, *owns_tail)

    messages = []
    for f in range(own_count):
        for e in range(n_blocks):
            if f == 0 and e == 0:
                messages.append(land(message, own_count * n_blocks))
                continue
            pairs = []
            for s in range(sources):
                for b in range(n_blocks):
                    pairs.append(((s ^ f) * n_blocks + (b - e) % n_blocks, s * n_blocks + b))
            messages.append(land(lax.ppermute(message, ("samples", "blocks"), pairs), own_count * n_blocks))

    preds, gram, cross = pl.pallas_call(
        functools.partial(level_kernel, own_count, trait_rows, held_rows),
        out_shape=[
            jax.ShapeDtypeStruct((own_count, 1, traits, levels, width), BF16),
            jax.ShapeDtypeStruct((own_count, 1, levels, n_blocks, levels, traits), F32),
            jax.ShapeDtypeStruct((own_count, 1, levels, traits), F32),
        ],
        in_specs=[vmem] * (1 + len(messages)),
        out_specs=[vmem] * 3,
        scratch_shapes=[pltpu.VMEM((n_blocks, message_rows, sources * width), F32)],
        name="level_one",
    )(land(trait_rows_held, sources), *messages)
    return jnp.swapaxes(preds, 2, 3), jnp.moveaxis(gram, 5, 3), cross


def solution(mesh):
    in_specs = (
        P("blocks", ("groups", "samples")),
        P(None, ("groups", "samples")),
        P(("groups", "samples")),
        P(),
    )
    out_specs = (
        P("folds", "blocks", None, None, ("groups", "samples")),
        P(("groups", "folds"), "blocks", None, None, None, None),
        P(("groups", "folds"), "blocks", None, None),
    )
    return jax.shard_map(
        per_device, mesh=mesh, in_specs=in_specs, out_specs=out_specs, check_vma=False
    )
```

```python
import functools

import jax
import jax.numpy as jnp
from jax import lax
from jax.experimental import pallas as pl
from jax.experimental.pallas import tpu as pltpu
from jax.sharding import PartitionSpec as P

SHRINK_LEVELS = 2
FOLDS = 4
LANES = 128
PANEL = 32
PIVOTS = 8
HIGHEST = lax.Precision.HIGHEST
VMEM_SHARE = 2 << 20
F32 = jnp.float32
BF16 = jnp.bfloat16


def round_up(value, step):
    return (value + step - 1) // step * step


def dot_nt(left, right):
    return lax.dot_general(left, right, (((1,), (1,)), ((), ())), preferred_element_type=F32)


def spread(value):
    return jnp.broadcast_to(value, (8, LANES))


def sort_kernel(own_count, offset, variants, geno_ref, trait_ref, label_ref, other_ref, own_ref):
    rows = label_ref.shape[1]
    core = lax.axis_index("folds")
    cores = lax.axis_size("folds")
    slot = lax.rem(label_ref[...] + own_count * (cores - 1 - core), FOLDS)
    width = rows // FOLDS
    before = lax.broadcasted_iota(jnp.int32, (rows, rows), 0) < lax.broadcasted_iota(jnp.int32, (rows, rows), 1)
    fold_row = lax.broadcasted_iota(jnp.int32, (16, rows), 0)
    hit = jnp.broadcast_to(slot, (16, rows)) == fold_row
    rank = jnp.dot(
        jnp.where(hit, 1.0, 0.0).astype(BF16),
        jnp.where(before, 1.0, 0.0).astype(BF16),
        preferred_element_type=F32,
    )
    place = jnp.sum(jnp.where(hit, rank + (fold_row * width).astype(F32), 0.0), axis=0, keepdims=True)
    place = place.astype(jnp.int32)
    target = lax.broadcasted_iota(jnp.int32, (rows, rows), 0)
    move = jnp.where(target == jnp.broadcast_to(place, (rows, rows)), 1.0, 0.0).astype(BF16)
    sorted_geno = dot_nt(geno_ref[offset : offset + variants, :], move).astype(BF16)
    height, half = other_ref.shape
    size = height if trait_ref is None else height - round_up(trait_ref.shape[0], 32)
    for part, ref in enumerate((other_ref, own_ref)):
        lanes = slice(part * half, (part + 1) * half)
        low = variants // 16 * 16
        if low < height:
            ref[low:height, :] = jnp.zeros((height - low, half), BF16)
        ref[0:variants, :] = sorted_geno[:, lanes]
        if trait_ref is not None:
            ref[size : size + trait_ref.shape[0], :] = dot_nt(trait_ref[...], move)[:, lanes].astype(BF16)


def eliminate_panel(panels, first, ones):
    lane = lax.broadcasted_iota(jnp.int32, (8, LANES), 1)
    sub = lax.broadcasted_iota(jnp.int32, (8, LANES), 0)
    systems = range(len(panels))
    count = len(panels[0])
    panels = [list(panel) for panel in panels]
    for b in range(count):
        base_col = first + 8 * b
        in_pivot = (lane >= base_col) & (lane < base_col + 8)
        rest = [(b + 1 + i) % count for i in range(count - 1)]
        cols = [[None] * 8 for _ in systems]
        factors = [{i: [None] * 8 for i in rest} for _ in systems]
        for u in range(8):
            for q in systems:
                cols[q][u] = spread(panels[q][b][:, base_col + u : base_col + u + 1]) * ones
        for u in range(8):
            for q in systems:
                for i in rest:
                    factors[q][i][u] = spread(panels[q][i][:, base_col + u : base_col + u + 1])
        for t in range(0, 8, 2):
            first_lane, second_lane = lane == base_col + t, lane == base_col + t + 1
            first_row, second_row = sub == t, sub == t + 1
            for q in systems:
                left, right, panel = cols[q][t], cols[q][t + 1], panels[q][b]
                corner = spread(left[t : t + 1, :])
                upper = spread(right[t : t + 1, :])
                lower = spread(left[t + 1 : t + 2, :])
                other = spread(right[t + 1 : t + 2, :])
                inverse = 1.0 / corner
                second = corner * (1.0 / (corner * other - upper * lower))
                ratio = lower * inverse
                factor = jnp.where(first_row, -1.0, left) * inverse
                after = jnp.where(first_row, 0.0, right) - factor * upper
                after = jnp.where(second_row, -1.0, after) * second
                factor = jnp.where(second_row, 0.0, factor)
                pair = first_row | second_row
                for u in range(t + 2, 8):
                    col = cols[q][u]
                    row = spread(col[t : t + 1, :])
                    next_row = spread(col[t + 1 : t + 2, :]) - ratio * row
                    cols[q][u] = jnp.where(pair, 0.0, col) - factor * row - after * next_row
                row = jnp.where(first_lane, 1.0, jnp.where(second_lane, 0.0, spread(panel[t : t + 1, :])))
                next_row = jnp.where(first_lane, 0.0, spread(panel[t + 1 : t + 2, :])) - ratio * row
                next_row = jnp.where(second_lane, 1.0, next_row)
                keep = jnp.where(pair | first_lane | second_lane, 0.0, panel)
                panels[q][b] = keep - factor * row - after * next_row
        for q in systems:
            rows = [spread(panels[q][b][t : t + 1, :]) for t in range(8)]
            for i in rest:
                parts = [factors[q][i][t] * rows[t] for t in range(8)]
                while len(parts) > 1:
                    parts = [parts[k] + parts[k + 1] for k in range(0, len(parts), 2)]
                panels[q][i] = jnp.where(in_pivot, 0.0, panels[q][i]) - parts[0]
    return panels


def invert_blocks(blocks, ones):
    lane = lax.broadcasted_iota(jnp.int32, (LANES, LANES), 1)
    row = lax.broadcasted_iota(jnp.int32, (LANES, LANES), 0)
    blocks = list(blocks)
    for b in range(LANES // PANEL):
        r0 = PANEL * b
        panels = eliminate_panel(
            [[block[r0 + 8 * i : r0 + 8 * i + 8, :] for i in range(PANEL // 8)] for block in blocks], r0, ones
        )
        for q, block in enumerate(blocks):
            pieces = list(panels[q])
            if r0:
                pieces.insert(0, jnp.zeros((r0, LANES), F32))
            if LANES - PANEL - r0:
                pieces.append(jnp.zeros((LANES - PANEL - r0, LANES), F32))
            wide = jnp.concatenate(pieces, axis=0)
            keep = jnp.where((lane >= r0) & (lane < r0 + PANEL), 0.0, block)
            update = keep - jnp.dot(block, wide, precision=HIGHEST, preferred_element_type=F32)
            blocks[q] = jnp.where((row >= r0) & (row < r0 + PANEL), wide, update)
    return blocks


def dot_f32(left, right):
    return jnp.dot(left, right, precision=HIGHEST, preferred_element_type=F32)


def fold_lanes(own_count, width):
    pick = lax.rem(lax.axis_index("samples"), own_count)
    held = pl.multiple_of(pick * width, width)
    train = [pl.multiple_of((pick ^ f) * width, width) for f in range(1, own_count)]
    return held, train


def training_product(left, right, train, width, rows):
    lefts, rights = [], []
    for left_other, left_own, right_other, right_own in zip(*left, *right):
        lefts.append(left_other[rows, :])
        rights.append(right_other[...])
        for start in train:
            lefts.append(left_own[rows, pl.ds(start, width)])
            rights.append(right_own[:, pl.ds(start, width)])
    return dot_nt(jnp.concatenate(lefts, axis=1), jnp.concatenate(rights, axis=1))


def stages(count, levels, mat_ref, inv_ref, ones_ref, follow):
    def stage(j, carry):
        start = pl.multiple_of(j * LANES, LANES)
        inverses = invert_blocks(
            [mat_ref[r, pl.ds(start, LANES), pl.ds(start, LANES)] for r in range(levels)], ones_ref[...]
        )
        for r in range(levels):
            inv_ref[r] = inverses[r]
        for jj in range(count):

            @pl.when(j == jj)
            def _():
                for r in range(levels):
                    follow(jj, r)

        return carry

    lax.fori_loop(0, count, stage, 0)


def lead_kernel(sources, own_count, learning_tally, *refs):
    shrink_ref = refs[0]
    others, owns = refs[1 : 1 + sources], refs[1 + sources : 1 + 2 * sources]
    out_ref, inv_ref, ones_ref = refs[1 + 2 * sources :]
    levels, size = out_ref.shape[0], out_ref.shape[1]
    width = others[0].shape[1] // own_count
    _, train = fold_lanes(own_count, width)
    ones_ref[...] = jnp.ones((8, LANES), F32)
    diagonal = lax.broadcasted_iota(jnp.int32, (size, size), 1) == lax.broadcasted_iota(jnp.int32, (size, size), 0)
    acc = training_product((others, owns), (others, owns), train, width, slice(0, size)) / learning_tally
    for r in range(levels):
        out_ref[r] = acc + jnp.where(diagonal, shrink_ref[r], 0.0)

    def follow(j, r):
        c0, c1 = j * LANES, (j + 1) * LANES
        inverse = inv_ref[r]
        spans = [(lo, hi) for lo, hi in ((0, c0), (c1, size)) if hi > lo]
        solved = [dot_f32(inverse, out_ref[r, c0:c1, lo:hi]) for lo, hi in spans]
        for lo, hi in spans:
            column = out_ref[r, lo:hi, c0:c1]
            for (left, right), value in zip(spans, solved):
                out_ref[r, lo:hi, left:right] = out_ref[r, lo:hi, left:right] - dot_f32(column, value)
            out_ref[r, lo:hi, c0:c1] = -dot_f32(column, inverse)
        for (left, right), value in zip(spans, solved):
            out_ref[r, c0:c1, left:right] = value
        out_ref[r, c0:c1, c0:c1] = inverse

    stages(size // LANES, levels, out_ref, inv_ref, ones_ref, follow)


def tail_kernel(sources, own_count, learning_tally, traits, trait_rows, *refs):
    shrink_ref, lead_ref = refs[0:2]
    first = (refs[2 : 2 + sources], refs[2 + sources : 2 + 2 * sources])
    last = (refs[2 + 2 * sources : 2 + 3 * sources], refs[2 + 3 * sources : 2 + 4 * sources])
    message_ref, trait_ref, wide_ref, solved_ref, mat_ref, inv_ref, ones_ref, beta_ref = refs[2 + 4 * sources :]
    levels, lead = lead_ref.shape[0], lead_ref.shape[1]
    size, total = mat_ref.shape[1], mat_ref.shape[2]
    width = first[0][0].shape[1] // own_count
    height = size + trait_rows
    held, train = fold_lanes(own_count, width)
    ones_ref[...] = jnp.ones((8, LANES), F32)
    wide_ref[:, 0:height] = training_product(first, last, train, width, slice(0, lead)) / learning_tally
    wide_ref[:, height:total] = jnp.zeros((lead, total - height), F32)
    solved = dot_f32(lead_ref[...].reshape(levels * lead, lead), wide_ref[...])
    for r in range(levels):
        solved_ref[:, r * total : (r + 1) * total] = solved[r * lead : (r + 1) * lead]
    diagonal = lax.broadcasted_iota(jnp.int32, (size, height), 1) == lax.broadcasted_iota(
        jnp.int32, (size, height), 0
    )
    rows = slice(0, size)
    side = training_product(last, first, train, width, rows) / learning_tally
    acc = training_product(last, last, train, width, rows) / learning_tally
    known = dot_f32(side, solved_ref[...])
    for r in range(levels):
        mat_ref[r, :, 0:height] = (
            acc + jnp.where(diagonal, shrink_ref[r], 0.0) - known[:, r * total : r * total + height]
        )
        mat_ref[r, :, height:total] = jnp.zeros((size, total - height), F32)

    def follow(j, r):
        c0, c1 = j * LANES, (j + 1) * LANES
        solved = dot_f32(inv_ref[r], mat_ref[r, c0:c1, c1:total])
        for lo, hi in ((0, c0), (c1, size)):
            if hi > lo:
                mat_ref[r, lo:hi, c1:total] = mat_ref[r, lo:hi, c1:total] - dot_f32(mat_ref[r, lo:hi, c0:c1], solved)
        mat_ref[r, c0:c1, c1:total] = solved

    stages(size // LANES, levels, mat_ref, inv_ref, ones_ref, follow)
    beta_ref[...] = jnp.zeros(beta_ref.shape, F32)
    for r in range(levels):
        low = mat_ref[r, :, size:total]
        top = solved_ref[:, r * total + size : (r + 1) * total] - dot_f32(
            solved_ref[:, r * total : r * total + size], low
        )
        beta_ref[r * traits : (r + 1) * traits, 0:lead] = jnp.transpose(top)[0:traits, :]
        beta_ref[r * traits : (r + 1) * traits, lead : lead + size] = jnp.transpose(low)[0:traits, :]
    betas = beta_ref[...].astype(BF16)
    for s in range(sources):
        lanes = slice(s * width, (s + 1) * width)
        held_geno = jnp.concatenate(
            [first[1][s][:, pl.ds(held, width)], last[1][s][0:size, pl.ds(held, width)]], axis=0
        )
        message_ref[:, lanes] = jnp.dot(betas, held_geno, preferred_element_type=F32).astype(BF16)
        for f, start in enumerate([held] + train):
            trait_ref[f, :, lanes] = last[1][s ^ f][size : size + trait_rows, pl.ds(start, width)]


def level_kernel(own_count, trait_rows, held_rows, trait_ref, *refs):
    pred_ref, gram_ref, cross_ref, wide_ref = refs[-4:]
    n_blocks = (len(refs) - 4) // own_count
    traits, levels, width = pred_ref.shape[2:]
    rows = round_up(traits, 8)
    me = lax.axis_index("samples")
    block = lax.axis_index("blocks")
    pick = lax.rem(me, own_count)
    lane = lax.broadcasted_iota(jnp.int32, (rows, LANES), 1)
    for f in range(own_count):
        slot = pick ^ f
        for e in range(n_blocks):
            wide_ref[e] = refs[f * n_blocks + e][...].astype(F32)
        pred_ref[slot, 0] = jnp.stack(
            [wide_ref[0, r * traits : (r + 1) * traits, f * width : (f + 1) * width] for r in range(levels)], axis=1
        ).astype(BF16)
        wide = [[wide_ref[e, s * traits : s * traits + rows, :] for s in range(levels)] for e in range(n_blocks)]
        trait = trait_ref[f].astype(F32)[0:rows]
        for r in range(levels):
            out = jnp.where(lane == n_blocks * levels, jnp.sum(wide[0][r] * trait, axis=1, keepdims=True), 0.0)
            for e in range(n_blocks):
                column = lax.rem(block - e + n_blocks, n_blocks) * levels
                for s in range(levels):
                    total = jnp.sum(wide[0][r] * wide[e][s], axis=1, keepdims=True)
                    out = out + jnp.where(lane == column + s, total, 0.0)
            turned = jnp.transpose(out) / held_rows
            for c in range(n_blocks):
                gram_ref[slot, 0, r, c] = turned[c * levels : (c + 1) * levels, 0:traits]
            cross_ref[slot, 0, r : r + 1, :] = turned[n_blocks * levels : n_blocks * levels + 1, 0:traits]


def land(value, copies):
    if copies * value.size * value.dtype.itemsize > VMEM_SHARE:
        return value
    return pltpu.with_memory_space_constraint(value, pltpu.VMEM)


def kept(shape, dtype, copies):
    struct = jax.ShapeDtypeStruct(shape, dtype)
    if copies * struct.size * struct.dtype.itemsize > VMEM_SHARE:
        return struct
    return pltpu.VMEM(shape, dtype)


def per_device(allele_dosage_table, phenotype_values, individual_partition_label, shrink_strengths):
    cores = lax.axis_size("folds")
    sources = lax.axis_size("samples")
    n_blocks = lax.axis_size("blocks")
    own_count = FOLDS // cores
    levels = shrink_strengths.shape[0]
    variants, samples = allele_dosage_table.shape
    traits = phenotype_values.shape[0]
    width = samples // FOLDS
    held_rows = sources * width
    learning_tally = sources * samples - held_rows
    pad_rows = round_up(variants, LANES)
    lead = pad_rows // LANES // 2 * LANES
    size = pad_rows - lead
    trait_rows = round_up(traits, 32)
    half = own_count * width
    vmem = pl.BlockSpec(memory_space=pltpu.VMEM)
    smem = pl.BlockSpec(memory_space=pltpu.SMEM)

    def sort(offset, height, with_traits):
        count = min(variants - offset, height)
        inputs = [allele_dosage_table, phenotype_values, individual_partition_label.reshape(1, samples)]
        block = lead if lead == size else variants
        specs = [
            pl.BlockSpec((block, samples), lambda i: (offset // block, 0)),
            pl.BlockSpec((traits, samples), lambda i: (0, 0)),
            pl.BlockSpec((1, samples), lambda i: (0, 0)),
        ]
        kernel = functools.partial(sort_kernel, own_count, offset % block, count)
        if not with_traits:
            del inputs[1], specs[1]

            def kernel(geno_ref, label_ref, *outs):
                sort_kernel(own_count, offset % block, count, geno_ref, None, label_ref, *outs)

        return pl.pallas_call(
            kernel,
            grid=(1,),
            out_shape=[kept((height, half), BF16, 2 * sources)] * 2,
            in_specs=specs,
            out_specs=[pl.BlockSpec((height, half), lambda i: (0, 0))] * 2,
            name="sort_samples",
        )(*inputs)

    other_lead, own_lead = sort(0, lead, False)
    other_tail, own_tail = sort(lead, size + trait_rows, True)

    def move(other, d):
        return land(lax.ppermute(other, "samples", [(i, i ^ d) for i in range(sources)]), 2 * sources)

    def fetch(other, first, last):
        return [move(other, d) for d in range(first, last)]

    def swap(own, others):
        return [land(own, 2 * sources)] + [land(lax.ppermute(x, "folds", [(i, cores - 1 - i) for i in range(cores)]), 2 * sources) for x in others[1:]]

    others_lead = [land(other_lead, 2 * sources)] + fetch(other_lead, 1, sources)
    owns_lead = swap(own_lead, others_lead)
    others_tail = [land(other_tail, 2 * sources)] + fetch(other_tail, 1, 3)
    other_tail, *others_lead[1:] = lax.optimization_barrier((other_tail, *others_lead[1:]))
    others_tail += fetch(other_tail, 3, sources)
    lead_inverse = pl.pallas_call(
        functools.partial(lead_kernel, sources, own_count, learning_tally),
        out_shape=kept((levels, lead, lead), F32, sources // 2),
        in_specs=[smem] + [vmem] * (2 * sources),
        out_specs=vmem,
        scratch_shapes=[pltpu.VMEM((levels, LANES, LANES), F32), pltpu.VMEM((8, LANES), F32)],
        name="invert_lead",
    )(shrink_strengths, *others_lead, *owns_lead)
    lead_inverse, *others_tail[1:] = lax.optimization_barrier((lead_inverse, *others_tail[1:]))
    lead_inverse = land(lead_inverse, sources // 2)
    owns_tail = swap(own_tail, others_tail)
    message_rows = round_up((levels - 1) * traits + round_up(traits, 8), 16)
    message, trait_rows_held = pl.pallas_call(
        functools.partial(tail_kernel, sources, own_count, learning_tally, traits, trait_rows),
        out_shape=[
            kept((message_rows, sources * width), BF16, sources),
            kept((own_count, trait_rows, sources * width), BF16, sources),
        ],
        in_specs=[smem] + [vmem] * (1 + 4 * sources),
        out_specs=[vmem] * 2,
        scratch_shapes=[
            pltpu.VMEM((lead, size + LANES), F32),
            pltpu.VMEM((lead, levels * (size + LANES)), F32),
            pltpu.VMEM((levels, size, size + LANES), F32),
            pltpu.VMEM((levels, LANES, LANES), F32),
            pltpu.VMEM((8, LANES), F32),
            pltpu.VMEM((message_rows, pad_rows), F32),
        ],
        name="solve_tail",
    )(shrink_strengths, lead_inverse, *others_lead, *owns_lead, *others_tail, *owns_tail)

    messages = []
    for f in range(own_count):
        for e in range(n_blocks):
            if f == 0 and e == 0:
                messages.append(land(message, own_count * n_blocks))
                continue
            pairs = []
            for s in range(sources):
                for b in range(n_blocks):
                    pairs.append(((s ^ f) * n_blocks + (b - e) % n_blocks, s * n_blocks + b))
            messages.append(land(lax.ppermute(message, ("samples", "blocks"), pairs), own_count * n_blocks))

    preds, gram, cross = pl.pallas_call(
        functools.partial(level_kernel, own_count, trait_rows, held_rows),
        out_shape=[
            jax.ShapeDtypeStruct((own_count, 1, traits, levels, width), BF16),
            jax.ShapeDtypeStruct((own_count, 1, levels, n_blocks, levels, traits), F32),
            jax.ShapeDtypeStruct((own_count, 1, levels, traits), F32),
        ],
        in_specs=[vmem] * (1 + len(messages)),
        out_specs=[vmem] * 3,
        scratch_shapes=[pltpu.VMEM((n_blocks, message_rows, sources * width), F32)],
        name="level_one",
    )(land(trait_rows_held, sources), *messages)
    return jnp.swapaxes(preds, 2, 3), jnp.moveaxis(gram, 5, 3), cross


def solution(mesh):
    in_specs = (
        P("blocks", ("groups", "samples")),
        P(None, ("groups", "samples")),
        P(("groups", "samples")),
        P(),
    )
    out_specs = (
        P("folds", "blocks", None, None, ("groups", "samples")),
        P(("groups", "folds"), "blocks", None, None, None, None),
        P(("groups", "folds"), "blocks", None, None),
    )
    return jax.shard_map(
        per_device, mesh=mesh, in_specs=in_specs, out_specs=out_specs, check_vma=False
    )
```
